32 devices in a mesh: groups: 2 (over y), dp: 16 (over z, x, core).
Axes of the slice: x: 2, y: 2, z: 4, core: 2. Of those that a mesh axis runs over, the one named last changes fastest.
Arguments:
- particles: bfloat16 [2048, 128, 128], P(('groups', 'dp')), parts along dimension 0, may hold values from -20 to 20
- refs: bfloat16 [128, 256, 128], P('dp', 'groups'), parts along dimension 1, may hold values from -0.5 to 0.5
- ctf_group: int32 [2048], P(('groups', 'dp')), parts along dimension 0, may hold values from 0 to 31, as said below
- defocus: float32 [64], P('groups'), parts along dimension 0, may hold values from 0.5 to 2
- class_prior: float32 [256], P('groups'), parts along dimension 0, may hold values from 0.25 to 4
- cycle_weight: float32 [64], replicated, may hold values from 0.5 to 2
Outputs:
- new_refs: float32 [128, 256, 128], P('dp', 'groups'), parts along dimension 1
- log_evidence: float32 [2048], P(('groups', 'dp')), parts along dimension 0
The draws below stay inside these ranges and needn't reach their ends.
There are 2 independent parts, one for each index of `groups`. The reference program is written for one: setup_inputs(seed, part) draws one part's arguments, and reference() takes and returns one part's arrays. A program takes and returns all parts, laid end to end along the dimension named above; an argument that names none is the same for every part. Nothing has to cross between parts.
Inputs may be any that keep to these rules, and one draw needn't show every extreme that they name: `ctf_group`: CTF groups follow the particle order: particle n belongs to group n * 32 // 1024 or the next one, capped at 31.
All inputs are finite; a program needn't handle non-finite values.
Results may differ from the reference program's by a relative error of at most 0.0045.
Values may be sent and summed in bfloat16 or wider, within the bound.
A program may use at most 64 MiB of HBM per device.

```python
import math
import jax
import jax.numpy as jnp
from jax import lax

M = 128
R = 64
K = 128
ROT = 36
G = 32
NP_DEV = 64
NALL = 1024


def ctf_values(defocus):
    radius = (jnp.arange(R, dtype=jnp.float32) + 1.0) / R
    phase = 20.0 * defocus[:, None] * radius[None, :] ** 2
    return -(0.995 * jnp.sin(phase) + 0.1 * jnp.cos(phase))


def shared_draw(key):
    key_ref = jax.random.fold_in(key, 11)
    key_label = jax.random.fold_in(key, 12)
    key_group = jax.random.fold_in(key, 13)
    key_focus = jax.random.fold_in(key, 14)
    key_noise = jax.random.fold_in(key, 15)
    index = jnp.arange(NALL, dtype=jnp.int32)
    base = index * G // NALL + jax.random.randint(key_group, (NALL,), 0, 2)
    ctf_group = jnp.minimum(base, G - 1).astype(jnp.int32)
    labels = jax.random.randint(key_label, (NALL,), 0, K)
    refs = jnp.clip(jax.random.normal(key_ref, (M, K, 2 * R), jnp.float32), -6.0, 6.0) / 64.0
    amplitude = jnp.full((NALL,), 4.0, jnp.float32)
    defocus = jnp.exp(jax.random.uniform(key_focus, (G,), jnp.float32, math.log(0.5), math.log(2.0)))
    noise = jnp.clip(jax.random.normal(key_noise, (NALL, M, 2 * R), jnp.float32), -6.0, 6.0)
    ctf = ctf_values(defocus)
    gain = jnp.concatenate([ctf, ctf], axis=1)[ctf_group]
    signal = jnp.take(jnp.transpose(refs, (1, 0, 2)), labels, axis=0)
    particles = amplitude[:, None, None] * gain[:, None, :] * signal + noise
    return (particles, refs, ctf_group, defocus)


def draw_particles(key, part):
    return shared_draw(key)[0].astype(jnp.bfloat16)


def draw_refs(key, part):
    return shared_draw(key)[1].astype(jnp.bfloat16)


def draw_ctf_group(key, part):
    return shared_draw(key)[2]


def draw_defocus(key, part):
    return shared_draw(key)[3]


def setup_inputs(seed: int = 0, part: int = 0) -> dict:
    keys = jax.random.split(jax.random.key(seed), 7)
    part_keys = jax.random.split(jax.random.fold_in(keys[6], part), 7)
    return {
        "particles": draw_particles(jax.random.fold_in(jax.random.fold_in(keys[6], part), 71), part),
        "refs": draw_refs(jax.random.fold_in(jax.random.fold_in(keys[6], part), 71), part),
        "ctf_group": draw_ctf_group(jax.random.fold_in(jax.random.fold_in(keys[6], part), 71), part),
        "defocus": draw_defocus(jax.random.fold_in(jax.random.fold_in(keys[6], part), 71), part),
        "class_prior": jnp.clip(jnp.exp(jax.random.uniform(part_keys[4], (K,), jnp.float32, math.log(0.25), math.log(4.0))), 0.25, 4.0),
        "cycle_weight": jnp.clip(jnp.exp(jax.random.uniform(keys[5], (R,), jnp.float32, math.log(0.5), math.log(2.0))), 0.5, 2.0),
    }


def ctf_table(defocus):
    radius = (jnp.arange(R, dtype=jnp.float32) + 1.0) / R
    phase = 20.0 * defocus[:, None] * radius[None, :] ** 2
    return -(0.995 * jnp.sin(phase) + 0.1 * jnp.cos(phase))


def angle_tables():
    harmonic = jnp.arange(M, dtype=jnp.float32)[:, None]
    turning = jnp.arange(ROT, dtype=jnp.float32)[None, :]
    theta = 2.0 * math.pi * harmonic * turning / ROT
    return jnp.cos(theta), jnp.sin(theta)


def reference(particles, refs, ctf_group, defocus, class_prior, cycle_weight):
    highest = lax.Precision.HIGHEST
    ctf = ctf_table(defocus)
    cos_table, sin_table = angle_tables()
    refs_wide = refs.astype(jnp.float32)
    energy = jnp.sum(refs_wide[:, :, :R] ** 2 + refs_wide[:, :, R:] ** 2, axis=0)
    quadratic = jnp.dot(cycle_weight[None, :] * ctf * ctf, energy.T, precision=highest)
    log_prior = jnp.log(class_prior)
    gain_table = jnp.concatenate([cycle_weight[None, :] * ctf, cycle_weight[None, :] * ctf], axis=1)

    def block_step(totals, inputs):
        numer, mass = totals
        images, labels = inputs
        onehot = (labels[:, None] == jnp.arange(G, dtype=jnp.int32)[None, :]).astype(jnp.float32)
        gain = jnp.dot(onehot, gain_table, precision=highest)
        weighted = (images.astype(jnp.float32) * gain[:, None, :]).astype(jnp.bfloat16)
        turned = jnp.concatenate([weighted[:, :, R:], -weighted[:, :, :R]], axis=2)
        wide_weighted = weighted.astype(jnp.float32)
        wide_turned = turned.astype(jnp.float32)
        cross_real = jnp.einsum('nmq,mkq->mnk', wide_weighted, refs_wide, precision=highest)
        cross_imag = jnp.einsum('nmq,mkq->mnk', wide_turned, refs_wide, precision=highest)
        corr = jnp.einsum('mnk,mj->nkj', cross_real, cos_table, precision=highest)
        corr = corr - jnp.einsum('mnk,mj->nkj', cross_imag, sin_table, precision=highest)
        norm_term = jnp.dot(onehot, quadratic, precision=highest)
        scores = corr - 0.5 * norm_term[:, :, None] + log_prior[None, :, None]
        flat = scores.reshape(scores.shape[0], K * ROT)
        top = jnp.max(flat, axis=1, keepdims=True)
        expo = jnp.exp(flat - top)
        total = jnp.sum(expo, axis=1, keepdims=True)
        posterior = (expo / total).reshape(scores.shape)
        evidence = top[:, 0] + jnp.log(total[:, 0])
        mass = mass + jnp.dot(onehot.T, jnp.sum(posterior, axis=2), precision=highest)
        post_real = jnp.einsum('nkj,mj->mnk', posterior, cos_table, precision=highest).astype(jnp.bfloat16)
        post_imag = jnp.einsum('nkj,mj->mnk', posterior, sin_table, precision=highest).astype(jnp.bfloat16)
        numer = numer + jnp.einsum('mnk,nmq->mkq', post_real.astype(jnp.float32), wide_weighted, precision=highest)
        numer = numer - jnp.einsum('mnk,nmq->mkq', post_imag.astype(jnp.float32), wide_turned, precision=highest)
        return (numer, mass), evidence

    blocks = NALL // NP_DEV
    images_all = particles.reshape(blocks, NP_DEV, M, 2 * R)
    labels_all = ctf_group.reshape(blocks, NP_DEV)
    start_numer = jnp.zeros((M, K, 2 * R), jnp.float32)
    start_mass = jnp.zeros((G, K), jnp.float32)
    (numer, mass), evidence = lax.scan(block_step, (start_numer, start_mass), (images_all, labels_all))
    denom = 1.0 + jnp.dot(mass.T, cycle_weight[None, :] * ctf * ctf, precision=highest)
    denom_wide = jnp.concatenate([denom, denom], axis=1)
    new_refs = numer / denom_wide[None, :, :]
    return new_refs, evidence.reshape(NALL)
```

```python
import functools
import math

import jax
import jax.numpy as jnp
from jax import lax
from jax.experimental import pallas as pl
from jax.experimental.pallas import tpu as pltpu
from jax.sharding import PartitionSpec as P

R = 64
ROT = 36
HALF = ROT // 2
NC = HALF + 1
G = 32
MESH = pl.DeviceIdType.MESH
HIGHEST = lax.Precision.HIGHEST


def dev(index):
    return {"dp": index}


def ring_steps(zn):
    plus = zn // 2
    minus = zn - 1 - plus
    steps = []
    for d in range(1, plus + 1):
        steps.append((1, d))
        if d <= minus:
            steps.append((-1, d))
    return steps


def gather_kernel(zn, dp, window, refs_ref, part_ref, row_ref, focus_ref, cw_ref, prior_ref,
                  wt_ref, wpart_ref, table_ref, pp_ref, ev_ref, mass_ref,
                  out_ref, cres, energy, bias, psum, evcol, local_sem, send, recv, wsend, wrecv):
    me = lax.axis_index("dp")
    z, x, c = me // 4, (me // 2) % 2, me % 2
    flip_x = z * 4 + (1 - x) * 2 + c
    flip_c = z * 4 + x * 2 + (1 - c)
    n, m_all, q = part_ref.shape
    mb, k, _ = refs_ref.shape
    nall = n * dp
    steps = [(s, d) for d in range(1, zn) for s in (1, -1)]
    beside = {s: lax.rem(z + zn + s, zn) * 4 + x * 2 + c for s in (1, -1)}

    def holds(s, d):
        return z >= d if s == 1 else z + d < zn

    def goes(s):
        return z + 1 < zn if s == 1 else z >= 1

    def origin(s, d):
        return lax.rem(z + zn - s * d, zn) * 4

    barrier = pltpu.get_barrier_semaphore()
    greet = [beside[1], beside[-1], flip_x, flip_c]
    for p in greet:
        pl.semaphore_signal(barrier, inc=1, device_id=dev(p), device_id_type=MESH)
    pl.semaphore_wait(barrier, len(greet))

    count = 2 * (zn - 1)
    x0, c0 = count, 2 * count + 1

    def copy_of(src, block, target, slot):
        return pltpu.make_async_remote_copy(
            src_ref=src,
            dst_ref=out_ref.at[block],
            send_sem=send.at[slot],
            recv_sem=recv.at[slot],
            device_id=dev(target),
            device_id_type=MESH,
        )

    slot_of = {step: i for i, step in enumerate(steps)}
    for s in (1, -1):
        @pl.when(goes(s))
        def _():
            copy_of(refs_ref, me, beside[s], slot_of[(s, 1)]).start()
    copy_of(refs_ref, me, flip_x, x0).start()
    copy_of(refs_ref, me, flip_c, c0).start()
    keep = pltpu.make_async_copy(refs_ref, out_ref.at[me], local_sem)
    keep.start()

    lane = lax.broadcasted_iota(jnp.int32, (G, q), 1)
    radius = (jnp.where(lane < R, lane, lane - R).astype(jnp.float32) + 1.0) / R
    eye = lax.broadcasted_iota(jnp.int32, (G, G), 0) == lax.broadcasted_iota(jnp.int32, (G, G), 1)
    focus = jnp.sum(jnp.where(eye, jnp.broadcast_to(focus_ref[...], (G, G)), 0.0), axis=1, keepdims=True)
    phase = 20.0 * focus * (radius * radius)
    ctf = -(0.995 * jnp.sin(phase) + 0.1 * jnp.cos(phase))
    cw = jnp.concatenate([cw_ref[...], cw_ref[...]], axis=1)
    gain_table = cw * ctf
    power = gain_table * ctf

    def dot(a, b):
        return jnp.dot(a, b, precision=HIGHEST, preferred_element_type=jnp.float32)

    onehot = (row_ref[...] == lax.broadcasted_iota(jnp.int32, (G, n), 0)).astype(jnp.float32)

    def picked(table):
        return lax.dot_general(
            onehot, table, (((0,), (0,)), ((), ())),
            preferred_element_type=jnp.float32, precision=HIGHEST,
        )

    gain = picked(gain_table)
    anorm = 0.5 * picked(power)
    start = (me * (n * G)) // nall
    hot = (
        row_ref[...] == lax.broadcasted_iota(jnp.int32, (window, n), 0) + start
    ).astype(jnp.float32)
    below = lax.broadcasted_iota(jnp.int32, (window, G), 0) - lax.broadcasted_iota(jnp.int32, (window, G), 1)
    for d in range(dp):
        pick = (below == -(d * n * G // nall)).astype(jnp.float32)
        table_ref[d * window:(d + 1) * window, :] = dot(pick, power)

    chunk = 16

    @pl.loop(0, m_all // chunk)
    def _(i):
        at = pl.ds(pl.multiple_of(i * chunk, chunk), chunk)
        wide = part_ref[:, at, :].astype(jnp.float32) * gain[:, None, :]
        wt_ref[at] = jnp.swapaxes(wide, 0, 1).astype(jnp.bfloat16)

    wcopies = []
    for b in range(dp // 2):
        copy = pltpu.make_async_remote_copy(
            src_ref=wt_ref.at[pl.ds((2 * b + 1 - c) * mb, mb)],
            dst_ref=wpart_ref.at[b],
            send_sem=wsend.at[b],
            recv_sem=wrecv.at[b],
            device_id=dev(flip_c),
            device_id_type=MESH,
        )
        copy.start()
        wcopies.append(copy)

    cres[...] = jnp.zeros_like(cres)
    energy[...] = jnp.zeros_like(energy)
    lane_n = lax.broadcasted_iota(jnp.int32, (n, q), 1)
    sign = jnp.where(lane_n < R, jnp.float32(1.0), jnp.float32(-1.0))

    def products(block):
        total = None
        for i in range(mb):
            m = block * mb + i
            r = lax.rem(m, ROT)
            w = wt_ref[m]
            turned = (pltpu.roll(w.astype(jnp.float32), R, 1) * sign).astype(jnp.bfloat16)
            both = jnp.concatenate([w, turned], axis=0)
            ref = out_ref[block, i]
            cres[r] += lax.dot_general(
                both, ref, (((1,), (1,)), ((), ())), preferred_element_type=jnp.float32
            )
            wide = ref.astype(jnp.float32)
            total = wide * wide if total is None else total + wide * wide
        energy[...] += total

    keep.wait()
    products(me)
    for i, (s, d) in enumerate(steps):
        @pl.when(holds(s, d))
        def _():
            block = origin(s, d) + x * 2 + c
            copy_of(out_ref.at[block], block, beside[s], slot_of[(s, d)]).wait_recv()
            if d + 1 < zn:
                @pl.when(goes(s))
                def _():
                    copy_of(out_ref.at[block], block, beside[s], slot_of[(s, d + 1)]).start()
            copy_of(out_ref.at[block], block, flip_x, x0 + 1 + i).start()
            copy_of(out_ref.at[block], block, flip_c, c0 + 1 + i).start()
            products(block)
    every = [(None, (1, 0))] + list(enumerate(steps))

    def guarded(s, d, body):
        if d == 0:
            body()
        else:
            pl.when(holds(s, d))(body)

    for i, (s, d) in every:
        j = 0 if i is None else i + 1

        def from_x(s=s, d=d, j=j):
            block = origin(s, d) + (1 - x) * 2 + c
            copy_of(out_ref.at[block], block, flip_x, x0 + j).wait_recv()
            copy_of(out_ref.at[block], block, flip_c, c0 + count + 1 + j).start()
            products(block)
            mine = origin(s, d) + x * 2 + (1 - c)
            copy_of(out_ref.at[mine], mine, flip_c, c0 + j).wait_recv()
            products(mine)

        guarded(s, d, from_x)
    for i, (s, d) in every:
        j = 0 if i is None else i + 1

        def from_core(s=s, d=d, j=j):
            block = origin(s, d) + (1 - x) * 2 + (1 - c)
            copy_of(out_ref.at[block], block, flip_c, c0 + count + 1 + j).wait_recv()
            products(block)

        guarded(s, d, from_core)

    scores_and_posterior(anorm, hot, prior_ref, pp_ref, ev_ref, mass_ref, cres, energy, bias, psum, evcol, n)

    for copy in wcopies:
        copy.wait()
    for i, (s, d) in every:
        j = 0 if i is None else i + 1

        def sent(s=s, d=d, j=j):
            block = origin(s, d) + x * 2 + c
            other = origin(s, d) + (1 - x) * 2 + c
            copy_of(out_ref.at[block], block, flip_x, x0 + j).wait_send()
            copy_of(out_ref.at[block], block, flip_c, c0 + j).wait_send()
            copy_of(out_ref.at[other], other, flip_c, c0 + count + 1 + j).wait_send()

        guarded(s, d, sent)
    for s in (1, -1):
        for d in range(0, zn - 1):
            room = jnp.minimum(z - d, zn - 2 - z) if s == 1 else jnp.minimum(zn - 1 - d - z, z - 1)

            @pl.when(room >= 0)
            def _():
                block = origin(s, d) + x * 2 + c
                copy_of(out_ref.at[block], block, beside[s], slot_of[(s, d + 1)]).wait_send()


def dft_even_odd(even_in, odd_in, use_cos):
    f = math.cos if use_cos else math.sin

    def one(items, j):
        total = None
        for i, v in items:
            w = f(2.0 * math.pi * ((i * j) % ROT) / ROT)
            if abs(w) < 1e-12:
                continue
            if abs(w - 1.0) < 1e-12:
                term = v
            elif abs(w + 1.0) < 1e-12:
                term = -v
            else:
                term = v * jnp.float32(w)
            total = term if total is None else total + term
        return total

    count = HALF // 2 + 1
    return [one(even_in, j) for j in range(count)], [one(odd_in, j) for j in range(count)]


def half_transform(values, use_cos):
    even = [(i, v) for i, v in values.items() if i % 2 == 0]
    odd = [(i, v) for i, v in values.items() if i % 2 == 1]
    es, os_ = dft_even_odd(even, odd, use_cos)
    zero = jnp.zeros_like(next(iter(values.values())))
    out = {}
    for j in range(HALF // 2 + 1):
        e = zero if es[j] is None else es[j]
        o = zero if os_[j] is None else os_[j]
        out[j] = e + o
        out[HALF - j] = (e - o) if use_cos else (o - e)
    return out


def scores_and_posterior(anorm, hot, prior_ref, pp_ref, ev_ref, mass_ref, cres, energy, bias, psum, evcol, n):
    norm = lax.dot_general(
        anorm, energy[...], (((1,), (1,)), ((), ())),
        preferred_element_type=jnp.float32, precision=HIGHEST,
    )
    bias[...] = jnp.log(prior_ref[...]) - norm

    rows = 16

    @pl.loop(0, n // rows)
    def _(i):
        at = pl.ds(pl.multiple_of(i * rows, rows), rows)
        at_im = pl.ds(pl.multiple_of(n + i * rows, rows), rows)
        a = {0: cres[0, at, :], HALF: cres[HALF, at, :]}
        b = {}
        for r in range(1, HALF):
            a[r] = cres[r, at, :] + cres[ROT - r, at, :]
            b[r] = cres[r, at_im, :] - cres[ROT - r, at_im, :]
        cosine = half_transform(a, True)
        sine = half_transform(b, False)
        add = bias[at, :]
        scores = {}
        for j in range(NC):
            base = cosine[j] + add
            if j in (0, HALF):
                scores[j] = base
            else:
                scores[j] = base - sine[j]
                scores[ROT - j] = base + sine[j]
        top = scores[0]
        for j in range(1, ROT):
            top = jnp.maximum(top, scores[j])
        top = jnp.max(top, axis=1, keepdims=True)
        total = None
        expo = {}
        for j in range(ROT):
            expo[j] = jnp.exp(scores[j] - top)
            total = expo[j] if total is None else total + expo[j]
        norm_total = jnp.sum(total, axis=1, keepdims=True)
        evcol[at, :] = jnp.broadcast_to(top + jnp.log(norm_total), (rows, n))
        inv = 1.0 / norm_total
        psum[at, :] = total * inv
        u = {0: expo[0] * inv, HALF: expo[HALF] * inv}
        v = {}
        for j in range(1, HALF):
            u[j] = (expo[j] + expo[ROT - j]) * inv
            v[j] = (expo[j] - expo[ROT - j]) * inv
        real = half_transform(u, True)
        imag = half_transform(v, False)
        for r in range(NC):
            pp_ref[r, at, :] = real[r].astype(jnp.bfloat16)
            pp_ref[NC + r, at, :] = imag[r].astype(jnp.bfloat16)

    square = (n, n)
    eye = lax.broadcasted_iota(jnp.int32, square, 0) == lax.broadcasted_iota(jnp.int32, square, 1)
    ev_ref[...] = jnp.sum(jnp.where(eye, evcol[...], 0.0), axis=0, keepdims=True)
    mass_ref[...] = lax.dot_general(
        hot, psum[...], (((1,), (0,)), ((), ())),
        preferred_element_type=jnp.float32, precision=HIGHEST,
    )


def mstep_kernel(zn, dp, pp_ref, wt_ref, wpart_ref, mass_ref, table_ref, out_ref,
                 pbuf, pt, xsend, xrecv, acc, zsend, zrecv, mslots,
                 psend_s, psend_r, xs, xr, zs, zr, ms, mr):
    me = lax.axis_index("dp")
    z, x, c = me // 4, (me // 2) % 2, me % 2
    flip_x = z * 4 + (1 - x) * 2 + c
    flip_c = z * 4 + x * 2 + (1 - c)
    mb, k, q = out_ref.shape

    barrier = pltpu.get_barrier_semaphore()
    for o in range(1, dp):
        pl.semaphore_signal(barrier, inc=1, device_id=dev(lax.rem(me + o, dp)), device_id_type=MESH)
    pl.semaphore_wait(barrier, dp - 1)

    pcopy = pltpu.make_async_remote_copy(
        src_ref=pp_ref, dst_ref=pbuf, send_sem=psend_s, recv_sem=psend_r,
        device_id=dev(flip_c), device_id_type=MESH,
    )
    pcopy.start()
    mcopies = []
    for o in range(1, dp):
        copy = pltpu.make_async_remote_copy(
            src_ref=mass_ref, dst_ref=mslots.at[me], send_sem=ms.at[o], recv_sem=mr.at[o],
            device_id=dev(lax.rem(me + o, dp)), device_id_type=MESH,
        )
        copy.start()
        mcopies.append(copy)
    mslots[me] = mass_ref[...]
    pcopy.wait()

    @pl.loop(0, 2 * NC)
    def _(i):
        pt[i] = jnp.concatenate([pp_ref[i], pbuf[i]], axis=0).T

    lane = lax.broadcasted_iota(jnp.int32, (k, q), 1)
    mask = jnp.where(lane < R, jnp.float32(-1.0), jnp.float32(1.0))

    def numer(zx, i):
        m = (zx * 2 + c) * mb + i
        r = lax.rem(m, ROT)
        rr = jnp.minimum(r, ROT - r)
        s = jnp.where(r > HALF, -1, 1).astype(jnp.float32)
        w = jnp.concatenate([wt_ref[m], wpart_ref[zx, i]], axis=0)
        u = jnp.dot(pt[rr], w, preferred_element_type=jnp.float32)
        v = jnp.dot(pt[NC + rr], w, preferred_element_type=jnp.float32)
        return u + pltpu.roll(v, R, 1) * (mask * s)

    steps = ring_steps(zn)
    reach = {1: zn // 2, -1: zn - 1 - zn // 2}
    order = [((s * (reach[s] + 1 - d)) % zn, s, d) for s, d in steps] + [(0, 0, 0)]
    xcopies = []
    for o, _, _ in order:
        zz = lax.rem(z + o, zn)

        for i in range(mb):
            xsend[o, i] = numer(zz * 2 + 1 - x, i).astype(jnp.bfloat16)

        copy = pltpu.make_async_remote_copy(
            src_ref=xsend.at[o], dst_ref=xrecv.at[o], send_sem=xs.at[o], recv_sem=xr.at[o],
            device_id=dev(flip_x), device_id_type=MESH,
        )
        copy.start()
        xcopies.append(copy)

    zcopies = {}
    last = []
    for j, ((o, s, d), xcopy) in enumerate(zip(order, xcopies)):
        zz = lax.rem(z + o, zn)

        for i in range(mb):
            acc[i] = numer(zz * 2 + x, i)

        xcopy.wait_recv()
        if o:
            before = None
            if d > 1:
                before, got = zcopies[(s, d - 1)]
                got.wait_recv()

            @pl.loop(0, mb)
            def _(i):
                total = acc[i] + xrecv[o, i].astype(jnp.float32)
                if before is not None:
                    total = total + zrecv[before, i].astype(jnp.float32)
                zsend[j, i] = total.astype(jnp.bfloat16)

            copy = pltpu.make_async_remote_copy(
                src_ref=zsend.at[j], dst_ref=zrecv.at[j], send_sem=zs.at[j], recv_sem=zr.at[j],
                device_id=dev(lax.rem(z + zn + s, zn) * 4 + x * 2 + c), device_id_type=MESH,
            )
            copy.start()
            zcopies[(s, d)] = (j, copy)
            if d == reach[s]:
                last.append((j, copy))
    for copy in mcopies:
        copy.wait_recv()
    wide = mslots[...].reshape(dp * mslots.shape[1], k)
    denom = 1.0 + lax.dot_general(
        wide, table_ref[...], (((0,), (0,)), ((), ())),
        preferred_element_type=jnp.float32, precision=HIGHEST,
    )
    inv = 1.0 / denom
    for _, copy in last:
        copy.wait_recv()

    @pl.loop(0, mb)
    def _(i):
        total = acc[i] + xrecv[0, i].astype(jnp.float32)
        for j, _ in last:
            total = total + zrecv[j, i].astype(jnp.float32)
        out_ref[i] = total * inv

    for copy in xcopies + [copy for _, copy in zcopies.values()] + mcopies:
        copy.wait_send()


def shards(dp, particles, refs, ctf_group, defocus, class_prior, cycle_weight):
    n, m_all, q = particles.shape
    mb, k, _ = refs.shape
    zn = dp // 4
    nall = n * dp
    window = -(-((n * G) // nall + 2) // 8) * 8

    vmem = pl.BlockSpec(memory_space=pltpu.VMEM)
    hbm = pl.BlockSpec(memory_space=pl.ANY)
    sem = pltpu.SemaphoreType.DMA
    copies = 8 * zn - 5
    wt, wpart, table, pp, ev, mass = pl.pallas_call(
        functools.partial(gather_kernel, zn, dp, window),
        out_shape=(
            jax.ShapeDtypeStruct((m_all, n, q), jnp.bfloat16),
            jax.ShapeDtypeStruct((dp // 2, mb, n, q), jnp.bfloat16),
            jax.ShapeDtypeStruct((dp * window, q), jnp.float32),
            jax.ShapeDtypeStruct((2 * NC, n, k), jnp.bfloat16),
            jax.ShapeDtypeStruct((1, n), jnp.float32),
            jax.ShapeDtypeStruct((window, k), jnp.float32),
        ),
        in_specs=[vmem] * 6,
        out_specs=(vmem, hbm, vmem, vmem, vmem, vmem),
        scratch_shapes=[
            pltpu.VMEM((dp, mb, k, q), jnp.bfloat16),
            pltpu.VMEM((ROT, 2 * n, k), jnp.float32),
            pltpu.VMEM((k, q), jnp.float32),
            pltpu.VMEM((n, k), jnp.float32),
            pltpu.VMEM((n, k), jnp.float32),
            pltpu.VMEM((n, n), jnp.float32),
            sem, sem((copies,)), sem((copies,)), sem((dp // 2,)), sem((dp // 2,)),
        ],
        compiler_params=pltpu.CompilerParams(collective_id=0, has_side_effects=True),
        name="gather",
    )(refs, particles, ctf_group[None, :], defocus[None, :], cycle_weight[None, :], class_prior[None, :])

    new_refs = pl.pallas_call(
        functools.partial(mstep_kernel, zn, dp),
        out_shape=jax.ShapeDtypeStruct((mb, k, q), jnp.float32),
        in_specs=[vmem] * 5,
        out_specs=vmem,
        scratch_shapes=[
            pltpu.VMEM((2 * NC, n, k), jnp.bfloat16),
            pltpu.VMEM((2 * NC, k, 2 * n), jnp.bfloat16),
            pltpu.VMEM((zn, mb, k, q), jnp.bfloat16),
            pltpu.VMEM((zn, mb, k, q), jnp.bfloat16),
            pltpu.VMEM((mb, k, q), jnp.float32),
            pltpu.VMEM((zn, mb, k, q), jnp.bfloat16),
            pltpu.VMEM((zn, mb, k, q), jnp.bfloat16),
            pltpu.VMEM((dp, window, k), jnp.float32),
            sem, sem,
            sem((zn,)), sem((zn,)), sem((zn,)), sem((zn,)), sem((dp,)), sem((dp,)),
        ],
        compiler_params=pltpu.CompilerParams(collective_id=1, has_side_effects=True),
        name="mstep",
    )(pp, wt, wpart, mass, table)
    return (new_refs, ev[0])


def solution(mesh):
    in_specs = (
        P(("groups", "dp"), None, None),
        P("dp", "groups", None),
        P(("groups", "dp")),
        P("groups"),
        P("groups"),
        P(),
    )
    out_specs = (P("dp", "groups", None), P(("groups", "dp")))
    return jax.shard_map(
        functools.partial(shards, mesh.shape["dp"]),
        mesh=mesh, in_specs=in_specs, out_specs=out_specs, check_vma=False,
    )
```

```python
import functools
import math

import jax
import jax.numpy as jnp
from jax import lax
from jax.experimental import pallas as pl
from jax.experimental.pallas import tpu as pltpu
from jax.sharding import PartitionSpec as P

R = 64
ROT = 36
HALF = ROT // 2
NC = HALF + 1
G = 32
MESH = pl.DeviceIdType.MESH
HIGHEST = lax.Precision.HIGHEST
F32 = jnp.float32
BF16 = jnp.bfloat16


def dev(index):
    return {"dp": index}


def dft_even_odd(even_in, odd_in, use_cos):
    f = math.cos if use_cos else math.sin

    def one(items, j):
        total = None
        for i, v in items:
            w = f(2.0 * math.pi * ((i * j) % ROT) / ROT)
            if abs(w) < 1e-12:
                continue
            if abs(w - 1.0) < 1e-12:
                term = v
            elif abs(w + 1.0) < 1e-12:
                term = -v
            else:
                term = v * jnp.float32(w)
            total = term if total is None else total + term
        return total

    count = HALF // 2 + 1
    return [one(even_in, j) for j in range(count)], [one(odd_in, j) for j in range(count)]


def half_transform(values, use_cos):
    even = [(i, v) for i, v in values.items() if i % 2 == 0]
    odd = [(i, v) for i, v in values.items() if i % 2 == 1]
    es, os_ = dft_even_odd(even, odd, use_cos)
    zero = jnp.zeros_like(next(iter(values.values())))
    out = {}
    for j in range(HALF // 2 + 1):
        e = zero if es[j] is None else es[j]
        o = zero if os_[j] is None else os_[j]
        out[j] = e + o
        out[HALF - j] = (e - o) if use_cos else (o - e)
    return out


def step_kernel(zn, dp, window, *refs):
    (refs_ref, part_ref, row_ref, focus_ref, cw_ref, prior_ref,
     out_ref, inv_ref, ev_ref,
     part, both, held, cres, energy, sbuf, psum, pp, rows2, table,
     stat, stat_got, mass, mslots,
     xsend, xrecv, zsend, zrecv, xlast, esend, erecv, sib, acc, finx, finz,
     psem, keep, ksend, krecv, wsend, wrecv, rsend, rrecv,
     ax_s, ax_r, az_s, az_r, ae_s, ae_r, ssend, srecv, msend, mrecv,
     rx_s, rx_r, rz_s, rz_r, re_s, re_r, fx_r, fz_r, bsend, brecv) = refs
    me = lax.axis_index("dp")
    z, x, c = me // 4, (me // 2) % 2, me % 2
    o = 1 - c
    y = 1 - x
    n = part.shape[0]
    m_all, q = both.shape[0], both.shape[-1]
    mb, kh = held.shape[2], held.shape[3]
    k = 2 * kh
    n2 = 2 * n
    nall = n * dp
    end = zn - 1

    def at(zz, xx, cc):
        return zz * 4 + xx * 2 + cc

    def chip(zz, xx):
        return zz * 2 + xx

    def remote(src, dst, ss, rs, target):
        return pltpu.make_async_remote_copy(
            src_ref=src, dst_ref=dst, send_sem=ss, recv_sem=rs,
            device_id=dev(target), device_id_type=MESH,
        )

    def is_end(zz):
        return jnp.logical_or(zz == 0, zz == end)

    def inside(zz):
        return jnp.logical_and(zz >= 0, zz < zn)

    def sign_of(s):
        return 1 - 2 * s

    def slot(d, s, e):
        return (d * 2 + s) * 2 + e

    sibling = at(z, x, o)

    barrier = pltpu.get_barrier_semaphore()

    def greet(target):
        pl.semaphore_signal(barrier, inc=1, device_id=dev(target), device_id_type=MESH)

    greet(sibling)
    greet(at(z, y, 0))
    greet(at(z, y, 1))
    for zz in (z - 1, z + 1):
        @pl.when(inside(zz))
        def _():
            greet(at(zz, x, 0))
            greet(at(zz, x, 1))

    load = pltpu.make_async_copy(part_ref, part, psem)
    load.start()
    mine = pltpu.make_async_copy(refs_ref.at[:, c], held.at[chip(z, x), c], keep)
    mine.start()

    lane = lax.broadcasted_iota(jnp.int32, (G, q), 1)
    radius = (jnp.where(lane < R, lane, lane - R).astype(F32) + 1.0) / R
    eye = lax.broadcasted_iota(jnp.int32, (G, G), 0) == lax.broadcasted_iota(jnp.int32, (G, G), 1)
    focus = jnp.sum(jnp.where(eye, jnp.broadcast_to(focus_ref[...], (G, G)), 0.0), axis=1, keepdims=True)
    phase = 20.0 * focus * (radius * radius)
    ctf = -(0.995 * jnp.sin(phase) + 0.1 * jnp.cos(phase))
    cw = jnp.concatenate([cw_ref[...], cw_ref[...]], axis=1)
    gain_table = cw * ctf
    power = gain_table * ctf

    onehot = (row_ref[...] == lax.broadcasted_iota(jnp.int32, (G, n), 0)).astype(F32)
    gain = lax.dot_general(
        onehot, gain_table, (((0,), (0,)), ((), ())),
        preferred_element_type=F32, precision=HIGHEST,
    )
    row = row_ref[...].astype(F32)
    rows2[c] = jnp.broadcast_to(jnp.concatenate([row, row], axis=1), rows2.shape[1:])

    pl.semaphore_wait(
        barrier, 3 + 2 * (z > 0).astype(jnp.int32) + 2 * (z < end).astype(jnp.int32)
    )

    here = chip(z, x)

    def first_z(s, e):
        cc = jnp.bitwise_xor(c, e)
        return remote(refs_ref.at[:, cc], held.at[here, c], az_s.at[slot(0, s, e)],
                      az_r.at[slot(1, s, e)], at(z + sign_of(s), x, cc))

    def first_x(e):
        cc = jnp.bitwise_xor(c, e)
        return remote(refs_ref.at[:, cc], held.at[here, c], ax_s.at[slot(0, 0, e)],
                      ax_r.at[slot(0, 0, e)], at(z, y, cc))

    for e in range(2):
        for s in range(2):
            @pl.when(inside(z + sign_of(s)))
            def _():
                first_z(s, e).start()
        first_x(e).start()
    own_half = remote(refs_ref.at[:, o], held.at[here, c], ksend, krecv, sibling)
    own_half.start()
    rows_copy = remote(rows2.at[c], rows2.at[c], rsend, rrecv, sibling)
    rows_copy.start()

    load.wait()
    turn = jnp.where(lax.broadcasted_iota(jnp.int32, (1, 1, q), 2) < R, F32(1.0), F32(-1.0))
    chunk = 16

    def weighted_copy(i):
        span = pl.ds(pl.multiple_of(i * chunk, chunk), chunk)
        return remote(both.at[span, :, c], both.at[span, :, c], wsend.at[i], wrecv.at[i], sibling)

    @pl.loop(0, m_all // chunk)
    def _(i):
        span = pl.ds(pl.multiple_of(i * chunk, chunk), chunk)
        wide = part[:, span, :].astype(F32) * gain[:, None, :]
        w = jnp.swapaxes(wide, 0, 1).astype(BF16)
        both[span, 0, c] = w
        both[span, 1, c] = (pltpu.roll(w.astype(F32), R, 2) * turn).astype(BF16)
        weighted_copy(i).start()

    cres[...] = jnp.zeros_like(cres)
    energy[...] = jnp.zeros_like(energy)
    below = lax.broadcasted_iota(jnp.int32, (window, G), 0) - lax.broadcasted_iota(jnp.int32, (window, G), 1)
    for p in range(dp // 2):
        pick = (below == -((p * n2 * G) // nall)).astype(F32)
        span = jnp.dot(pick, power, precision=HIGHEST, preferred_element_type=F32)
        table[2 * p * window:(2 * p + 1) * window, :] = span
        table[(2 * p + 1) * window:(2 * p + 2) * window, :] = span

    @pl.loop(0, m_all // chunk)
    def _(i):
        weighted_copy(i).wait_recv()

    def products(block, cc):
        total = None
        for i in range(mb):
            m = (block * 2 + cc) * mb + i
            r = lax.rem(m, ROT)
            images = both[m].reshape(2 * n2, q)
            ref = held[block, cc, i]
            cres[r] += lax.dot_general(
                ref, images, (((1,), (1,)), ((), ())), preferred_element_type=F32
            )
            wide = ref.astype(F32)
            total = wide * wide if total is None else total + wide * wide
        energy[...] += total

    def z_copy(d, s, e):
        piece = held.at[chip(z - sign_of(s) * d, x), jnp.bitwise_xor(c, e)]
        return remote(piece, piece, az_s.at[slot(d, s, e)], az_r.at[slot(d + 1, s, e)],
                      at(z + sign_of(s), x, c))

    def z_wait(d, s, e):
        piece = held.at[chip(z - sign_of(s) * d, x), jnp.bitwise_xor(c, e)]
        return remote(piece, piece, az_s.at[slot(d, s, e)], az_r.at[slot(d, s, e)], sibling)

    def x_copy(d, s, e):
        piece = held.at[chip(z - sign_of(s) * d, x), jnp.bitwise_xor(c, e)]
        return remote(piece, piece, ax_s.at[slot(d, s, e)], ax_r.at[slot(d, s, e)], at(z, y, c))

    def x_wait(d, s, e):
        piece = held.at[chip(z - sign_of(s) * d, y), jnp.bitwise_xor(c, e)]
        return remote(piece, piece, ax_s.at[slot(d, s, e)], ax_r.at[slot(d, s, e)], sibling)

    def e_piece(s):
        return held.at[chip(s * end, y), o]

    def e_copy(s):
        piece = e_piece(s)
        return remote(piece, piece, ae_s.at[s], ae_r.at[s], at(z + sign_of(s), x, c))

    def by_x(zo, e):
        return jnp.logical_not(jnp.logical_and(e == 1, is_end(zo)))

    def z_held(d, s):
        return jnp.logical_and(d < zn, inside(z - sign_of(s) * d))

    def x_held(d, s, e):
        far = jnp.logical_and(inside(z - sign_of(s) * d), by_x(z - sign_of(s) * d, e))
        return jnp.logical_or(jnp.logical_and(d > 0, far), jnp.logical_and(d == 0, s == 0))

    own_done = [False]
    mine.wait()
    products(here, c)
    own_half.wait_recv()
    products(here, o)

    @pl.loop(1, zn + 1)
    def _(d):
        @pl.loop(0, 4)
        def _(j):
            e, s = j // 2, j % 2

            @pl.when(z_held(d, s))
            def _():
                zo = z - sign_of(s) * d
                z_wait(d, s, e).wait_recv()

                @pl.when(inside(z + sign_of(s)))
                def _():
                    z_copy(d, s, e).start()

                @pl.when(by_x(zo, e))
                def _():
                    x_copy(d, s, e).start()

                products(chip(zo, x), jnp.bitwise_xor(c, e))

        @pl.loop(0, 4)
        def _(j):
            e, s = j // 2, j % 2

            @pl.when(x_held(d - 1, s, e))
            def _():
                x_wait(d - 1, s, e).wait_recv()
                for t in range(2):
                    @pl.when(jnp.logical_and(jnp.logical_and(d == 1, e == 1), z == t * end))
                    def _():
                        e_copy(t).start()

                products(chip(z - sign_of(s) * (d - 1), y), jnp.bitwise_xor(c, e))

        @pl.loop(0, 2)
        def _(s):
            gone = jnp.where(s == 0, z, end - z)

            @pl.when(jnp.logical_and(gone == d - 1, gone > 0))
            def _():
                e_copy(s).wait_recv()

                @pl.when(gone < end)
                def _():
                    e_copy(s).start()

                products(chip(s * end, y), o)

    rows_copy.wait_recv()
    group = jnp.concatenate([rows2[0, 0:1, :n], rows2[1, 0:1, :n]], axis=1)
    hot_g = (group == lax.broadcasted_iota(jnp.int32, (G, n2), 0).astype(F32)).astype(F32)
    quad = lax.dot_general(
        energy[...], power, (((1,), (1,)), ((), ())), preferred_element_type=F32, precision=HIGHEST,
    )
    norm = jnp.dot(quad, hot_g, precision=HIGHEST, preferred_element_type=F32)
    diag = lax.broadcasted_iota(jnp.int32, (kh, k), 0) + c * kh == lax.broadcasted_iota(jnp.int32, (kh, k), 1)
    prior = jnp.sum(jnp.where(diag, jnp.broadcast_to(prior_ref[...], (kh, k)), 0.0), axis=1, keepdims=True)
    psum[...] = jnp.log(prior) - 0.5 * norm

    rows = 16

    def score_rows(i, top):
        span = pl.ds(pl.multiple_of(i * rows, rows), rows)
        re, im = pl.ds(0, n2), pl.ds(n2, n2)
        a = {0: cres[0, span, re], HALF: cres[HALF, span, re]}
        b = {}
        for r in range(1, HALF):
            a[r] = cres[r, span, re] + cres[ROT - r, span, re]
            b[r] = cres[r, span, im] - cres[ROT - r, span, im]
        cosine = half_transform(a, True)
        sine = half_transform(b, False)
        add = psum[span, :]
        for j in range(NC):
            base = cosine[j] + add
            if j in (0, HALF):
                sbuf[j, span, :] = base
                top = jnp.maximum(top, base)
            else:
                low, high = base - sine[j], base + sine[j]
                sbuf[j, span, :] = low
                sbuf[ROT - j, span, :] = high
                top = jnp.maximum(top, jnp.maximum(low, high))
        return top

    top = lax.fori_loop(0, kh // rows, score_rows, jnp.full((rows, n2), -jnp.inf, F32))
    top = jnp.max(top, axis=0, keepdims=True)

    def exp_rows(i, total):
        span = pl.ds(pl.multiple_of(i * rows, rows), rows)
        part_sum = None
        for j in range(ROT):
            value = jnp.exp(sbuf[j, span, :] - top)
            sbuf[j, span, :] = value
            part_sum = value if part_sum is None else part_sum + value
        psum[span, :] = part_sum
        return total + part_sum

    total = lax.fori_loop(0, kh // rows, exp_rows, jnp.zeros((rows, n2), F32))
    total = jnp.sum(total, axis=0, keepdims=True)
    which = lax.broadcasted_iota(jnp.int32, stat.shape, 0)
    stat[...] = jnp.where(which == 0, top, total)
    stat_copy = remote(stat, stat_got, ssend, srecv, sibling)
    stat_copy.start()
    stat_copy.wait_recv()
    other_top, other_total = stat_got[0:1, :], stat_got[1:2, :]
    most = jnp.maximum(top, other_top)
    shrink = jnp.exp(top - most)
    whole = total * shrink + other_total * jnp.exp(other_top - most)
    evidence = most + jnp.log(whole)
    ev_ref[...] = jnp.where(c == 0, evidence[:, :n], evidence[:, n:])
    scale = shrink / whole

    @pl.loop(0, kh // rows)
    def _(i):
        span = pl.ds(pl.multiple_of(i * rows, rows), rows)
        u = {0: sbuf[0, span, :] * scale, HALF: sbuf[HALF, span, :] * scale}
        v = {}
        for j in range(1, HALF):
            low, high = sbuf[j, span, :], sbuf[ROT - j, span, :]
            u[j] = (low + high) * scale
            v[j] = (low - high) * scale
        real = half_transform(u, True)
        imag = half_transform(v, False)
        for r in range(NC):
            re = real[r].astype(BF16)
            im = imag[r].astype(BF16)
            pp[r, span, 0:n2] = re
            pp[r, span, n2:] = -im
            if 0 < r < HALF:
                pp[ROT - r, span, 0:n2] = re
                pp[ROT - r, span, n2:] = im

    def numer(block, cc, i):
        m = (block * 2 + cc) * mb + i
        r = lax.rem(m, ROT)
        return jnp.dot(pp[r], both[m].reshape(2 * n2, q), preferred_element_type=F32)

    def e_sum(s):
        return remote(esend.at[s], erecv.at[s], re_s.at[s], re_r.at[s], at(z + sign_of(s), x, c))

    for s in range(2):
        @pl.when(z == s * end)
        def _():
            for i in range(mb):
                esend[s, i] = numer(chip(end - s * end, y), o, i).astype(BF16)
            e_sum(s).start()

    def x_sum(d, s, e):
        return remote(xsend.at[slot(d, s, e)], xrecv.at[slot(d, s, e)],
                      rx_s.at[slot(d, s, e)], rx_r.at[slot(d, s, e)], at(z, y, c))

    def x_last(e):
        return remote(xlast.at[e], finx.at[c], rx_s.at[slot(0, 0, e)], fx_r.at[c],
                      at(z, y, jnp.bitwise_xor(c, e)))

    def x_goes(d, s, e):
        zo = z + sign_of(s) * d
        return jnp.logical_and(inside(zo), by_x(zo, e))

    @pl.loop(0, zn - 1)
    def _(t):
        d = end - t

        @pl.loop(0, 4)
        def _(j):
            e, s = j // 2, j % 2

            @pl.when(x_goes(d, s, e))
            def _():
                for i in range(mb):
                    xsend[slot(d, s, e), i] = numer(
                        chip(z + sign_of(s) * d, y), jnp.bitwise_xor(c, e), i
                    ).astype(BF16)
                x_sum(d, s, e).start()

    def send_last(e, extra):
        for i in range(mb):
            value = numer(chip(z, y), jnp.bitwise_xor(c, e), i)
            if extra is not None:
                value = value + erecv[extra, i].astype(F32)
            xlast[e, i] = value.astype(BF16)
        x_last(e).start()

    @pl.loop(0, 2)
    def _(e):
        @pl.when(by_x(z, e))
        def _():
            send_last(e, None)

    start = (here * n2 * G) // nall
    hot = (
        group == (lax.broadcasted_iota(jnp.int32, (window, n2), 0) + start).astype(F32)
    ).astype(F32)
    part_mass = lax.dot_general(
        hot, psum[...] * scale, (((1,), (1,)), ((), ())), preferred_element_type=F32, precision=HIGHEST,
    )
    nothing = jnp.zeros_like(part_mass)
    mass[...] = jnp.where(
        c == 0, jnp.concatenate([part_mass, nothing], axis=1), jnp.concatenate([nothing, part_mass], axis=1)
    )
    mslots[me] = mass[...]

    def mass_copy(g):
        return remote(mass, mslots.at[me], msend.at[g], mrecv.at[g], lax.rem(me + g, dp))

    def mass_wait(g):
        return remote(mass, mslots.at[lax.rem(me + dp - g, dp)], msend.at[g], mrecv.at[g], sibling)

    @pl.loop(1, dp)
    def _(g):
        mass_copy(g).start()

    for i in range(mb):
        sib[i] = numer(here, o, i)
    sib_copy = remote(sib, acc.at[c], bsend, brecv, sibling)
    sib_copy.start()

    def z_sum(d, s, e):
        return remote(zsend.at[slot(d, s, e)], zrecv.at[slot(d - 1, s, e)],
                      rz_s.at[slot(d, s, e)], rz_r.at[slot(d - 1, s, e)], at(z + sign_of(s), x, c))

    def z_got(d, s, e):
        return remote(zsend.at[slot(d, s, e)], zrecv.at[slot(d, s, e)],
                      rz_s.at[slot(d, s, e)], rz_r.at[slot(d, s, e)], sibling)

    def z_last(s, e):
        return remote(zsend.at[slot(1, s, e)], finz.at[s, c], rz_s.at[slot(1, s, e)], fz_r.at[s, c],
                      at(z + sign_of(s), x, jnp.bitwise_xor(c, e)))

    near = (2 * z < zn).astype(jnp.int32)

    @pl.loop(0, zn - 1)
    def _(t):
        d = end - t

        for s in range(2):
            left = (end - z) if s == 0 else z

            @pl.when(jnp.logical_and(left == d, left < end))
            def _():
                e_sum(s).wait_recv()
                for i in range(mb):
                    esend[s, i] = (numer(chip(end - s * end, y), o, i) + erecv[s, i].astype(F32)).astype(BF16)
                e_sum(s).start()

        for s in range(2):
            @pl.when(jnp.logical_and(d == 1, z == (1 - s) * end))
            def _():
                e_sum(s).wait_recv()
                send_last(1, s)

        @pl.loop(0, 4)
        def _(j):
            e = 1 - j // 2
            s = jnp.bitwise_xor(j % 2, near)
            zo = z + sign_of(s) * d

            @pl.when(inside(zo))
            def _():
                here_slot = slot(d, s, e)
                crossed = by_x(zo, e)
                line = inside(z - sign_of(s))
                for i in range(mb):
                    acc[c, i] = numer(chip(zo, x), jnp.bitwise_xor(c, e), i)

                @pl.when(crossed)
                def _():
                    x_sum(d, s, e).wait_recv()
                    for i in range(mb):
                        acc[c, i] += xrecv[here_slot, i].astype(F32)

                @pl.when(line)
                def _():
                    z_got(d, s, e).wait_recv()
                    for i in range(mb):
                        acc[c, i] += zrecv[here_slot, i].astype(F32)

                for i in range(mb):
                    zsend[here_slot, i] = acc[c, i].astype(BF16)

                @pl.when(d > 1)
                def _():
                    z_sum(d, s, e).start()

                @pl.when(d == 1)
                def _():
                    z_last(s, e).start()

    for i in range(mb):
        acc[c, i] = numer(here, c, i)

    @pl.loop(1, dp)
    def _(g):
        mass_wait(g).wait_recv()

    denom = 1.0 + lax.dot_general(
        mslots[...].reshape(dp * window, k), table[...], (((0,), (0,)), ((), ())),
        preferred_element_type=F32, precision=HIGHEST,
    )
    inv_ref[...] = (1.0 / denom).reshape(inv_ref.shape)
    sib_copy.wait_recv()

    for h in range(2):
        remote(xlast.at[0], finx.at[h], rx_s.at[slot(0, 0, 0)], fx_r.at[h], sibling).wait_recv()
        acc[h] += finx[h].astype(F32)
    for s in range(2):
        @pl.when(inside(z - sign_of(s)))
        def _():
            for h in range(2):
                remote(xlast.at[0], finz.at[s, h], rx_s.at[slot(0, 0, 0)], fz_r.at[s, h], sibling).wait_recv()
                acc[h] += finz[s, h].astype(F32)
    for h in range(2):
        out_ref[:, h] = acc[h]

    for e in range(2):
        for s in range(2):
            @pl.when(inside(z + sign_of(s)))
            def _():
                first_z(s, e).wait_send()
        first_x(e).wait_send()
    own_half.wait_send()
    rows_copy.wait_send()
    stat_copy.wait_send()
    sib_copy.wait_send()

    @pl.loop(0, m_all // chunk)
    def _(i):
        weighted_copy(i).wait_send()

    @pl.loop(1, zn)
    def _(d):
        @pl.loop(0, 4)
        def _(j):
            e, s = j // 2, j % 2
            zo = z - sign_of(s) * d

            @pl.when(z_held(d, s))
            def _():
                @pl.when(inside(z + sign_of(s)))
                def _():
                    z_copy(d, s, e).wait_send()

                @pl.when(by_x(zo, e))
                def _():
                    x_copy(d, s, e).wait_send()

            @pl.when(x_goes(d, s, e))
            def _():
                x_sum(d, s, e).wait_send()

            @pl.when(inside(z + sign_of(s) * d))
            def _():
                z_got(d, s, e).wait_send()

    for s in range(2):
        @pl.when(inside(z + sign_of(s)))
        def _():
            e_copy(s).wait_send()
            e_sum(s).wait_send()
    for e in range(2):
        x_last(e).wait_send()

    @pl.loop(1, dp)
    def _(g):
        mass_copy(g).wait_send()


def finish_kernel(total_ref, inv_ref, ev_ref, out_ref, evidence_ref):
    for i in range(total_ref.shape[0]):
        out_ref[i] = total_ref[i] * inv_ref[...]
    evidence_ref[...] = ev_ref[...]


def shards(dp, particles, refs, ctf_group, defocus, class_prior, cycle_weight):
    n, m_all, q = particles.shape
    mb, k, _ = refs.shape
    zn = dp // 4
    nall = n * dp
    kh = k // 2
    n2 = 2 * n
    window = -(-((n2 * G) // nall + 3) // 8) * 8
    slots = 4 * zn
    weighted_chunks = m_all // 16

    vmem = pl.BlockSpec(memory_space=pltpu.VMEM)
    hbm = pl.BlockSpec(memory_space=pl.ANY)
    sem = pltpu.SemaphoreType.DMA
    total, inv, ev = pl.pallas_call(
        functools.partial(step_kernel, zn, dp, window),
        out_shape=(
            jax.ShapeDtypeStruct((mb, 2, kh, q), F32),
            jax.ShapeDtypeStruct((2, kh, q), F32),
            jax.ShapeDtypeStruct((1, n), F32),
        ),
        in_specs=[hbm, hbm] + [vmem] * 4,
        out_specs=(vmem, vmem, vmem),
        scratch_shapes=[
            pltpu.VMEM((n, m_all, q), BF16),
            pltpu.VMEM((m_all, 2, 2, n, q), BF16),
            pltpu.VMEM((dp // 2, 2, mb, kh, q), BF16),
            pltpu.VMEM((ROT, kh, 2 * n2), F32),
            pltpu.VMEM((kh, q), F32),
            pltpu.VMEM((ROT, kh, n2), F32),
            pltpu.VMEM((kh, n2), F32),
            pltpu.VMEM((ROT, kh, 2 * n2), BF16),
            pltpu.VMEM((2, 8, n2), F32),
            pltpu.VMEM((dp * window, q), F32),
            pltpu.VMEM((8, n2), F32),
            pltpu.VMEM((8, n2), F32),
            pltpu.VMEM((window, k), F32),
            pltpu.VMEM((dp, window, k), F32),
            pltpu.VMEM((slots, mb, kh, q), BF16),
            pltpu.VMEM((slots, mb, kh, q), BF16),
            pltpu.VMEM((slots, mb, kh, q), BF16),
            pltpu.VMEM((slots, mb, kh, q), BF16),
            pltpu.VMEM((2, mb, kh, q), BF16),
            pltpu.VMEM((2, mb, kh, q), BF16),
            pltpu.VMEM((2, mb, kh, q), BF16),
            pltpu.VMEM((mb, kh, q), F32),
            pltpu.VMEM((2, mb, kh, q), F32),
            pltpu.VMEM((2, mb, kh, q), BF16),
            pltpu.VMEM((2, 2, mb, kh, q), BF16),
            sem, sem, sem, sem, sem((weighted_chunks,)), sem((weighted_chunks,)), sem, sem,
            sem((slots,)), sem((slots,)), sem((slots,)), sem((slots + 4,)), sem((2,)), sem((2,)),
            sem, sem, sem((dp,)), sem((dp,)),
            sem((slots,)), sem((slots,)), sem((slots,)), sem((slots,)), sem((2,)), sem((2,)),
            sem((2,)), sem((2, 2)), sem, sem,
        ],
        compiler_params=pltpu.CompilerParams(collective_id=0, has_side_effects=True),
        name="step",
    )(
        refs.reshape(mb, 2, kh, q), particles, ctf_group[None, :], defocus[None, :],
        cycle_weight[None, :], class_prior[None, :],
    )

    new_refs, evidence = pl.pallas_call(
        finish_kernel,
        out_shape=(
            jax.ShapeDtypeStruct((mb, 2, kh, q), F32),
            jax.ShapeDtypeStruct((1, n), F32),
        ),
        in_specs=[vmem] * 3,
        out_specs=(vmem, vmem),
        name="finish",
    )(total, inv, ev)
    return (new_refs.reshape(mb, k, q), evidence[0])


def solution(mesh):
    in_specs = (
        P(("groups", "dp"), None, None),
        P("dp", "groups", None),
        P(("groups", "dp")),
        P("groups"),
        P("groups"),
        P(),
    )
    out_specs = (P("dp", "groups", None), P(("groups", "dp")))
    return jax.shard_map(
        functools.partial(shards, mesh.shape["dp"]),
        mesh=mesh, in_specs=in_specs, out_specs=out_specs, check_vma=False,
    )
```

```python
import functools
import math

import jax
import jax.numpy as jnp
from jax import lax
from jax.experimental import pallas as pl
from jax.experimental.pallas import tpu as pltpu
from jax.sharding import PartitionSpec as P

R = 64
ROT = 36
HALF = ROT // 2
NC = HALF + 1
G = 32
MESH = pl.DeviceIdType.MESH
HIGHEST = lax.Precision.HIGHEST
F32 = jnp.float32
BF16 = jnp.bfloat16


def dev(index):
    return {"dp": index}


def dft_even_odd(even_in, odd_in, use_cos):
    f = math.cos if use_cos else math.sin

    def one(items, j):
        total = None
        for i, v in items:
            w = f(2.0 * math.pi * ((i * j) % ROT) / ROT)
            if abs(w) < 1e-12:
                continue
            if abs(w - 1.0) < 1e-12:
                term = v
            elif abs(w + 1.0) < 1e-12:
                term = -v
            else:
                term = v * jnp.float32(w)
            total = term if total is None else total + term
        return total

    count = HALF // 2 + 1
    return [one(even_in, j) for j in range(count)], [one(odd_in, j) for j in range(count)]


def half_transform(values, use_cos):
    even = [(i, v) for i, v in values.items() if i % 2 == 0]
    odd = [(i, v) for i, v in values.items() if i % 2 == 1]
    es, os_ = dft_even_odd(even, odd, use_cos)
    zero = jnp.zeros_like(next(iter(values.values())))
    out = {}
    for j in range(HALF // 2 + 1):
        e = zero if es[j] is None else es[j]
        o = zero if os_[j] is None else os_[j]
        out[j] = e + o
        out[HALF - j] = (e - o) if use_cos else (o - e)
    return out


def step_kernel(zn, dp, window, *refs):
    (refs_ref, part_ref, row_hbm, focus_hbm, cw_hbm, prior_hbm,
     out_ref, inv_ref, ev_ref,
     row_ref, focus_ref, cw_ref, prior_ref, small, part, both, held, cres, energy, sbuf, psum, pp, rows2, table,
     stat, stat_got, mass, mslots,
     xsend, xrecv, zsend, zrecv, xlast, esend, erecv, sib, acc, finx, finz,
     psem, keep, ksend, krecv, wsend, wrecv, rsend, rrecv,
     ax_s, ax_r, az_s, az_r, ae_s, ae_r, ssend, srecv, msend, mrecv,
     rx_s, rx_r, rz_s, rz_r, re_s, re_r, fx_r, fz_r, bsend, brecv) = refs
    me = lax.axis_index("dp")
    z, x, c = me // 4, (me // 2) % 2, me % 2
    o = 1 - c
    y = 1 - x
    n = part.shape[0]
    m_all, q = both.shape[0], both.shape[-1]
    mb, kh = held.shape[2], held.shape[3]
    k = 2 * kh
    n2 = 2 * n
    nall = n * dp
    end = zn - 1

    def at(zz, xx, cc):
        return zz * 4 + xx * 2 + cc

    def chip(zz, xx):
        return zz * 2 + xx

    def remote(src, dst, ss, rs, target):
        return pltpu.make_async_remote_copy(
            src_ref=src, dst_ref=dst, send_sem=ss, recv_sem=rs,
            device_id=dev(target), device_id_type=MESH,
        )

    def is_end(zz):
        return jnp.logical_or(zz == 0, zz == end)

    def inside(zz):
        return jnp.logical_and(zz >= 0, zz < zn)

    def sign_of(s):
        return 1 - 2 * s

    def slot(d, s, e):
        return (d * 2 + s) * 2 + e

    sibling = at(z, x, o)

    barrier = pltpu.get_barrier_semaphore()

    def greet(target):
        pl.semaphore_signal(barrier, inc=1, device_id=dev(target), device_id_type=MESH)

    greet(sibling)
    greet(at(z, y, 0))
    greet(at(z, y, 1))
    for zz in (z - 1, z + 1):
        @pl.when(inside(zz))
        def _():
            greet(at(zz, x, 0))
            greet(at(zz, x, 1))

    smalls = [
        pltpu.make_async_copy(a, b, small.at[i])
        for i, (a, b) in enumerate((
            (row_hbm, row_ref), (focus_hbm, focus_ref), (cw_hbm, cw_ref), (prior_hbm, prior_ref)
        ))
    ]
    for copy in smalls:
        copy.start()
    load = pltpu.make_async_copy(part_ref, part, psem)
    load.start()
    mine = pltpu.make_async_copy(refs_ref.at[:, c], held.at[chip(z, x), c], keep)
    mine.start()

    for copy in smalls:
        copy.wait()
    lane = lax.broadcasted_iota(jnp.int32, (G, q), 1)
    radius = (jnp.where(lane < R, lane, lane - R).astype(F32) + 1.0) / R
    eye = lax.broadcasted_iota(jnp.int32, (G, G), 0) == lax.broadcasted_iota(jnp.int32, (G, G), 1)
    focus = jnp.sum(jnp.where(eye, jnp.broadcast_to(focus_ref[...], (G, G)), 0.0), axis=1, keepdims=True)
    phase = 20.0 * focus * (radius * radius)
    ctf = -(0.995 * jnp.sin(phase) + 0.1 * jnp.cos(phase))
    cw = jnp.concatenate([cw_ref[...], cw_ref[...]], axis=1)
    gain_table = cw * ctf
    power = gain_table * ctf

    onehot = (row_ref[...] == lax.broadcasted_iota(jnp.int32, (G, n), 0)).astype(F32)
    gain = lax.dot_general(
        onehot, gain_table, (((0,), (0,)), ((), ())),
        preferred_element_type=F32, precision=HIGHEST,
    )
    row = row_ref[...].astype(F32)
    rows2[c] = jnp.broadcast_to(jnp.concatenate([row, row], axis=1), rows2.shape[1:])

    pl.semaphore_wait(
        barrier, 3 + 2 * (z > 0).astype(jnp.int32) + 2 * (z < end).astype(jnp.int32)
    )

    here = chip(z, x)

    def first_z(s, e):
        cc = jnp.bitwise_xor(c, e)
        return remote(refs_ref.at[:, cc], held.at[here, c], az_s.at[slot(0, s, e)],
                      az_r.at[slot(1, s, e)], at(z + sign_of(s), x, cc))

    def first_x(e):
        cc = jnp.bitwise_xor(c, e)
        return remote(refs_ref.at[:, cc], held.at[here, c], ax_s.at[slot(0, 0, e)],
                      ax_r.at[slot(0, 0, e)], at(z, y, cc))

    for e in range(2):
        for s in range(2):
            @pl.when(inside(z + sign_of(s)))
            def _():
                first_z(s, e).start()
        first_x(e).start()
    own_half = remote(refs_ref.at[:, o], held.at[here, c], ksend, krecv, sibling)
    own_half.start()
    rows_copy = remote(rows2.at[c], rows2.at[c], rsend, rrecv, sibling)
    rows_copy.start()

    load.wait()
    turn = jnp.where(lax.broadcasted_iota(jnp.int32, (1, 1, q), 2) < R, F32(1.0), F32(-1.0))
    chunk = 16

    def weighted_copy(i):
        span = pl.ds(pl.multiple_of(i * chunk, chunk), chunk)
        return remote(both.at[span, :, c], both.at[span, :, c], wsend.at[i], wrecv.at[i], sibling)

    @pl.loop(0, m_all // chunk)
    def _(i):
        span = pl.ds(pl.multiple_of(i * chunk, chunk), chunk)
        wide = part[:, span, :].astype(F32) * gain[:, None, :]
        w = jnp.swapaxes(wide, 0, 1).astype(BF16)
        both[span, 0, c] = w
        both[span, 1, c] = (pltpu.roll(w.astype(F32), R, 2) * turn).astype(BF16)
        weighted_copy(i).start()

    cres[...] = jnp.zeros_like(cres)
    energy[...] = jnp.zeros_like(energy)
    below = lax.broadcasted_iota(jnp.int32, (window, G), 0) - lax.broadcasted_iota(jnp.int32, (window, G), 1)
    for p in range(dp // 2):
        pick = (below == -((p * n2 * G) // nall)).astype(F32)
        span = jnp.dot(pick, power, precision=HIGHEST, preferred_element_type=F32)
        table[2 * p * window:(2 * p + 1) * window, :] = span
        table[(2 * p + 1) * window:(2 * p + 2) * window, :] = span

    def products(block, cc):
        total = None
        for i in range(mb):
            m = (block * 2 + cc) * mb + i
            r = lax.rem(m, ROT)
            images = both[m].reshape(2 * n2, q)
            ref = held[block, cc, i]
            cres[r] += lax.dot_general(
                ref, images, (((1,), (1,)), ((), ())), preferred_element_type=F32
            )
            wide = ref.astype(F32)
            total = wide * wide if total is None else total + wide * wide
        energy[...] += total

    def z_copy(d, s, e):
        piece = held.at[chip(z - sign_of(s) * d, x), jnp.bitwise_xor(c, e)]
        return remote(piece, piece, az_s.at[slot(d, s, e)], az_r.at[slot(d + 1, s, e)],
                      at(z + sign_of(s), x, c))

    def z_wait(d, s, e):
        piece = held.at[chip(z - sign_of(s) * d, x), jnp.bitwise_xor(c, e)]
        return remote(piece, piece, az_s.at[slot(d, s, e)], az_r.at[slot(d, s, e)], sibling)

    def x_copy(d, s, e):
        piece = held.at[chip(z - sign_of(s) * d, x), jnp.bitwise_xor(c, e)]
        return remote(piece, piece, ax_s.at[slot(d, s, e)], ax_r.at[slot(d, s, e)], at(z, y, c))

    def x_wait(d, s, e):
        piece = held.at[chip(z - sign_of(s) * d, y), jnp.bitwise_xor(c, e)]
        return remote(piece, piece, ax_s.at[slot(d, s, e)], ax_r.at[slot(d, s, e)], sibling)

    def e_piece(s):
        return held.at[chip(s * end, y), o]

    def e_copy(s):
        piece = e_piece(s)
        return remote(piece, piece, ae_s.at[s], ae_r.at[s], at(z + sign_of(s), x, c))

    def by_x(zo, e):
        return jnp.logical_not(jnp.logical_and(e == 1, is_end(zo)))

    def z_held(d, s):
        return jnp.logical_and(d < zn, inside(z - sign_of(s) * d))

    def x_held(d, s, e):
        far = jnp.logical_and(inside(z - sign_of(s) * d), by_x(z - sign_of(s) * d, e))
        return jnp.logical_or(jnp.logical_and(d > 0, far), jnp.logical_and(d == 0, s == 0))

    def z_forward(d, s, e):
        @pl.when(z_held(d, s))
        def _():
            z_wait(d, s, e).wait_recv()

            @pl.when(inside(z + sign_of(s)))
            def _():
                z_copy(d, s, e).start()

            @pl.when(by_x(z - sign_of(s) * d, e))
            def _():
                x_copy(d, s, e).start()

    def half_step(d, e):
        @pl.loop(0, 2)
        def _(s):
            @pl.when(z_held(d, s))
            def _():
                products(chip(z - sign_of(s) * d, x), jnp.bitwise_xor(c, e))

        @pl.loop(0, 2)
        def _(s):
            @pl.when(x_held(d - 1, s, e))
            def _():
                x_wait(d - 1, s, e).wait_recv()
                for t in range(2):
                    @pl.when(jnp.logical_and(jnp.logical_and(d == 1, e == 1), z == t * end))
                    def _():
                        e_copy(t).start()

                products(chip(z - sign_of(s) * (d - 1), y), jnp.bitwise_xor(c, e))

    mine.wait()

    @pl.loop(1, zn + 1)
    def _(d):
        @pl.loop(0, 2)
        def _(e):
            for s in range(2):
                z_forward(d, s, e)

            @pl.when(jnp.logical_and(d == 1, e == 0))
            def _():
                @pl.loop(0, m_all // chunk)
                def _(i):
                    weighted_copy(i).wait_recv()

                own_half.wait_recv()

                @pl.loop(0, 2)
                def _(cc):
                    products(here, cc)

            half_step(d, e)

            @pl.when(e == 0)
            def _():
                @pl.loop(0, 2)
                def _(s):
                    gone = jnp.where(s == 0, z, end - z)

                    @pl.when(jnp.logical_and(gone == d - 1, gone > 0))
                    def _():
                        e_copy(s).wait_recv()

                        @pl.when(gone < end)
                        def _():
                            e_copy(s).start()

                        products(chip(s * end, y), o)

    rows_copy.wait_recv()
    group = jnp.concatenate([rows2[0, 0:1, :n], rows2[1, 0:1, :n]], axis=1)
    hot_g = (group == lax.broadcasted_iota(jnp.int32, (G, n2), 0).astype(F32)).astype(F32)
    quad = lax.dot_general(
        energy[...], power, (((1,), (1,)), ((), ())), preferred_element_type=F32, precision=HIGHEST,
    )
    norm = jnp.dot(quad, hot_g, precision=HIGHEST, preferred_element_type=F32)
    diag = lax.broadcasted_iota(jnp.int32, (kh, k), 0) + c * kh == lax.broadcasted_iota(jnp.int32, (kh, k), 1)
    prior = jnp.sum(jnp.where(diag, jnp.broadcast_to(prior_ref[...], (kh, k)), 0.0), axis=1, keepdims=True)
    psum[...] = jnp.log(prior) - 0.5 * norm

    rows = 16

    def score_rows(i, top):
        span = pl.ds(pl.multiple_of(i * rows, rows), rows)
        re, im = pl.ds(0, n2), pl.ds(n2, n2)
        a = {0: cres[0, span, re], HALF: cres[HALF, span, re]}
        b = {}
        for r in range(1, HALF):
            a[r] = cres[r, span, re] + cres[ROT - r, span, re]
            b[r] = cres[r, span, im] - cres[ROT - r, span, im]
        cosine = half_transform(a, True)
        sine = half_transform(b, False)
        add = psum[span, :]
        for j in range(NC):
            base = cosine[j] + add
            if j in (0, HALF):
                sbuf[j, span, :] = base
                top = jnp.maximum(top, base)
            else:
                low, high = base - sine[j], base + sine[j]
                sbuf[j, span, :] = low
                sbuf[ROT - j, span, :] = high
                top = jnp.maximum(top, jnp.maximum(low, high))
        return top

    top = lax.fori_loop(0, kh // rows, score_rows, jnp.full((rows, n2), -jnp.inf, F32))
    top = jnp.max(top, axis=0, keepdims=True)

    def exp_rows(i, total):
        span = pl.ds(pl.multiple_of(i * rows, rows), rows)
        part_sum = None
        for j in range(ROT):
            value = jnp.exp(sbuf[j, span, :] - top)
            sbuf[j, span, :] = value
            part_sum = value if part_sum is None else part_sum + value
        psum[span, :] = part_sum
        return total + part_sum

    total = lax.fori_loop(0, kh // rows, exp_rows, jnp.zeros((rows, n2), F32))
    total = jnp.sum(total, axis=0, keepdims=True)
    which = lax.broadcasted_iota(jnp.int32, stat.shape, 0)
    stat[...] = jnp.where(which == 0, top, total)
    stat_copy = remote(stat, stat_got, ssend, srecv, sibling)
    stat_copy.start()
    stat_copy.wait_recv()
    other_top, other_total = stat_got[0:1, :], stat_got[1:2, :]
    most = jnp.maximum(top, other_top)
    shrink = jnp.exp(top - most)
    whole = total * shrink + other_total * jnp.exp(other_top - most)
    evidence = most + jnp.log(whole)
    ev_ref[...] = jnp.where(c == 0, evidence[:, :n], evidence[:, n:])
    scale = shrink / whole

    @pl.loop(0, kh // rows)
    def _(i):
        span = pl.ds(pl.multiple_of(i * rows, rows), rows)
        u = {0: sbuf[0, span, :] * scale, HALF: sbuf[HALF, span, :] * scale}
        v = {}
        for j in range(1, HALF):
            low, high = sbuf[j, span, :], sbuf[ROT - j, span, :]
            u[j] = (low + high) * scale
            v[j] = (low - high) * scale
        real = half_transform(u, True)
        imag = half_transform(v, False)
        for r in range(NC):
            re = real[r].astype(BF16)
            im = imag[r].astype(BF16)
            pp[r, span, 0:n2] = re
            pp[r, span, n2:] = -im
            if 0 < r < HALF:
                pp[ROT - r, span, 0:n2] = re
                pp[ROT - r, span, n2:] = im

    def numer(block, cc, i):
        m = (block * 2 + cc) * mb + i
        r = lax.rem(m, ROT)
        return jnp.dot(pp[r], both[m].reshape(2 * n2, q), preferred_element_type=F32)

    def e_sum(s):
        return remote(esend.at[s], erecv.at[s], re_s.at[s], re_r.at[s], at(z + sign_of(s), x, c))

    for s in range(2):
        @pl.when(z == s * end)
        def _():
            for i in range(mb):
                esend[s, i] = numer(chip(end - s * end, y), o, i).astype(BF16)
            e_sum(s).start()

    def x_sum(d, s, e):
        return remote(xsend.at[slot(d, s, e)], xrecv.at[slot(d, s, e)],
                      rx_s.at[slot(d, s, e)], rx_r.at[slot(d, s, e)], at(z, y, c))

    def x_last(e):
        return remote(xlast.at[e], finx.at[c], rx_s.at[slot(0, 0, e)], fx_r.at[c],
                      at(z, y, jnp.bitwise_xor(c, e)))

    def x_goes(d, s, e):
        zo = z + sign_of(s) * d
        return jnp.logical_and(inside(zo), by_x(zo, e))

    @pl.loop(0, zn - 1)
    def _(t):
        d = end - t

        @pl.loop(0, 4)
        def _(j):
            e, s = j // 2, j % 2

            @pl.when(x_goes(d, s, e))
            def _():
                for i in range(mb):
                    xsend[slot(d, s, e), i] = numer(
                        chip(z + sign_of(s) * d, y), jnp.bitwise_xor(c, e), i
                    ).astype(BF16)
                x_sum(d, s, e).start()

    def send_last(e, extra):
        for i in range(mb):
            value = numer(chip(z, y), jnp.bitwise_xor(c, e), i)
            if extra is not None:
                value = value + erecv[extra, i].astype(F32)
            xlast[e, i] = value.astype(BF16)
        x_last(e).start()

    @pl.loop(0, 2)
    def _(e):
        @pl.when(by_x(z, e))
        def _():
            send_last(e, None)

    start = (here * n2 * G) // nall
    hot = (
        group == (lax.broadcasted_iota(jnp.int32, (window, n2), 0) + start).astype(F32)
    ).astype(F32)
    part_mass = lax.dot_general(
        hot, psum[...] * scale, (((1,), (1,)), ((), ())), preferred_element_type=F32, precision=HIGHEST,
    )
    nothing = jnp.zeros_like(part_mass)
    mass[...] = jnp.where(
        c == 0, jnp.concatenate([part_mass, nothing], axis=1), jnp.concatenate([nothing, part_mass], axis=1)
    )
    mslots[me] = mass[...]

    def mass_copy(g):
        return remote(mass, mslots.at[me], msend.at[g], mrecv.at[g], lax.rem(me + g, dp))

    def mass_wait(g):
        return remote(mass, mslots.at[lax.rem(me + dp - g, dp)], msend.at[g], mrecv.at[g], sibling)

    @pl.loop(1, dp)
    def _(g):
        mass_copy(g).start()

    for i in range(mb):
        sib[i] = numer(here, o, i)
    sib_copy = remote(sib, acc.at[c], bsend, brecv, sibling)
    sib_copy.start()

    def z_sum(d, s, e):
        return remote(zsend.at[slot(d, s, e)], zrecv.at[slot(d - 1, s, e)],
                      rz_s.at[slot(d, s, e)], rz_r.at[slot(d - 1, s, e)], at(z + sign_of(s), x, c))

    def z_got(d, s, e):
        return remote(zsend.at[slot(d, s, e)], zrecv.at[slot(d, s, e)],
                      rz_s.at[slot(d, s, e)], rz_r.at[slot(d, s, e)], sibling)

    def z_last(s, e):
        return remote(zsend.at[slot(1, s, e)], finz.at[s, c], rz_s.at[slot(1, s, e)], fz_r.at[s, c],
                      at(z + sign_of(s), x, jnp.bitwise_xor(c, e)))

    near = (2 * z < zn).astype(jnp.int32)

    @pl.loop(0, zn - 1)
    def _(t):
        d = end - t

        for s in range(2):
            left = (end - z) if s == 0 else z

            @pl.when(jnp.logical_and(left == d, left < end))
            def _():
                e_sum(s).wait_recv()
                for i in range(mb):
                    esend[s, i] = (numer(chip(end - s * end, y), o, i) + erecv[s, i].astype(F32)).astype(BF16)
                e_sum(s).start()

        for s in range(2):
            @pl.when(jnp.logical_and(d == 1, z == (1 - s) * end))
            def _():
                e_sum(s).wait_recv()
                send_last(1, s)

        @pl.loop(0, 4)
        def _(j):
            e = 1 - j // 2
            s = jnp.bitwise_xor(j % 2, near)
            zo = z + sign_of(s) * d

            @pl.when(inside(zo))
            def _():
                here_slot = slot(d, s, e)
                crossed = by_x(zo, e)
                line = inside(z - sign_of(s))
                for i in range(mb):
                    acc[c, i] = numer(chip(zo, x), jnp.bitwise_xor(c, e), i)

                @pl.when(crossed)
                def _():
                    x_sum(d, s, e).wait_recv()
                    for i in range(mb):
                        acc[c, i] += xrecv[here_slot, i].astype(F32)

                @pl.when(line)
                def _():
                    z_got(d, s, e).wait_recv()
                    for i in range(mb):
                        acc[c, i] += zrecv[here_slot, i].astype(F32)

                for i in range(mb):
                    zsend[here_slot, i] = acc[c, i].astype(BF16)

                @pl.when(d > 1)
                def _():
                    z_sum(d, s, e).start()

                @pl.when(d == 1)
                def _():
                    z_last(s, e).start()

    for i in range(mb):
        acc[c, i] = numer(here, c, i)

    @pl.loop(1, dp)
    def _(g):
        mass_wait(g).wait_recv()

    denom = 1.0 + lax.dot_general(
        mslots[...].reshape(dp * window, k), table[...], (((0,), (0,)), ((), ())),
        preferred_element_type=F32, precision=HIGHEST,
    )
    inv_ref[...] = (1.0 / denom).reshape(inv_ref.shape)
    sib_copy.wait_recv()

    for h in range(2):
        remote(xlast.at[0], finx.at[h], rx_s.at[slot(0, 0, 0)], fx_r.at[h], sibling).wait_recv()
        acc[h] += finx[h].astype(F32)
    for s in range(2):
        @pl.when(inside(z - sign_of(s)))
        def _():
            for h in range(2):
                remote(xlast.at[0], finz.at[s, h], rx_s.at[slot(0, 0, 0)], fz_r.at[s, h], sibling).wait_recv()
                acc[h] += finz[s, h].astype(F32)
    for h in range(2):
        out_ref[:, h] = acc[h]

    for e in range(2):
        for s in range(2):
            @pl.when(inside(z + sign_of(s)))
            def _():
                first_z(s, e).wait_send()
        first_x(e).wait_send()
    own_half.wait_send()
    rows_copy.wait_send()
    stat_copy.wait_send()
    sib_copy.wait_send()

    @pl.loop(0, m_all // chunk)
    def _(i):
        weighted_copy(i).wait_send()

    @pl.loop(1, zn)
    def _(d):
        @pl.loop(0, 4)
        def _(j):
            e, s = j // 2, j % 2
            zo = z - sign_of(s) * d

            @pl.when(z_held(d, s))
            def _():
                @pl.when(inside(z + sign_of(s)))
                def _():
                    z_copy(d, s, e).wait_send()

                @pl.when(by_x(zo, e))
                def _():
                    x_copy(d, s, e).wait_send()

            @pl.when(x_goes(d, s, e))
            def _():
                x_sum(d, s, e).wait_send()

            @pl.when(inside(z + sign_of(s) * d))
            def _():
                z_got(d, s, e).wait_send()

    for s in range(2):
        @pl.when(inside(z + sign_of(s)))
        def _():
            e_copy(s).wait_send()
            e_sum(s).wait_send()
    for e in range(2):
        x_last(e).wait_send()

    @pl.loop(1, dp)
    def _(g):
        mass_copy(g).wait_send()


def finish_kernel(total_ref, inv_ref, ev_ref, out_ref, evidence_ref, buf, sems):
    copies = []
    for i in range(total_ref.shape[0]):
        buf[i] = total_ref[i] * inv_ref[...]
        copy = pltpu.make_async_copy(buf.at[i], out_ref.at[i], sems.at[i])
        copy.start()
        copies.append(copy)
    evidence_ref[...] = ev_ref[...]
    for copy in copies:
        copy.wait()


def shards(dp, particles, refs, ctf_group, defocus, class_prior, cycle_weight):
    n, m_all, q = particles.shape
    mb, k, _ = refs.shape
    zn = dp // 4
    nall = n * dp
    kh = k // 2
    n2 = 2 * n
    window = -(-((n2 * G) // nall + 3) // 8) * 8
    slots = 4 * zn
    weighted_chunks = m_all // 16

    vmem = pl.BlockSpec(memory_space=pltpu.VMEM)
    hbm = pl.BlockSpec(memory_space=pl.ANY)
    sem = pltpu.SemaphoreType.DMA
    total, inv, ev = pl.pallas_call(
        functools.partial(step_kernel, zn, dp, window),
        out_shape=(
            jax.ShapeDtypeStruct((mb, 2, kh, q), F32),
            jax.ShapeDtypeStruct((2, kh, q), F32),
            jax.ShapeDtypeStruct((1, n), F32),
        ),
        in_specs=[pl.BlockSpec(memory_space=pltpu.MemorySpace.HBM)] * 6,
        out_specs=(vmem, vmem, vmem),
        scratch_shapes=[
            pltpu.VMEM((1, n), jnp.int32), pltpu.VMEM((1, G), F32),
            pltpu.VMEM((1, R), F32), pltpu.VMEM((1, k), F32), sem((4,)),
            pltpu.VMEM((n, m_all, q), BF16),
            pltpu.VMEM((m_all, 2, 2, n, q), BF16),
            pltpu.VMEM((dp // 2, 2, mb, kh, q), BF16),
            pltpu.VMEM((ROT, kh, 2 * n2), F32),
            pltpu.VMEM((kh, q), F32),
            pltpu.VMEM((ROT, kh, n2), F32),
            pltpu.VMEM((kh, n2), F32),
            pltpu.VMEM((ROT, kh, 2 * n2), BF16),
            pltpu.VMEM((2, 8, n2), F32),
            pltpu.VMEM((dp * window, q), F32),
            pltpu.VMEM((8, n2), F32),
            pltpu.VMEM((8, n2), F32),
            pltpu.VMEM((window, k), F32),
            pltpu.VMEM((dp, window, k), F32),
            pltpu.VMEM((slots, mb, kh, q), BF16),
            pltpu.VMEM((slots, mb, kh, q), BF16),
            pltpu.VMEM((slots, mb, kh, q), BF16),
            pltpu.VMEM((slots, mb, kh, q), BF16),
            pltpu.VMEM((2, mb, kh, q), BF16),
            pltpu.VMEM((2, mb, kh, q), BF16),
            pltpu.VMEM((2, mb, kh, q), BF16),
            pltpu.VMEM((mb, kh, q), F32),
            pltpu.VMEM((2, mb, kh, q), F32),
            pltpu.VMEM((2, mb, kh, q), BF16),
            pltpu.VMEM((2, 2, mb, kh, q), BF16),
            sem, sem, sem, sem, sem((weighted_chunks,)), sem((weighted_chunks,)), sem, sem,
            sem((slots,)), sem((slots,)), sem((slots,)), sem((slots + 4,)), sem((2,)), sem((2,)),
            sem, sem, sem((dp,)), sem((dp,)),
            sem((slots,)), sem((slots,)), sem((slots,)), sem((slots,)), sem((2,)), sem((2,)),
            sem((2,)), sem((2, 2)), sem, sem,
        ],
        compiler_params=pltpu.CompilerParams(
            collective_id=0, has_side_effects=True, vmem_limit_bytes=40 << 20
        ),
        name="step",
    )(*(
        pltpu.with_memory_space_constraint(a, pltpu.MemorySpace.HBM) for a in (
            refs.reshape(mb, 2, kh, q), particles, ctf_group[None, :], defocus[None, :],
            cycle_weight[None, :], class_prior[None, :],
        )
    ))

    new_refs, evidence = pl.pallas_call(
        finish_kernel,
        out_shape=(
            jax.ShapeDtypeStruct((mb, 2, kh, q), F32),
            jax.ShapeDtypeStruct((1, n), F32),
        ),
        in_specs=[vmem] * 3,
        out_specs=(hbm, vmem),
        scratch_shapes=[pltpu.VMEM((mb, 2, kh, q), F32), sem((mb,))],
        compiler_params=pltpu.CompilerParams(vmem_limit_bytes=8 << 20),
        name="finish",
    )(total, inv, ev)
    return (new_refs.reshape(mb, k, q), evidence[0])


def solution(mesh):
    in_specs = (
        P(("groups", "dp"), None, None),
        P("dp", "groups", None),
        P(("groups", "dp")),
        P("groups"),
        P("groups"),
        P(),
    )
    out_specs = (P("dp", "groups", None), P(("groups", "dp")))
    return jax.shard_map(
        functools.partial(shards, mesh.shape["dp"]),
        mesh=mesh, in_specs=in_specs, out_specs=out_specs, check_vma=False,
    )
```

```python
import functools
import math

import jax
import jax.numpy as jnp
from jax import lax
from jax.experimental import pallas as pl
from jax.experimental.pallas import tpu as pltpu
from jax.sharding import PartitionSpec as P

R = 64
ROT = 36
HALF = ROT // 2
NC = HALF + 1
G = 32
MESH = pl.DeviceIdType.MESH
HIGHEST = lax.Precision.HIGHEST
F32 = jnp.float32
BF16 = jnp.bfloat16


def dev(index):
    return {"dp": index}


def cosine9(x, a):
    c1, c2, c4 = (jnp.float32(math.cos(2.0 * math.pi * p / 9)) for p in (1, 2, 4))
    a1, a2, a3, a4 = a
    both = a1 + a2 + a4
    near = x + a3
    base = x - a3 * jnp.float32(0.5)
    d1, d2 = a1 - a4, a2 - a4
    y1 = c1 * d1 + c2 * d2
    y2 = c2 * d1 + c4 * d2
    return [near + both, base + y1, base + y2, near - both * jnp.float32(0.5), base - (y1 + y2)]


def sine9(b):
    s1, s4 = (jnp.float32(math.sin(2.0 * math.pi * p / 9)) for p in (1, 4))
    half = jnp.float32(math.sqrt(3.0) / 2.0)
    b1, b2, b3, b4 = b
    e1, e2 = b1 + b2, b2 + b4
    e3 = b1 - b4
    t = half * b3
    z1 = s1 * e1 + s4 * e2
    z2 = s1 * e3 + s4 * e1
    return [z1 + t, z2 - t, half * (b1 - b2 + b4), (z2 - z1) + t]


def turns(real, imag):
    a = {r: real(r) + real(ROT - r) for r in range(1, ROT) if r % 9 in (1, 2, 3, 4)}
    b = {r: imag(r) - imag(ROT - r) for r in a}
    a9, b9 = real(9) + real(27), imag(9) - imag(27)
    first, last = real(0), real(18)
    up, down = first + last, first - last
    flat = [up + a9, down - b9, up - a9, down + b9]
    cos_in, sin_in = [[], [], [], []], [[], [], [], []]
    for p in range(1, 5):
        r = [(9 * i + 28 * p) % ROT for i in range(4)]
        re, im = [a[v] for v in r], [b[v] for v in r]
        re02, re13, im02, im13 = re[0] + re[2], re[1] + re[3], im[0] + im[2], im[1] + im[3]
        dr02, dr13, di02, di13 = re[0] - re[2], re[1] - re[3], im[0] - im[2], im[1] - im[3]
        for t, v in enumerate((re02 + re13, dr02 - di13, re02 - re13, dr02 + di13)):
            cos_in[t].append(v)
        for t, v in enumerate((im02 + im13, di02 + dr13, im02 - im13, di02 - dr13)):
            sin_in[t].append(v)
    out = {}
    for t in range(4):
        cosine, sine = cosine9(flat[t], cos_in[t]), sine9(sin_in[t])
        out[(9 * t) % ROT] = cosine[0]
        for g in range(1, 5):
            out[(9 * t + 4 * g) % ROT] = cosine[g] - sine[g - 1]
            out[(9 * t + 4 * (9 - g)) % ROT] = cosine[g] + sine[g - 1]
    return out


def harmonics(value):
    real, imag = [], []
    for t in range(4):
        v = [value((9 * t + 4 * g) % ROT) for g in range(9)]
        real.append(cosine9(v[0], [v[g] + v[9 - g] for g in range(1, 5)]))
        imag.append(sine9([v[g] - v[9 - g] for g in range(1, 5)]))
    re, im = {}, {}

    def put(r, x, y):
        if r <= HALF:
            re[r] = x
            if y is not None:
                im[r] = y
        else:
            re[ROT - r] = x
            if y is not None:
                im[ROT - r] = -y

    x = [real[t][0] for t in range(4)]
    put(0, (x[0] + x[2]) + (x[1] + x[3]), None)
    put(18, (x[0] + x[2]) - (x[1] + x[3]), None)
    put(9, x[0] - x[2], x[1] - x[3])
    for p in range(1, 5):
        x = [real[t][p] for t in range(4)]
        y = [imag[t][p - 1] for t in range(4)]
        sx, tx, sy, ty = x[0] + x[2], x[1] + x[3], y[0] + y[2], y[1] + y[3]
        dx, ex, dy, ey = x[0] - x[2], x[1] - x[3], y[0] - y[2], y[1] - y[3]
        put((28 * p) % ROT, sx + tx, sy + ty)
        put((9 + 28 * p) % ROT, dx - ey, dy + ex)
        put((18 + 28 * p) % ROT, sx - tx, sy - ty)
        put((27 + 28 * p) % ROT, dx + ey, dy - ex)
    return re, im


def step_kernel(zn, dp, window, *refs):
    (refs_ref, part_ref, row_hbm, focus_hbm, cw_hbm, prior_hbm,
     out_ref, ev_ref,
     inv, row_ref, focus_ref, cw_ref, prior_ref, small, part, both, held, cres, energy, sbuf, psum, pp, rows2, table,
     stat, stat_got, mass, mslots,
     xsend, xrecv, zsend, zrecv, xlast, esend, erecv, sib, acc, finx, finz,
     psem, keep, ksend, krecv, wsend, wrecv, rsend, rrecv,
     ax_s, ax_r, az_s, az_r, ae_s, ae_r, ssend, srecv, msend, mrecv,
     rx_s, rx_r, rz_s, rz_r, re_s, re_r, fx_r, fz_r, bsend, brecv) = refs
    me = lax.axis_index("dp")
    z, x, c = me // 4, (me // 2) % 2, me % 2
    o = 1 - c
    y = 1 - x
    n = part.shape[0]
    m_all, q = both.shape[0], both.shape[-1]
    mb, kh = held.shape[2], held.shape[3]
    k = 2 * kh
    n2 = 2 * n
    nall = n * dp
    end = zn - 1

    def at(zz, xx, cc):
        return zz * 4 + xx * 2 + cc

    def chip(zz, xx):
        return zz * 2 + xx

    def remote(src, dst, ss, rs, target):
        return pltpu.make_async_remote_copy(
            src_ref=src, dst_ref=dst, send_sem=ss, recv_sem=rs,
            device_id=dev(target), device_id_type=MESH,
        )

    def is_end(zz):
        return jnp.logical_or(zz == 0, zz == end)

    def inside(zz):
        return jnp.logical_and(zz >= 0, zz < zn)

    def sign_of(s):
        return 1 - 2 * s

    def slot(d, s, e):
        return (d * 2 + s) * 2 + e

    sibling = at(z, x, o)

    barrier = pltpu.get_barrier_semaphore()

    def greet(target):
        pl.semaphore_signal(barrier, inc=1, device_id=dev(target), device_id_type=MESH)

    greet(sibling)
    greet(at(z, y, 0))
    greet(at(z, y, 1))
    for zz in (z - 1, z + 1):
        @pl.when(inside(zz))
        def _():
            greet(at(zz, x, 0))
            greet(at(zz, x, 1))

    smalls = [
        pltpu.make_async_copy(a, b, small.at[i])
        for i, (a, b) in enumerate((
            (row_hbm, row_ref), (focus_hbm, focus_ref), (cw_hbm, cw_ref), (prior_hbm, prior_ref)
        ))
    ]
    for copy in smalls:
        copy.start()
    load = pltpu.make_async_copy(part_ref, part, psem)
    load.start()
    mine = pltpu.make_async_copy(refs_ref.at[:, c], held.at[chip(z, x), c], keep)
    mine.start()

    for copy in smalls:
        copy.wait()
    lane = lax.broadcasted_iota(jnp.int32, (G, q), 1)
    radius = (jnp.where(lane < R, lane, lane - R).astype(F32) + 1.0) / R
    eye = lax.broadcasted_iota(jnp.int32, (G, G), 0) == lax.broadcasted_iota(jnp.int32, (G, G), 1)
    focus = jnp.sum(jnp.where(eye, jnp.broadcast_to(focus_ref[...], (G, G)), 0.0), axis=1, keepdims=True)
    phase = 20.0 * focus * (radius * radius)
    ctf = -(0.995 * jnp.sin(phase) + 0.1 * jnp.cos(phase))
    cw = jnp.concatenate([cw_ref[...], cw_ref[...]], axis=1)
    gain_table = cw * ctf
    power = gain_table * ctf

    onehot = (row_ref[...] == lax.broadcasted_iota(jnp.int32, (G, n), 0)).astype(F32)
    gain = lax.dot_general(
        onehot, gain_table, (((0,), (0,)), ((), ())),
        preferred_element_type=F32, precision=HIGHEST,
    )
    row = row_ref[...].astype(F32)
    rows2[c] = jnp.broadcast_to(jnp.concatenate([row, row], axis=1), rows2.shape[1:])

    pl.semaphore_wait(
        barrier, 3 + 2 * (z > 0).astype(jnp.int32) + 2 * (z < end).astype(jnp.int32)
    )

    here = chip(z, x)

    def first_z(s, e):
        cc = jnp.bitwise_xor(c, e)
        return remote(refs_ref.at[:, cc], held.at[here, c], az_s.at[slot(0, s, e)],
                      az_r.at[slot(1, s, e)], at(z + sign_of(s), x, cc))

    def first_x(e):
        cc = jnp.bitwise_xor(c, e)
        return remote(refs_ref.at[:, cc], held.at[here, c], ax_s.at[slot(0, 0, e)],
                      ax_r.at[slot(0, 0, e)], at(z, y, cc))

    for e in range(2):
        for s in range(2):
            @pl.when(inside(z + sign_of(s)))
            def _():
                first_z(s, e).start()
        first_x(e).start()
    own_half = remote(refs_ref.at[:, o], held.at[here, c], ksend, krecv, sibling)
    own_half.start()
    rows_copy = remote(rows2.at[c], rows2.at[c], rsend, rrecv, sibling)
    rows_copy.start()

    load.wait()
    turn = jnp.where(lax.broadcasted_iota(jnp.int32, (1, 1, q), 2) < R, F32(1.0), F32(-1.0))
    chunk = 16

    def weighted_copy(i):
        span = pl.ds(pl.multiple_of(i * chunk, chunk), chunk)
        return remote(both.at[span, :, c], both.at[span, :, c], wsend.at[i], wrecv.at[i], sibling)

    @pl.loop(0, m_all // chunk)
    def _(i):
        span = pl.ds(pl.multiple_of(i * chunk, chunk), chunk)
        wide = part[:, span, :].astype(F32) * gain[:, None, :]
        w = jnp.swapaxes(wide, 0, 1).astype(BF16)
        both[span, 0, c] = w
        both[span, 1, c] = (pltpu.roll(w.astype(F32), R, 2) * turn).astype(BF16)
        weighted_copy(i).start()

    cres[...] = jnp.zeros_like(cres)
    energy[...] = jnp.zeros_like(energy)
    below = lax.broadcasted_iota(jnp.int32, (window, G), 0) - lax.broadcasted_iota(jnp.int32, (window, G), 1)
    for p in range(dp // 2):
        pick = (below == -((p * n2 * G) // nall)).astype(F32)
        span = jnp.dot(pick, power, precision=HIGHEST, preferred_element_type=F32)
        table[2 * p * window:(2 * p + 1) * window, :] = span
        table[(2 * p + 1) * window:(2 * p + 2) * window, :] = span

    def products(block, cc):
        total = None
        for i in range(mb):
            m = (block * 2 + cc) * mb + i
            r = lax.rem(m, ROT)
            images = both[m].reshape(2 * n2, q)
            ref = held[block, cc, i]
            cres[r] += lax.dot_general(
                ref, images, (((1,), (1,)), ((), ())), preferred_element_type=F32
            )
            wide = ref.astype(F32)
            total = wide * wide if total is None else total + wide * wide
        energy[...] += total

    def z_copy(d, s, e):
        piece = held.at[chip(z - sign_of(s) * d, x), jnp.bitwise_xor(c, e)]
        return remote(piece, piece, az_s.at[slot(d, s, e)], az_r.at[slot(d + 1, s, e)],
                      at(z + sign_of(s), x, c))

    def z_wait(d, s, e):
        piece = held.at[chip(z - sign_of(s) * d, x), jnp.bitwise_xor(c, e)]
        return remote(piece, piece, az_s.at[slot(d, s, e)], az_r.at[slot(d, s, e)], sibling)

    def x_copy(d, s, e):
        piece = held.at[chip(z - sign_of(s) * d, x), jnp.bitwise_xor(c, e)]
        return remote(piece, piece, ax_s.at[slot(d, s, e)], ax_r.at[slot(d, s, e)], at(z, y, c))

    def x_wait(d, s, e):
        piece = held.at[chip(z - sign_of(s) * d, y), jnp.bitwise_xor(c, e)]
        return remote(piece, piece, ax_s.at[slot(d, s, e)], ax_r.at[slot(d, s, e)], sibling)

    def e_piece(s):
        return held.at[chip(s * end, y), o]

    def e_copy(s):
        piece = e_piece(s)
        return remote(piece, piece, ae_s.at[s], ae_r.at[s], at(z + sign_of(s), x, c))

    def by_x(zo, e):
        return jnp.logical_not(jnp.logical_and(e == 1, is_end(zo)))

    def z_held(d, s):
        return jnp.logical_and(d < zn, inside(z - sign_of(s) * d))

    def x_held(d, s, e):
        far = jnp.logical_and(inside(z - sign_of(s) * d), by_x(z - sign_of(s) * d, e))
        return jnp.logical_or(jnp.logical_and(d > 0, far), jnp.logical_and(d == 0, s == 0))

    def z_forward(d, s, e):
        @pl.when(z_held(d, s))
        def _():
            z_wait(d, s, e).wait_recv()

            @pl.when(inside(z + sign_of(s)))
            def _():
                z_copy(d, s, e).start()

            @pl.when(by_x(z - sign_of(s) * d, e))
            def _():
                x_copy(d, s, e).start()

    def half_step_z(d, e):
        @pl.loop(0, 2)
        def _(s):
            @pl.when(z_held(d, s))
            def _():
                products(chip(z - sign_of(s) * d, x), jnp.bitwise_xor(c, e))

    def half_step_x(d, e):
        @pl.loop(0, 2)
        def _(s):
            @pl.when(x_held(d - 1, s, e))
            def _():
                x_wait(d - 1, s, e).wait_recv()
                for t in range(2):
                    @pl.when(jnp.logical_and(jnp.logical_and(d == 1, e == 1), z == t * end))
                    def _():
                        e_copy(t).start()

                products(chip(z - sign_of(s) * (d - 1), y), jnp.bitwise_xor(c, e))

    mine.wait()

    @pl.loop(1, zn + 1)
    def _(d):
        @pl.loop(0, 2)
        def _(e):
            for s in range(2):
                z_forward(d, s, e)

            @pl.when(jnp.logical_and(d == 1, e == 0))
            def _():
                @pl.loop(0, m_all // chunk)
                def _(i):
                    weighted_copy(i).wait_recv()

                own_half.wait_recv()

                @pl.loop(0, 2)
                def _(cc):
                    products(here, cc)

            half_step_z(d, e)

            @pl.when(e == 0)
            def _():
                @pl.loop(0, 2)
                def _(s):
                    gone = jnp.where(s == 0, z, end - z)

                    @pl.when(jnp.logical_and(gone == d - 1, gone > 0))
                    def _():
                        e_copy(s).wait_recv()

                        @pl.when(gone < end)
                        def _():
                            e_copy(s).start()

                        products(chip(s * end, y), o)

            half_step_x(d, e)

    rows_copy.wait_recv()
    group = jnp.concatenate([rows2[0, 0:1, :n], rows2[1, 0:1, :n]], axis=1)
    hot_g = (group == lax.broadcasted_iota(jnp.int32, (G, n2), 0).astype(F32)).astype(F32)
    quad = lax.dot_general(
        energy[...], power, (((1,), (1,)), ((), ())), preferred_element_type=F32, precision=HIGHEST,
    )
    norm = jnp.dot(quad, hot_g, precision=HIGHEST, preferred_element_type=F32)
    diag = lax.broadcasted_iota(jnp.int32, (kh, k), 0) + c * kh == lax.broadcasted_iota(jnp.int32, (kh, k), 1)
    prior = jnp.sum(jnp.where(diag, jnp.broadcast_to(prior_ref[...], (kh, k)), 0.0), axis=1, keepdims=True)
    psum[...] = jnp.log(prior) - 0.5 * norm

    rows = 8

    def score_rows(i, top):
        span = pl.ds(pl.multiple_of(i * rows, rows), rows)
        re, im = pl.ds(0, n2), pl.ds(n2, n2)
        corr = turns(lambda r: cres[r, span, re], lambda r: cres[r, span, im])
        best = None
        for j in range(ROT):
            sbuf[j, span, :] = corr[j]
            best = corr[j] if best is None else jnp.maximum(best, corr[j])
        return jnp.maximum(top, best + psum[span, :])

    top = lax.fori_loop(0, kh // rows, score_rows, jnp.full((rows, n2), -jnp.inf, F32))
    top = jnp.max(top, axis=0, keepdims=True)

    def exp_rows(i, total):
        span = pl.ds(pl.multiple_of(i * rows, rows), rows)
        part_sum = None
        shift = psum[span, :] - top
        for j in range(ROT):
            value = jnp.exp(sbuf[j, span, :] + shift)
            sbuf[j, span, :] = value
            part_sum = value if part_sum is None else part_sum + value
        psum[span, :] = part_sum
        return total + part_sum

    total = lax.fori_loop(0, kh // rows, exp_rows, jnp.zeros((rows, n2), F32))
    total = jnp.sum(total, axis=0, keepdims=True)
    which = lax.broadcasted_iota(jnp.int32, stat.shape, 0)
    stat[...] = jnp.where(which == 0, top, total)
    stat_copy = remote(stat, stat_got, ssend, srecv, sibling)
    stat_copy.start()

    @pl.loop(0, kh // rows)
    def _(i):
        span = pl.ds(pl.multiple_of(i * rows, rows), rows)
        real, imag = harmonics(lambda j: sbuf[j, span, :])
        for r in range(NC):
            sbuf[r, span, :] = real[r]
        for r in range(1, HALF):
            sbuf[HALF + r, span, :] = imag[r]

    stat_copy.wait_recv()
    other_top, other_total = stat_got[0:1, :], stat_got[1:2, :]
    most = jnp.maximum(top, other_top)
    shrink = jnp.exp(top - most)
    whole = total * shrink + other_total * jnp.exp(other_top - most)
    evidence = most + jnp.log(whole)
    ev_ref[...] = jnp.where(c == 0, evidence[:, :n], evidence[:, n:])
    scale = shrink / whole

    tile = 16

    @pl.loop(0, kh // tile)
    def _(i):
        span = pl.ds(pl.multiple_of(i * tile, tile), tile)
        for r in range(NC):
            re = (sbuf[r, span, :] * scale).astype(BF16)
            pp[r, span, 0:n2] = re
            if r in (0, HALF):
                pp[r, span, n2:] = jnp.zeros_like(re)
            else:
                im = (sbuf[HALF + r, span, :] * scale).astype(BF16)
                pp[r, span, n2:] = -im
                pp[ROT - r, span, 0:n2] = re
                pp[ROT - r, span, n2:] = im

    def numer(block, cc, i):
        m = (block * 2 + cc) * mb + i
        r = lax.rem(m, ROT)
        return jnp.dot(pp[r], both[m].reshape(2 * n2, q), preferred_element_type=F32)

    def e_sum(s):
        return remote(esend.at[s], erecv.at[s], re_s.at[s], re_r.at[s], at(z + sign_of(s), x, c))

    for s in range(2):
        @pl.when(z == s * end)
        def _():
            for i in range(mb):
                esend[s, i] = numer(chip(end - s * end, y), o, i).astype(BF16)
            e_sum(s).start()

    def x_sum(d, s, e):
        return remote(xsend.at[slot(d, s, e)], xrecv.at[slot(d, s, e)],
                      rx_s.at[slot(d, s, e)], rx_r.at[slot(d, s, e)], at(z, y, c))

    def x_last(e):
        return remote(xlast.at[e], finx.at[c], rx_s.at[slot(0, 0, e)], fx_r.at[c],
                      at(z, y, jnp.bitwise_xor(c, e)))

    def x_goes(d, s, e):
        zo = z + sign_of(s) * d
        return jnp.logical_and(inside(zo), by_x(zo, e))

    @pl.loop(0, zn - 1)
    def _(t):
        d = end - t

        @pl.loop(0, 4)
        def _(j):
            e, s = 1 - j // 2, j % 2

            @pl.when(x_goes(d, s, e))
            def _():
                for i in range(mb):
                    xsend[slot(d, s, e), i] = numer(
                        chip(z + sign_of(s) * d, y), jnp.bitwise_xor(c, e), i
                    ).astype(BF16)
                x_sum(d, s, e).start()

    def send_last(e, extra):
        for i in range(mb):
            value = numer(chip(z, y), jnp.bitwise_xor(c, e), i)
            if extra is not None:
                value = value + erecv[extra, i].astype(F32)
            xlast[e, i] = value.astype(BF16)
        x_last(e).start()

    @pl.loop(0, 2)
    def _(e):
        @pl.when(by_x(z, e))
        def _():
            send_last(e, None)

    start = (here * n2 * G) // nall
    hot = (
        group == (lax.broadcasted_iota(jnp.int32, (window, n2), 0) + start).astype(F32)
    ).astype(F32)
    part_mass = lax.dot_general(
        hot, psum[...] * scale, (((1,), (1,)), ((), ())), preferred_element_type=F32, precision=HIGHEST,
    )
    nothing = jnp.zeros_like(part_mass)
    mass[...] = jnp.where(
        c == 0, jnp.concatenate([part_mass, nothing], axis=1), jnp.concatenate([nothing, part_mass], axis=1)
    )
    mslots[me] = mass[...]

    def mass_copy(g):
        return remote(mass, mslots.at[me], msend.at[g], mrecv.at[g], lax.rem(me + g, dp))

    def mass_wait(g):
        return remote(mass, mslots.at[lax.rem(me + dp - g, dp)], msend.at[g], mrecv.at[g], sibling)

    @pl.loop(1, dp)
    def _(g):
        mass_copy(g).start()

    for i in range(mb):
        sib[i] = numer(here, o, i)
    sib_copy = remote(sib, acc.at[c], bsend, brecv, sibling)
    sib_copy.start()

    def z_sum(d, s, e):
        return remote(zsend.at[slot(d, s, e)], zrecv.at[slot(d - 1, s, e)],
                      rz_s.at[slot(d, s, e)], rz_r.at[slot(d - 1, s, e)], at(z + sign_of(s), x, c))

    def z_got(d, s, e):
        return remote(zsend.at[slot(d, s, e)], zrecv.at[slot(d, s, e)],
                      rz_s.at[slot(d, s, e)], rz_r.at[slot(d, s, e)], sibling)

    def z_last(s, e):
        return remote(zsend.at[slot(1, s, e)], finz.at[s, c], rz_s.at[slot(1, s, e)], fz_r.at[s, c],
                      at(z + sign_of(s), x, jnp.bitwise_xor(c, e)))

    near = (2 * z < zn).astype(jnp.int32)

    @pl.loop(0, zn - 1)
    def _(t):
        d = end - t

        for s in range(2):
            left = (end - z) if s == 0 else z

            @pl.when(jnp.logical_and(left == d, left < end))
            def _():
                e_sum(s).wait_recv()
                for i in range(mb):
                    esend[s, i] = (numer(chip(end - s * end, y), o, i) + erecv[s, i].astype(F32)).astype(BF16)
                e_sum(s).start()

        for s in range(2):
            @pl.when(jnp.logical_and(d == 1, z == (1 - s) * end))
            def _():
                e_sum(s).wait_recv()
                send_last(1, s)

        @pl.loop(0, 4)
        def _(j):
            e = 1 - j // 2
            s = jnp.bitwise_xor(j % 2, near)
            zo = z + sign_of(s) * d

            @pl.when(inside(zo))
            def _():
                here_slot = slot(d, s, e)
                crossed = by_x(zo, e)
                line = inside(z - sign_of(s))
                for i in range(mb):
                    acc[c, i] = numer(chip(zo, x), jnp.bitwise_xor(c, e), i)

                @pl.when(crossed)
                def _():
                    x_sum(d, s, e).wait_recv()
                    for i in range(mb):
                        acc[c, i] += xrecv[here_slot, i].astype(F32)

                @pl.when(line)
                def _():
                    z_got(d, s, e).wait_recv()
                    for i in range(mb):
                        acc[c, i] += zrecv[here_slot, i].astype(F32)

                for i in range(mb):
                    zsend[here_slot, i] = acc[c, i].astype(BF16)

                @pl.when(d > 1)
                def _():
                    z_sum(d, s, e).start()

                @pl.when(d == 1)
                def _():
                    z_last(s, e).start()

    for i in range(mb):
        acc[c, i] = numer(here, c, i)

    for e in range(2):
        for s in range(2):
            @pl.when(inside(z + sign_of(s)))
            def _():
                first_z(s, e).wait_send()
        first_x(e).wait_send()
    own_half.wait_send()
    rows_copy.wait_send()
    stat_copy.wait_send()
    sib_copy.wait_send()

    @pl.loop(0, m_all // chunk)
    def _(i):
        weighted_copy(i).wait_send()

    @pl.loop(1, zn)
    def _(d):
        @pl.loop(0, 4)
        def _(j):
            e, s = j // 2, j % 2
            zo = z - sign_of(s) * d

            @pl.when(z_held(d, s))
            def _():
                @pl.when(inside(z + sign_of(s)))
                def _():
                    z_copy(d, s, e).wait_send()

                @pl.when(by_x(zo, e))
                def _():
                    x_copy(d, s, e).wait_send()

            @pl.when(x_goes(d, s, e))
            def _():
                x_sum(d, s, e).wait_send()

    for s in range(2):
        @pl.when(inside(z + sign_of(s)))
        def _():
            e_copy(s).wait_send()
            e_sum(s).wait_send()

    @pl.loop(1, dp)
    def _(g):
        mass_copy(g).wait_send()

    @pl.loop(1, dp)
    def _(g):
        mass_wait(g).wait_recv()

    denom = 1.0 + lax.dot_general(
        mslots[...].reshape(dp * window, k), table[...], (((0,), (0,)), ((), ())),
        preferred_element_type=F32, precision=HIGHEST,
    )
    inv[...] = (1.0 / denom).reshape(inv.shape)
    sib_copy.wait_recv()

    def got_x(h):
        remote(xlast.at[0], finx.at[h], rx_s.at[slot(0, 0, 0)], fx_r.at[h], sibling).wait_recv()

    def got_z(s, h):
        remote(xlast.at[0], finz.at[s, h], rx_s.at[slot(0, 0, 0)], fz_r.at[s, h], sibling).wait_recv()

    for h in range(2):
        got_z(near, h)
        for i in range(mb):
            acc[h, i] += finz[near, h, i].astype(F32)
    for h in range(2):
        got_x(h)

    @pl.when(is_end(z))
    def _():
        for h in range(2):
            for i in range(mb):
                out_ref[i, h] = (acc[h, i] + finx[h, i].astype(F32)) * inv[h]

    @pl.when(jnp.logical_not(is_end(z)))
    def _():
        for h in range(2):
            got_z(1 - near, h)
            for i in range(mb):
                total = acc[h, i] + finx[h, i].astype(F32)
                out_ref[i, h] = (total + finz[1 - near, h, i].astype(F32)) * inv[h]

    @pl.loop(1, zn)
    def _(d):
        @pl.loop(0, 4)
        def _(j):
            e, s = j // 2, j % 2

            @pl.when(inside(z + sign_of(s) * d))
            def _():
                z_got(d, s, e).wait_send()

    for e in range(2):
        x_last(e).wait_send()


def finish_kernel(total_ref, ev_ref, out_ref, evidence_ref, sem):
    copy = pltpu.make_async_copy(total_ref, out_ref, sem)
    copy.start()
    evidence_ref[...] = ev_ref[...]
    copy.wait()


def shards(dp, particles, refs, ctf_group, defocus, class_prior, cycle_weight):
    n, m_all, q = particles.shape
    mb, k, _ = refs.shape
    zn = dp // 4
    nall = n * dp
    kh = k // 2
    n2 = 2 * n
    window = -(-((n2 * G) // nall + 3) // 8) * 8
    slots = 4 * zn
    weighted_chunks = m_all // 16

    vmem = pl.BlockSpec(memory_space=pltpu.VMEM)
    hbm = pl.BlockSpec(memory_space=pl.ANY)
    sem = pltpu.SemaphoreType.DMA
    total, ev = pl.pallas_call(
        functools.partial(step_kernel, zn, dp, window),
        out_shape=(
            jax.ShapeDtypeStruct((mb, 2, kh, q), F32),
            jax.ShapeDtypeStruct((1, n), F32),
        ),
        in_specs=[pl.BlockSpec(memory_space=pltpu.MemorySpace.HBM)] * 6,
        out_specs=(vmem, vmem),
        scratch_shapes=[
            pltpu.VMEM((2, kh, q), F32),
            pltpu.VMEM((1, n), jnp.int32), pltpu.VMEM((1, G), F32),
            pltpu.VMEM((1, R), F32), pltpu.VMEM((1, k), F32), sem((4,)),
            pltpu.VMEM((n, m_all, q), BF16),
            pltpu.VMEM((m_all, 2, 2, n, q), BF16),
            pltpu.VMEM((dp // 2, 2, mb, kh, q), BF16),
            pltpu.VMEM((ROT, kh, 2 * n2), F32),
            pltpu.VMEM((kh, q), F32),
            pltpu.VMEM((ROT, kh, n2), F32),
            pltpu.VMEM((kh, n2), F32),
            pltpu.VMEM((ROT, kh, 2 * n2), BF16),
            pltpu.VMEM((2, 8, n2), F32),
            pltpu.VMEM((dp * window, q), F32),
            pltpu.VMEM((8, n2), F32),
            pltpu.VMEM((8, n2), F32),
            pltpu.VMEM((window, k), F32),
            pltpu.VMEM((dp, window, k), F32),
            pltpu.VMEM((slots, mb, kh, q), BF16),
            pltpu.VMEM((slots, mb, kh, q), BF16),
            pltpu.VMEM((slots, mb, kh, q), BF16),
            pltpu.VMEM((slots, mb, kh, q), BF16),
            pltpu.VMEM((2, mb, kh, q), BF16),
            pltpu.VMEM((2, mb, kh, q), BF16),
            pltpu.VMEM((2, mb, kh, q), BF16),
            pltpu.VMEM((mb, kh, q), F32),
            pltpu.VMEM((2, mb, kh, q), F32),
            pltpu.VMEM((2, mb, kh, q), BF16),
            pltpu.VMEM((2, 2, mb, kh, q), BF16),
            sem, sem, sem, sem, sem((weighted_chunks,)), sem((weighted_chunks,)), sem, sem,
            sem((slots,)), sem((slots,)), sem((slots,)), sem((slots + 4,)), sem((2,)), sem((2,)),
            sem, sem, sem((dp,)), sem((dp,)),
            sem((slots,)), sem((slots,)), sem((slots,)), sem((slots,)), sem((2,)), sem((2,)),
            sem((2,)), sem((2, 2)), sem, sem,
        ],
        compiler_params=pltpu.CompilerParams(
            collective_id=0, has_side_effects=True, vmem_limit_bytes=40 << 20
        ),
        name="step",
    )(*(
        pltpu.with_memory_space_constraint(a, pltpu.MemorySpace.HBM) for a in (
            refs.reshape(mb, 2, kh, q), particles, ctf_group[None, :], defocus[None, :],
            cycle_weight[None, :], class_prior[None, :],
        )
    ))

    new_refs, evidence = pl.pallas_call(
        finish_kernel,
        out_shape=(
            jax.ShapeDtypeStruct((mb, 2, kh, q), F32),
            jax.ShapeDtypeStruct((1, n), F32),
        ),
        in_specs=[vmem] * 2,
        out_specs=(hbm, vmem),
        scratch_shapes=[sem],
        compiler_params=pltpu.CompilerParams(vmem_limit_bytes=8 << 20),
        name="finish",
    )(total, ev)
    return (new_refs.reshape(mb, k, q), evidence[0])


def solution(mesh):
    in_specs = (
        P(("groups", "dp"), None, None),
        P("dp", "groups", None),
        P(("groups", "dp")),
        P("groups"),
        P("groups"),
        P(),
    )
    out_specs = (P("dp", "groups", None), P(("groups", "dp")))
    return jax.shard_map(
        functools.partial(shards, mesh.shape["dp"]),
        mesh=mesh, in_specs=in_specs, out_specs=out_specs, check_vma=False,
    )
```

```python
import functools
import math

import jax
import jax.numpy as jnp
from jax import lax
from jax.experimental import pallas as pl
from jax.experimental.pallas import tpu as pltpu
from jax.sharding import PartitionSpec as P

R = 64
ROT = 36
HALF = ROT // 2
NC = HALF + 1
G = 32
MESH = pl.DeviceIdType.MESH
HIGHEST = lax.Precision.HIGHEST
F32 = jnp.float32
BF16 = jnp.bfloat16


def dev(index):
    return {"dp": index}


def cosine9(x, a):
    c1, c2, c4 = (jnp.float32(math.cos(2.0 * math.pi * p / 9)) for p in (1, 2, 4))
    a1, a2, a3, a4 = a
    both = a1 + a2 + a4
    near = x + a3
    base = x - a3 * jnp.float32(0.5)
    d1, d2 = a1 - a4, a2 - a4
    y1 = c1 * d1 + c2 * d2
    y2 = c2 * d1 + c4 * d2
    return [near + both, base + y1, base + y2, near - both * jnp.float32(0.5), base - (y1 + y2)]


def sine9(b):
    s1, s4 = (jnp.float32(math.sin(2.0 * math.pi * p / 9)) for p in (1, 4))
    half = jnp.float32(math.sqrt(3.0) / 2.0)
    b1, b2, b3, b4 = b
    e1, e2 = b1 + b2, b2 + b4
    e3 = b1 - b4
    t = half * b3
    z1 = s1 * e1 + s4 * e2
    z2 = s1 * e3 + s4 * e1
    return [z1 + t, z2 - t, half * (b1 - b2 + b4), (z2 - z1) + t]


def turns(real, imag):
    a = {r: real(r) + real(ROT - r) for r in range(1, ROT) if r % 9 in (1, 2, 3, 4)}
    b = {r: imag(r) - imag(ROT - r) for r in a}
    a9, b9 = real(9) + real(27), imag(9) - imag(27)
    first, last = real(0), real(18)
    up, down = first + last, first - last
    flat = [up + a9, down - b9, up - a9, down + b9]
    cos_in, sin_in = [[], [], [], []], [[], [], [], []]
    for p in range(1, 5):
        r = [(9 * i + 28 * p) % ROT for i in range(4)]
        re, im = [a[v] for v in r], [b[v] for v in r]
        re02, re13, im02, im13 = re[0] + re[2], re[1] + re[3], im[0] + im[2], im[1] + im[3]
        dr02, dr13, di02, di13 = re[0] - re[2], re[1] - re[3], im[0] - im[2], im[1] - im[3]
        for t, v in enumerate((re02 + re13, dr02 - di13, re02 - re13, dr02 + di13)):
            cos_in[t].append(v)
        for t, v in enumerate((im02 + im13, di02 + dr13, im02 - im13, di02 - dr13)):
            sin_in[t].append(v)
    out = {}
    for t in range(4):
        cosine, sine = cosine9(flat[t], cos_in[t]), sine9(sin_in[t])
        out[(9 * t) % ROT] = cosine[0]
        for g in range(1, 5):
            out[(9 * t + 4 * g) % ROT] = cosine[g] - sine[g - 1]
            out[(9 * t + 4 * (9 - g)) % ROT] = cosine[g] + sine[g - 1]
    return out


def harmonics(value):
    real, imag = [], []
    for t in range(4):
        v = [value((9 * t + 4 * g) % ROT) for g in range(9)]
        real.append(cosine9(v[0], [v[g] + v[9 - g] for g in range(1, 5)]))
        imag.append(sine9([v[g] - v[9 - g] for g in range(1, 5)]))
    re, im = {}, {}

    def put(r, x, y):
        if r <= HALF:
            re[r] = x
            if y is not None:
                im[r] = y
        else:
            re[ROT - r] = x
            if y is not None:
                im[ROT - r] = -y

    x = [real[t][0] for t in range(4)]
    put(0, (x[0] + x[2]) + (x[1] + x[3]), None)
    put(18, (x[0] + x[2]) - (x[1] + x[3]), None)
    put(9, x[0] - x[2], x[1] - x[3])
    for p in range(1, 5):
        x = [real[t][p] for t in range(4)]
        y = [imag[t][p - 1] for t in range(4)]
        sx, tx, sy, ty = x[0] + x[2], x[1] + x[3], y[0] + y[2], y[1] + y[3]
        dx, ex, dy, ey = x[0] - x[2], x[1] - x[3], y[0] - y[2], y[1] - y[3]
        put((28 * p) % ROT, sx + tx, sy + ty)
        put((9 + 28 * p) % ROT, dx - ey, dy + ex)
        put((18 + 28 * p) % ROT, sx - tx, sy - ty)
        put((27 + 28 * p) % ROT, dx + ey, dy - ex)
    return re, im


def step_kernel(zn, dp, window, *refs):
    (refs_ref, part_ref, row_hbm, focus_hbm, cw_hbm, prior_hbm,
     out_ref, ev_ref,
     inv, row_ref, focus_ref, cw_ref, prior_ref, small, part, both, held, cres, energy, sbuf, psum, pp, rows2, table,
     stat, stat_got, mass, mslots,
     xsend, xrecv, zsend, zrecv, xlast, esend, erecv, sib, acc, finx, finz,
     psem, keep, ksend, krecv, wsend, wrecv, rsend, rrecv,
     ax_s, ax_r, az_s, az_r, ae_s, ae_r, ssend, srecv, msend, mrecv,
     rx_s, rx_r, rz_s, rz_r, re_s, re_r, fx_r, fz_r, bsend, brecv) = refs
    me = lax.axis_index("dp")
    z, x, c = me // 4, (me // 2) % 2, me % 2
    o = 1 - c
    y = 1 - x
    n = part.shape[0]
    m_all, q = both.shape[0], both.shape[-1]
    mb, kh = held.shape[2], held.shape[3]
    k = 2 * kh
    n2 = 2 * n
    nall = n * dp
    end = zn - 1

    def at(zz, xx, cc):
        return zz * 4 + xx * 2 + cc

    def chip(zz, xx):
        return zz * 2 + xx

    def remote(src, dst, ss, rs, target):
        return pltpu.make_async_remote_copy(
            src_ref=src, dst_ref=dst, send_sem=ss, recv_sem=rs,
            device_id=dev(target), device_id_type=MESH,
        )

    def is_end(zz):
        return jnp.logical_or(zz == 0, zz == end)

    def inside(zz):
        return jnp.logical_and(zz >= 0, zz < zn)

    def sign_of(s):
        return 1 - 2 * s

    def slot(d, s, e):
        return (d * 2 + s) * 2 + e

    sibling = at(z, x, o)

    def each(low, high, body):
        if high - low <= 8:
            for value in range(low, high):
                body(value)
        else:
            pl.loop(low, high)(body)

    def fixed(d, value):
        return isinstance(d, int) and d == value

    barrier = pltpu.get_barrier_semaphore()

    def greet(target):
        pl.semaphore_signal(barrier, inc=1, device_id=dev(target), device_id_type=MESH)

    greet(sibling)
    greet(at(z, y, 0))
    greet(at(z, y, 1))
    for zz in (z - 1, z + 1):
        @pl.when(inside(zz))
        def _():
            greet(at(zz, x, 0))
            greet(at(zz, x, 1))

    smalls = [
        pltpu.make_async_copy(a, b, small.at[i])
        for i, (a, b) in enumerate((
            (row_hbm, row_ref), (focus_hbm, focus_ref), (cw_hbm, cw_ref), (prior_hbm, prior_ref)
        ))
    ]
    for copy in smalls:
        copy.start()
    load = pltpu.make_async_copy(part_ref, part, psem)
    load.start()
    mine = pltpu.make_async_copy(refs_ref.at[:, c], held.at[chip(z, x), c], keep)
    mine.start()

    pl.semaphore_wait(
        barrier, 3 + 2 * (z > 0).astype(jnp.int32) + 2 * (z < end).astype(jnp.int32)
    )

    here = chip(z, x)

    def first_z(s, e):
        cc = jnp.bitwise_xor(c, e)
        return remote(refs_ref.at[:, cc], held.at[here, c], az_s.at[slot(0, s, e)],
                      az_r.at[slot(1, s, e)], at(z + sign_of(s), x, cc))

    def first_x(e):
        cc = jnp.bitwise_xor(c, e)
        return remote(refs_ref.at[:, cc], held.at[here, c], ax_s.at[slot(0, 0, e)],
                      ax_r.at[slot(0, 0, e)], at(z, y, cc))

    for e in range(2):
        for s in range(2):
            @pl.when(inside(z + sign_of(s)))
            def _():
                first_z(s, e).start()
        first_x(1 - e).start()
    own_half = remote(refs_ref.at[:, o], held.at[here, c], ksend, krecv, sibling)
    own_half.start()

    for copy in smalls:
        copy.wait()
    lane = lax.broadcasted_iota(jnp.int32, (G, q), 1)
    radius = (jnp.where(lane < R, lane, lane - R).astype(F32) + 1.0) / R
    eye = lax.broadcasted_iota(jnp.int32, (G, G), 0) == lax.broadcasted_iota(jnp.int32, (G, G), 1)
    focus = jnp.sum(jnp.where(eye, jnp.broadcast_to(focus_ref[...], (G, G)), 0.0), axis=1, keepdims=True)
    phase = 20.0 * focus * (radius * radius)
    ctf = -(0.995 * jnp.sin(phase) + 0.1 * jnp.cos(phase))
    cw = jnp.concatenate([cw_ref[...], cw_ref[...]], axis=1)
    gain_table = cw * ctf
    power = gain_table * ctf

    onehot = (row_ref[...] == lax.broadcasted_iota(jnp.int32, (G, n), 0)).astype(F32)
    gain = lax.dot_general(
        onehot, gain_table, (((0,), (0,)), ((), ())),
        preferred_element_type=F32, precision=HIGHEST,
    )
    row = row_ref[...].astype(F32)
    rows2[c] = jnp.broadcast_to(jnp.concatenate([row, row], axis=1), rows2.shape[1:])
    rows_copy = remote(rows2.at[c], rows2.at[c], rsend, rrecv, sibling)
    rows_copy.start()

    load.wait()
    turn = jnp.where(lax.broadcasted_iota(jnp.int32, (1, 1, q), 2) < R, F32(1.0), F32(-1.0))
    chunk = 16

    def weighted_copy(i):
        span = pl.ds(pl.multiple_of(i * chunk, chunk), chunk)
        return remote(both.at[span, :, c], both.at[span, :, c], wsend.at[i], wrecv.at[i], sibling)

    @pl.loop(0, m_all // chunk)
    def _(i):
        span = pl.ds(pl.multiple_of(i * chunk, chunk), chunk)
        wide = part[:, span, :].astype(F32) * gain[:, None, :]
        w = jnp.swapaxes(wide, 0, 1).astype(BF16)
        both[span, 0, c] = w
        both[span, 1, c] = (pltpu.roll(w.astype(F32), R, 2) * turn).astype(BF16)
        weighted_copy(i).start()

    cres[...] = jnp.zeros_like(cres)
    energy[...] = jnp.zeros_like(energy)
    below = lax.broadcasted_iota(jnp.int32, (window, G), 0) - lax.broadcasted_iota(jnp.int32, (window, G), 1)
    for p in range(dp // 2):
        pick = (below == -((p * n2 * G) // nall)).astype(F32)
        span = jnp.dot(pick, power, precision=HIGHEST, preferred_element_type=F32)
        table[2 * p * window:(2 * p + 1) * window, :] = span
        table[(2 * p + 1) * window:(2 * p + 2) * window, :] = span

    def products(block, cc):
        total = None
        for i in range(mb):
            m = (block * 2 + cc) * mb + i
            r = lax.rem(m, ROT)
            images = both[m].reshape(2 * n2, q)
            ref = held[block, cc, i]
            cres[r] += lax.dot_general(
                ref, images, (((1,), (1,)), ((), ())), preferred_element_type=F32
            )
            wide = ref.astype(F32)
            total = wide * wide if total is None else total + wide * wide
        energy[...] += total

    def z_copy(d, s, e):
        piece = held.at[chip(z - sign_of(s) * d, x), jnp.bitwise_xor(c, e)]
        return remote(piece, piece, az_s.at[slot(d, s, e)], az_r.at[slot(d + 1, s, e)],
                      at(z + sign_of(s), x, c))

    def z_wait(d, s, e):
        piece = held.at[chip(z - sign_of(s) * d, x), jnp.bitwise_xor(c, e)]
        return remote(piece, piece, az_s.at[slot(d, s, e)], az_r.at[slot(d, s, e)], sibling)

    def x_copy(d, s, e):
        piece = held.at[chip(z - sign_of(s) * d, x), jnp.bitwise_xor(c, e)]
        return remote(piece, piece, ax_s.at[slot(d, s, e)], ax_r.at[slot(d, s, e)], at(z, y, c))

    def x_wait(d, s, e):
        piece = held.at[chip(z - sign_of(s) * d, y), jnp.bitwise_xor(c, e)]
        return remote(piece, piece, ax_s.at[slot(d, s, e)], ax_r.at[slot(d, s, e)], sibling)

    def e_piece(s):
        return held.at[chip(s * end, y), o]

    def e_copy(s):
        piece = e_piece(s)
        return remote(piece, piece, ae_s.at[s], ae_r.at[s], at(z + sign_of(s), x, c))

    def by_x(zo, e):
        return jnp.logical_not(jnp.logical_and(e == 1, is_end(zo)))

    def z_held(d, s):
        return jnp.logical_and(d < zn, inside(z - sign_of(s) * d))

    def x_held(d, s, e):
        far = jnp.logical_and(inside(z - sign_of(s) * d), by_x(z - sign_of(s) * d, e))
        if isinstance(d, int):
            return far
        return jnp.logical_or(jnp.logical_and(d > 0, far), jnp.logical_and(d == 0, s == 0))

    def z_forward(d, s, e):
        @pl.when(z_held(d, s))
        def _():
            z_wait(d, s, e).wait_recv()

            if not fixed(d, end):
                @pl.when(inside(z + sign_of(s)))
                def _():
                    z_copy(d, s, e).start()

            if not (fixed(d, end) and e == 1):
                @pl.when(by_x(z - sign_of(s) * d, e))
                def _():
                    x_copy(d, s, e).start()

    def x_take(d, s, e):
        x_wait(d - 1, s, e).wait_recv()
        for t in range(2):
            if e == 1 and (not isinstance(d, int) or d == 1):
                @pl.when(z == t * end if isinstance(d, int) else jnp.logical_and(d == 1, z == t * end))
                def _():
                    e_copy(t).start()

        products(chip(z - sign_of(s) * (d - 1), y), jnp.bitwise_xor(c, e))

    def e_take(d, s):
        gone = z if s == 0 else end - z

        @pl.when(jnp.logical_and(gone == d - 1, gone > 0))
        def _():
            e_copy(s).wait_recv()

            if not fixed(d, zn):
                @pl.when(gone < end)
                def _():
                    e_copy(s).start()

            products(chip(s * end, y), o)

    def opening():
        @pl.loop(0, m_all // chunk)
        def _(i):
            weighted_copy(i).wait_recv()

        own_half.wait_recv()

        @pl.loop(0, 2)
        def _(cc):
            products(here, cc)

    mine.wait()

    def gather_step(d):
        for e in range(2):
            if not fixed(d, zn):
                for s in range(2):
                    z_forward(d, s, e)

            if e == 0:
                if isinstance(d, int):
                    if d == 1:
                        opening()
                else:
                    pl.when(d == 1)(opening)

            if not fixed(d, zn):
                for s in range(2):
                    @pl.when(z_held(d, s))
                    def _():
                        products(chip(z - sign_of(s) * d, x), jnp.bitwise_xor(c, e))

            if e == 0 and not fixed(d, 1):
                for s in range(2):
                    e_take(d, s)

            if fixed(d, 1):
                x_take(d, 0, e)
            elif not (fixed(d, zn) and e == 1):
                for s in range(2):
                    @pl.when(x_held(d - 1, s, e))
                    def _():
                        x_take(d, s, e)

    def x_arrive(e):
        x_wait(0, 0, e).wait_recv()
        if e == 1:
            for t in range(2):
                @pl.when(z == t * end)
                def _():
                    e_copy(t).start()

    def z_products(d, e):
        for s in range(2):
            @pl.when(z_held(d, s))
            def _():
                products(chip(z - sign_of(s) * d, x), jnp.bitwise_xor(c, e))

    def e_taken(s, d):
        gone = z if s == 0 else end - z
        return jnp.logical_and(gone == d - 1, gone > 0)

    def gather_fixed(d):
        if d < zn:
            for s in range(2):
                z_forward(d, s, 0)
        if d == 1:
            x_arrive(1)
            opening()
        else:
            for s in range(2):
                @pl.when(e_taken(s, d))
                def _():
                    e_copy(s).wait_recv()
                    if d < zn:
                        e_copy(s).start()
        if d < zn:
            z_products(d, 0)
        if d > 1:
            for s in range(2):
                @pl.when(e_taken(s, d))
                def _():
                    products(chip(s * end, y), o)
        if d < zn:
            for s in range(2):
                z_forward(d, s, 1)
        if d == 1:
            x_arrive(0)
        for e in range(2):
            if e == 1 and d < zn:
                z_products(d, 1)
            if d == 1:
                products(chip(z, y), jnp.bitwise_xor(c, 1 - e))
            elif not (d == zn and e == 1):
                for s in range(2):
                    @pl.when(x_held(d - 1, s, e))
                    def _():
                        x_take(d, s, e)

    if zn <= 8:
        for d in range(1, zn + 1):
            gather_fixed(d)
    else:
        each(1, zn + 1, gather_step)

    rows_copy.wait_recv()
    group = jnp.concatenate([rows2[0, 0:1, :n], rows2[1, 0:1, :n]], axis=1)
    hot_g = (group == lax.broadcasted_iota(jnp.int32, (G, n2), 0).astype(F32)).astype(F32)
    quad = lax.dot_general(
        energy[...], power, (((1,), (1,)), ((), ())), preferred_element_type=F32, precision=HIGHEST,
    )
    norm = jnp.dot(quad, hot_g, precision=HIGHEST, preferred_element_type=F32)
    diag = lax.broadcasted_iota(jnp.int32, (kh, k), 0) + c * kh == lax.broadcasted_iota(jnp.int32, (kh, k), 1)
    prior = jnp.sum(jnp.where(diag, jnp.broadcast_to(prior_ref[...], (kh, k)), 0.0), axis=1, keepdims=True)
    psum[...] = jnp.log(prior) - 0.5 * norm

    rows = 8

    def score_rows(i, top):
        span = pl.ds(pl.multiple_of(i * rows, rows), rows)
        re, im = pl.ds(0, n2), pl.ds(n2, n2)
        corr = turns(lambda r: cres[r, span, re], lambda r: cres[r, span, im])
        best = None
        for j in range(ROT):
            sbuf[j, span, :] = corr[j]
            best = corr[j] if best is None else jnp.maximum(best, corr[j])
        return jnp.maximum(top, best + psum[span, :])

    top = lax.fori_loop(0, kh // rows, score_rows, jnp.full((rows, n2), -jnp.inf, F32))
    top = jnp.max(top, axis=0, keepdims=True)

    def exp_rows(i, total):
        span = pl.ds(pl.multiple_of(i * rows, rows), rows)
        part_sum = None
        shift = psum[span, :] - top
        for j in range(ROT):
            value = jnp.exp(sbuf[j, span, :] + shift)
            sbuf[j, span, :] = value
            part_sum = value if part_sum is None else part_sum + value
        psum[span, :] = part_sum
        return total + part_sum

    total = lax.fori_loop(0, kh // rows, exp_rows, jnp.zeros((rows, n2), F32))
    total = jnp.sum(total, axis=0, keepdims=True)
    which = lax.broadcasted_iota(jnp.int32, stat.shape, 0)
    stat[...] = jnp.where(which == 0, top, total)
    stat_copy = remote(stat, stat_got, ssend, srecv, sibling)
    stat_copy.start()

    @pl.loop(0, kh // rows)
    def _(i):
        span = pl.ds(pl.multiple_of(i * rows, rows), rows)
        real, imag = harmonics(lambda j: sbuf[j, span, :])
        for r in range(NC):
            sbuf[r, span, :] = real[r]
        for r in range(1, HALF):
            sbuf[HALF + r, span, :] = imag[r]

    stat_copy.wait_recv()
    other_top, other_total = stat_got[0:1, :], stat_got[1:2, :]
    most = jnp.maximum(top, other_top)
    shrink = jnp.exp(top - most)
    whole = total * shrink + other_total * jnp.exp(other_top - most)
    evidence = most + jnp.log(whole)
    ev_ref[...] = jnp.where(c == 0, evidence[:, :n], evidence[:, n:])
    scale = shrink / whole

    tile = 16

    @pl.loop(0, kh // tile)
    def _(i):
        span = pl.ds(pl.multiple_of(i * tile, tile), tile)
        for r in range(NC):
            re = (sbuf[r, span, :] * scale).astype(BF16)
            pp[r, span, 0:n2] = re
            if r in (0, HALF):
                pp[r, span, n2:] = jnp.zeros_like(re)
            else:
                im = (sbuf[HALF + r, span, :] * scale).astype(BF16)
                pp[r, span, n2:] = -im
                pp[ROT - r, span, 0:n2] = re
                pp[ROT - r, span, n2:] = im

    def numer(block, cc, i):
        m = (block * 2 + cc) * mb + i
        r = lax.rem(m, ROT)
        return jnp.dot(pp[r], both[m].reshape(2 * n2, q), preferred_element_type=F32)

    def e_sum(s):
        return remote(esend.at[s], erecv.at[s], re_s.at[s], re_r.at[s], at(z + sign_of(s), x, c))

    for s in range(2):
        @pl.when(z == s * end)
        def _():
            for i in range(mb):
                esend[s, i] = numer(chip(end - s * end, y), o, i).astype(BF16)
            e_sum(s).start()

    def x_sum(d, s, e):
        return remote(xsend.at[slot(d, s, e)], xrecv.at[slot(d, s, e)],
                      rx_s.at[slot(d, s, e)], rx_r.at[slot(d, s, e)], at(z, y, c))

    def x_last(e):
        return remote(xlast.at[e], finx.at[c], rx_s.at[slot(0, 0, e)], fx_r.at[c],
                      at(z, y, jnp.bitwise_xor(c, e)))

    def x_goes(d, s, e):
        zo = z + sign_of(s) * d
        return jnp.logical_and(inside(zo), by_x(zo, e))

    def x_step(t):
        d = end - t
        for e in (1, 0):
            for s in range(2):
                if fixed(d, end) and e == 1:
                    continue

                @pl.when(x_goes(d, s, e))
                def _():
                    for i in range(mb):
                        xsend[slot(d, s, e), i] = numer(
                            chip(z + sign_of(s) * d, y), jnp.bitwise_xor(c, e), i
                        ).astype(BF16)
                    x_sum(d, s, e).start()

    each(0, zn - 1, x_step)

    def send_last(e, extra):
        for i in range(mb):
            value = numer(chip(z, y), jnp.bitwise_xor(c, e), i)
            if extra is not None:
                value = value + erecv[extra, i].astype(F32)
            xlast[e, i] = value.astype(BF16)
        x_last(e).start()

    @pl.loop(0, 2)
    def _(e):
        @pl.when(by_x(z, e))
        def _():
            send_last(e, None)

    def z_sum(d, s, e):
        return remote(zsend.at[slot(d, s, e)], zrecv.at[slot(d - 1, s, e)],
                      rz_s.at[slot(d, s, e)], rz_r.at[slot(d - 1, s, e)], at(z + sign_of(s), x, c))

    def z_got(d, s, e):
        return remote(zsend.at[slot(d, s, e)], zrecv.at[slot(d, s, e)],
                      rz_s.at[slot(d, s, e)], rz_r.at[slot(d, s, e)], sibling)

    def z_last(s, e):
        return remote(zsend.at[slot(1, s, e)], finz.at[s, c], rz_s.at[slot(1, s, e)], fz_r.at[s, c],
                      at(z + sign_of(s), x, jnp.bitwise_xor(c, e)))

    near = (2 * z < zn).astype(jnp.int32)

    def e_pass(d):
        for s in range(2):
            left = (end - z) if s == 0 else z

            @pl.when(jnp.logical_and(left == d - 1, jnp.logical_and(left > 0, left < end)))
            def _():
                e_sum(s).wait_recv()
                for i in range(mb):
                    esend[s, i] = (numer(chip(end - s * end, y), o, i) + erecv[s, i].astype(F32)).astype(BF16)
                e_sum(s).start()

    def e_cross():
        for s in range(2):
            @pl.when(z == (1 - s) * end)
            def _():
                e_sum(s).wait_recv()
                send_last(1, s)

    def z_step(t, between=None):
        d = end - t

        def part(j):
            e = 1 - j // 2
            s = jnp.bitwise_xor(j % 2, near)
            zo = z + sign_of(s) * d

            @pl.when(inside(zo))
            def _():
                here_slot = slot(d, s, e)
                crossed = by_x(zo, e)
                line = inside(z - sign_of(s))
                for i in range(mb):
                    acc[c, i] = numer(chip(zo, x), jnp.bitwise_xor(c, e), i)

                @pl.when(crossed)
                def _():
                    x_sum(d, s, e).wait_recv()
                    for i in range(mb):
                        acc[c, i] += xrecv[here_slot, i].astype(F32)

                @pl.when(line)
                def _():
                    z_got(d, s, e).wait_recv()
                    for i in range(mb):
                        acc[c, i] += zrecv[here_slot, i].astype(F32)

                for i in range(mb):
                    zsend[here_slot, i] = acc[c, i].astype(BF16)

                if isinstance(d, int):
                    (z_sum(d, s, e) if d > 1 else z_last(s, e)).start()
                else:
                    @pl.when(d > 1)
                    def _():
                        z_sum(d, s, e).start()

                    @pl.when(d == 1)
                    def _():
                        z_last(s, e).start()

        for j in range(2):
            part(j)
        if between is not None:
            between()
        if isinstance(d, int):
            if d == 1:
                e_cross()
            else:
                e_pass(d)
        else:
            pl.when(d == 1)(e_cross)
            e_pass(d)
        for j in range(2, 4):
            part(j)

    def mass_copy(g):
        return remote(mass, mslots.at[me], msend.at[g], mrecv.at[g], lax.rem(me + g, dp))

    def mass_wait(g):
        return remote(mass, mslots.at[lax.rem(me + dp - g, dp)], msend.at[g], mrecv.at[g], sibling)

    sib_copy = remote(sib, acc.at[c], bsend, brecv, sibling)

    def side_work():
        start = (here * n2 * G) // nall
        hot = (
            group == (lax.broadcasted_iota(jnp.int32, (window, n2), 0) + start).astype(F32)
        ).astype(F32)
        part_mass = lax.dot_general(
            hot, psum[...] * scale, (((1,), (1,)), ((), ())), preferred_element_type=F32, precision=HIGHEST,
        )
        nothing = jnp.zeros_like(part_mass)
        mass[...] = jnp.where(
            c == 0, jnp.concatenate([part_mass, nothing], axis=1), jnp.concatenate([nothing, part_mass], axis=1)
        )
        mslots[me] = mass[...]

        @pl.loop(1, dp)
        def _(g):
            mass_copy(g).start()

        for i in range(mb):
            sib[i] = numer(here, o, i)
        sib_copy.start()

    z_step(0, side_work)
    each(1, zn - 1, z_step)

    for i in range(mb):
        acc[c, i] = numer(here, c, i)

    for e in range(2):
        for s in range(2):
            @pl.when(inside(z + sign_of(s)))
            def _():
                first_z(s, e).wait_send()
        first_x(e).wait_send()
    own_half.wait_send()
    rows_copy.wait_send()
    stat_copy.wait_send()
    sib_copy.wait_send()

    @pl.loop(0, m_all // chunk)
    def _(i):
        weighted_copy(i).wait_send()

    @pl.loop(1, zn)
    def _(d):
        @pl.loop(0, 4)
        def _(j):
            e, s = j // 2, j % 2
            zo = z - sign_of(s) * d

            @pl.when(z_held(d, s))
            def _():
                @pl.when(inside(z + sign_of(s)))
                def _():
                    z_copy(d, s, e).wait_send()

                @pl.when(by_x(zo, e))
                def _():
                    x_copy(d, s, e).wait_send()

            @pl.when(x_goes(d, s, e))
            def _():
                x_sum(d, s, e).wait_send()

    for s in range(2):
        @pl.when(inside(z + sign_of(s)))
        def _():
            e_copy(s).wait_send()
            e_sum(s).wait_send()

    @pl.loop(1, dp)
    def _(g):
        mass_copy(g).wait_send()

    @pl.loop(1, dp)
    def _(g):
        mass_wait(g).wait_recv()

    denom = 1.0 + lax.dot_general(
        mslots[...].reshape(dp * window, k), table[...], (((0,), (0,)), ((), ())),
        preferred_element_type=F32, precision=HIGHEST,
    )
    inv[...] = (1.0 / denom).reshape(inv.shape)
    sib_copy.wait_recv()

    def got_x(h):
        remote(xlast.at[0], finx.at[h], rx_s.at[slot(0, 0, 0)], fx_r.at[h], sibling).wait_recv()

    def got_z(s, h):
        remote(xlast.at[0], finz.at[s, h], rx_s.at[slot(0, 0, 0)], fz_r.at[s, h], sibling).wait_recv()

    for h in range(2):
        got_z(near, h)
        for i in range(mb):
            acc[h, i] += finz[near, h, i].astype(F32)
    for h in range(2):
        got_x(h)

    @pl.when(is_end(z))
    def _():
        for h in range(2):
            for i in range(mb):
                out_ref[i, h] = (acc[h, i] + finx[h, i].astype(F32)) * inv[h]

    @pl.when(jnp.logical_not(is_end(z)))
    def _():
        for h in range(2):
            got_z(1 - near, h)
            for i in range(mb):
                total = acc[h, i] + finx[h, i].astype(F32)
                out_ref[i, h] = (total + finz[1 - near, h, i].astype(F32)) * inv[h]

    def sums_sent(d):
        for s in range(2):
            @pl.when(inside(z + sign_of(s) * d))
            def _():
                for e in range(2):
                    z_got(d, s, e).wait_send()

    each(1, zn, sums_sent)

    for e in range(2):
        x_last(e).wait_send()


def finish_kernel(total_ref, ev_ref, out_ref, evidence_ref, sems):
    copies = [
        pltpu.make_async_copy(total_ref.at[i], out_ref.at[i], sems.at[i])
        for i in range(total_ref.shape[0])
    ]
    for copy in copies:
        copy.start()
    evidence_ref[...] = ev_ref[...]
    for copy in copies:
        copy.wait()


def shards(dp, particles, refs, ctf_group, defocus, class_prior, cycle_weight):
    n, m_all, q = particles.shape
    mb, k, _ = refs.shape
    zn = dp // 4
    nall = n * dp
    kh = k // 2
    n2 = 2 * n
    window = -(-((n2 * G) // nall + 3) // 8) * 8
    slots = 4 * zn
    weighted_chunks = m_all // 16

    vmem = pl.BlockSpec(memory_space=pltpu.VMEM)
    hbm = pl.BlockSpec(memory_space=pl.ANY)
    sem = pltpu.SemaphoreType.DMA
    total, ev = pl.pallas_call(
        functools.partial(step_kernel, zn, dp, window),
        out_shape=(
            jax.ShapeDtypeStruct((mb, 2, kh, q), F32),
            jax.ShapeDtypeStruct((1, n), F32),
        ),
        in_specs=[pl.BlockSpec(memory_space=pltpu.MemorySpace.HBM)] * 6,
        out_specs=(vmem, vmem),
        scratch_shapes=[
            pltpu.VMEM((2, kh, q), F32),
            pltpu.VMEM((1, n), jnp.int32), pltpu.VMEM((1, G), F32),
            pltpu.VMEM((1, R), F32), pltpu.VMEM((1, k), F32), sem((4,)),
            pltpu.VMEM((n, m_all, q), BF16),
            pltpu.VMEM((m_all, 2, 2, n, q), BF16),
            pltpu.VMEM((dp // 2, 2, mb, kh, q), BF16),
            pltpu.VMEM((ROT, kh, 2 * n2), F32),
            pltpu.VMEM((kh, q), F32),
            pltpu.VMEM((ROT, kh, n2), F32),
            pltpu.VMEM((kh, n2), F32),
            pltpu.VMEM((ROT, kh, 2 * n2), BF16),
            pltpu.VMEM((2, 8, n2), F32),
            pltpu.VMEM((dp * window, q), F32),
            pltpu.VMEM((8, n2), F32),
            pltpu.VMEM((8, n2), F32),
            pltpu.VMEM((window, k), F32),
            pltpu.VMEM((dp, window, k), F32),
            pltpu.VMEM((slots, mb, kh, q), BF16),
            pltpu.VMEM((slots, mb, kh, q), BF16),
            pltpu.VMEM((slots, mb, kh, q), BF16),
            pltpu.VMEM((slots, mb, kh, q), BF16),
            pltpu.VMEM((2, mb, kh, q), BF16),
            pltpu.VMEM((2, mb, kh, q), BF16),
            pltpu.VMEM((2, mb, kh, q), BF16),
            pltpu.VMEM((mb, kh, q), F32),
            pltpu.VMEM((2, mb, kh, q), F32),
            pltpu.VMEM((2, mb, kh, q), BF16),
            pltpu.VMEM((2, 2, mb, kh, q), BF16),
            sem, sem, sem, sem, sem((weighted_chunks,)), sem((weighted_chunks,)), sem, sem,
            sem((slots,)), sem((slots,)), sem((slots,)), sem((slots + 4,)), sem((2,)), sem((2,)),
            sem, sem, sem((dp,)), sem((dp,)),
            sem((slots,)), sem((slots,)), sem((slots,)), sem((slots,)), sem((2,)), sem((2,)),
            sem((2,)), sem((2, 2)), sem, sem,
        ],
        compiler_params=pltpu.CompilerParams(
            collective_id=0, has_side_effects=True, vmem_limit_bytes=40 << 20
        ),
        name="step",
    )(*(
        pltpu.with_memory_space_constraint(a, pltpu.MemorySpace.HBM) for a in (
            refs.reshape(mb, 2, kh, q), particles, ctf_group[None, :], defocus[None, :],
            cycle_weight[None, :], class_prior[None, :],
        )
    ))

    new_refs, evidence = pl.pallas_call(
        finish_kernel,
        out_shape=(
            jax.ShapeDtypeStruct((mb, 2, kh, q), F32),
            jax.ShapeDtypeStruct((1, n), F32),
        ),
        in_specs=[vmem] * 2,
        out_specs=(hbm, vmem),
        scratch_shapes=[sem((mb,))],
        compiler_params=pltpu.CompilerParams(vmem_limit_bytes=8 << 20),
        name="finish",
    )(total, ev)
    return (new_refs.reshape(mb, k, q), evidence[0])


def solution(mesh):
    in_specs = (
        P(("groups", "dp"), None, None),
        P("dp", "groups", None),
        P(("groups", "dp")),
        P("groups"),
        P("groups"),
        P(),
    )
    out_specs = (P("dp", "groups", None), P(("groups", "dp")))
    return jax.shard_map(
        functools.partial(shards, mesh.shape["dp"]),
        mesh=mesh, in_specs=in_specs, out_specs=out_specs, check_vma=False,
    )
```

```python
import functools
import math

import jax
import jax.numpy as jnp
from jax import lax
from jax.experimental import pallas as pl
from jax.experimental.pallas import tpu as pltpu
from jax.sharding import PartitionSpec as P

R = 64
ROT = 36
HALF = ROT // 2
NC = HALF + 1
G = 32
MESH = pl.DeviceIdType.MESH
HIGHEST = lax.Precision.HIGHEST
F32 = jnp.float32
BF16 = jnp.bfloat16


def dev(index):
    return {"dp": index}


def cosine9(x, a):
    c1, c2, c4 = (jnp.float32(math.cos(2.0 * math.pi * p / 9)) for p in (1, 2, 4))
    a1, a2, a3, a4 = a
    both = a1 + a2 + a4
    near = x + a3
    base = x - a3 * jnp.float32(0.5)
    d1, d2 = a1 - a4, a2 - a4
    y1 = c1 * d1 + c2 * d2
    y2 = c2 * d1 + c4 * d2
    return [near + both, base + y1, base + y2, near - both * jnp.float32(0.5), base - (y1 + y2)]


def sine9(b):
    s1, s4 = (jnp.float32(math.sin(2.0 * math.pi * p / 9)) for p in (1, 4))
    half = jnp.float32(math.sqrt(3.0) / 2.0)
    b1, b2, b3, b4 = b
    e1, e2 = b1 + b2, b2 + b4
    e3 = b1 - b4
    t = half * b3
    z1 = s1 * e1 + s4 * e2
    z2 = s1 * e3 + s4 * e1
    return [z1 + t, z2 - t, half * (b1 - b2 + b4), (z2 - z1) + t]


def turns(real, imag):
    a = {r: real(r) + real(ROT - r) for r in range(1, ROT) if r % 9 in (1, 2, 3, 4)}
    b = {r: imag(r) - imag(ROT - r) for r in a}
    a9, b9 = real(9) + real(27), imag(9) - imag(27)
    first, last = real(0), real(18)
    up, down = first + last, first - last
    flat = [up + a9, down - b9, up - a9, down + b9]
    cos_in, sin_in = [[], [], [], []], [[], [], [], []]
    for p in range(1, 5):
        r = [(9 * i + 28 * p) % ROT for i in range(4)]
        re, im = [a[v] for v in r], [b[v] for v in r]
        re02, re13, im02, im13 = re[0] + re[2], re[1] + re[3], im[0] + im[2], im[1] + im[3]
        dr02, dr13, di02, di13 = re[0] - re[2], re[1] - re[3], im[0] - im[2], im[1] - im[3]
        for t, v in enumerate((re02 + re13, dr02 - di13, re02 - re13, dr02 + di13)):
            cos_in[t].append(v)
        for t, v in enumerate((im02 + im13, di02 + dr13, im02 - im13, di02 - dr13)):
            sin_in[t].append(v)
    out = {}
    for t in range(4):
        cosine, sine = cosine9(flat[t], cos_in[t]), sine9(sin_in[t])
        out[(9 * t) % ROT] = cosine[0]
        for g in range(1, 5):
            out[(9 * t + 4 * g) % ROT] = cosine[g] - sine[g - 1]
            out[(9 * t + 4 * (9 - g)) % ROT] = cosine[g] + sine[g - 1]
    return out


def harmonics(value):
    real, imag = [], []
    for t in range(4):
        v = [value((9 * t + 4 * g) % ROT) for g in range(9)]
        real.append(cosine9(v[0], [v[g] + v[9 - g] for g in range(1, 5)]))
        imag.append(sine9([v[g] - v[9 - g] for g in range(1, 5)]))
    re, im = {}, {}

    def put(r, x, y):
        if r <= HALF:
            re[r] = x
            if y is not None:
                im[r] = y
        else:
            re[ROT - r] = x
            if y is not None:
                im[ROT - r] = -y

    x = [real[t][0] for t in range(4)]
    put(0, (x[0] + x[2]) + (x[1] + x[3]), None)
    put(18, (x[0] + x[2]) - (x[1] + x[3]), None)
    put(9, x[0] - x[2], x[1] - x[3])
    for p in range(1, 5):
        x = [real[t][p] for t in range(4)]
        y = [imag[t][p - 1] for t in range(4)]
        sx, tx, sy, ty = x[0] + x[2], x[1] + x[3], y[0] + y[2], y[1] + y[3]
        dx, ex, dy, ey = x[0] - x[2], x[1] - x[3], y[0] - y[2], y[1] - y[3]
        put((28 * p) % ROT, sx + tx, sy + ty)
        put((9 + 28 * p) % ROT, dx - ey, dy + ex)
        put((18 + 28 * p) % ROT, sx - tx, sy - ty)
        put((27 + 28 * p) % ROT, dx + ey, dy - ex)
    return re, im


def step_kernel(zn, dp, window, *refs):
    (refs_ref, part_ref, row_hbm, focus_hbm, cw_hbm, prior_hbm,
     out_ref, ev_ref,
     inv, row_ref, focus_ref, cw_ref, prior_ref, small, part, both, held, cres, energy, sbuf, psum, pp, rows2, table,
     stat, stat_got, halves, mass, mslots,
     xsend, xrecv, zsend, zrecv, xlast, esend, erecv, sib, acc, finx, finz,
     psem, keep, ksend, krecv, wsend, wrecv, rsend, rrecv,
     ax_s, ax_r, az_s, az_r, ae_s, ae_r, ssend, srecv, msend, mrecv,
     rx_s, rx_r, rz_s, rz_r, re_s, re_r, fx_r, fz_r, bsend, brecv) = refs
    me = lax.axis_index("dp")
    z, x, c = me // 4, (me // 2) % 2, me % 2
    o = 1 - c
    y = 1 - x
    n = part.shape[0]
    m_all, q = both.shape[0], both.shape[-1]
    mb, kh = held.shape[2], held.shape[3]
    k = 2 * kh
    n2 = 2 * n
    nall = n * dp
    end = zn - 1

    def at(zz, xx, cc):
        return zz * 4 + xx * 2 + cc

    def chip(zz, xx):
        return zz * 2 + xx

    def remote(src, dst, ss, rs, target):
        return pltpu.make_async_remote_copy(
            src_ref=src, dst_ref=dst, send_sem=ss, recv_sem=rs,
            device_id=dev(target), device_id_type=MESH,
        )

    def is_end(zz):
        return jnp.logical_or(zz == 0, zz == end)

    def inside(zz):
        return jnp.logical_and(zz >= 0, zz < zn)

    def sign_of(s):
        return 1 - 2 * s

    def slot(d, s, e):
        return (d * 2 + s) * 2 + e

    sibling = at(z, x, o)

    def each(low, high, body):
        if high - low <= 8:
            for value in range(low, high):
                body(value)
        else:
            pl.loop(low, high)(body)

    def fixed(d, value):
        return isinstance(d, int) and d == value

    barrier = pltpu.get_barrier_semaphore()

    def greet(target):
        pl.semaphore_signal(barrier, inc=1, device_id=dev(target), device_id_type=MESH)

    greet(sibling)
    greet(at(z, y, 0))
    greet(at(z, y, 1))
    for zz in (z - 1, z + 1):
        @pl.when(inside(zz))
        def _():
            greet(at(zz, x, 0))
            greet(at(zz, x, 1))

    smalls = [
        pltpu.make_async_copy(a, b, small.at[i])
        for i, (a, b) in enumerate((
            (row_hbm, row_ref), (focus_hbm, focus_ref), (cw_hbm, cw_ref), (prior_hbm, prior_ref)
        ))
    ]
    for copy in smalls:
        copy.start()
    load = pltpu.make_async_copy(part_ref, part, psem)
    load.start()
    mine = pltpu.make_async_copy(refs_ref.at[:, c], held.at[chip(z, x), c], keep)
    mine.start()

    pl.semaphore_wait(
        barrier, 3 + 2 * (z > 0).astype(jnp.int32) + 2 * (z < end).astype(jnp.int32)
    )

    here = chip(z, x)

    def first_z(s, e):
        cc = jnp.bitwise_xor(c, e)
        return remote(refs_ref.at[:, cc], held.at[here, c], az_s.at[slot(0, s, e)],
                      az_r.at[slot(1, s, e)], at(z + sign_of(s), x, cc))

    def first_x(e):
        cc = jnp.bitwise_xor(c, e)
        return remote(refs_ref.at[:, cc], held.at[here, c], ax_s.at[slot(0, 0, e)],
                      ax_r.at[slot(0, 0, e)], at(z, y, cc))

    for e in range(2):
        for s in range(2):
            @pl.when(inside(z + sign_of(s)))
            def _():
                first_z(s, e).start()
        first_x(1 - e).start()
    own_half = remote(refs_ref.at[:, o], held.at[here, c], ksend, krecv, sibling)
    own_half.start()

    for copy in smalls:
        copy.wait()
    lane = lax.broadcasted_iota(jnp.int32, (G, q), 1)
    radius = (jnp.where(lane < R, lane, lane - R).astype(F32) + 1.0) / R
    eye = lax.broadcasted_iota(jnp.int32, (G, G), 0) == lax.broadcasted_iota(jnp.int32, (G, G), 1)
    focus = jnp.sum(jnp.where(eye, jnp.broadcast_to(focus_ref[...], (G, G)), 0.0), axis=1, keepdims=True)
    phase = 20.0 * focus * (radius * radius)
    ctf = -(0.995 * jnp.sin(phase) + 0.1 * jnp.cos(phase))
    cw = jnp.concatenate([cw_ref[...], cw_ref[...]], axis=1)
    gain_table = cw * ctf
    power = gain_table * ctf

    onehot = (row_ref[...] == lax.broadcasted_iota(jnp.int32, (G, n), 0)).astype(F32)
    gain = lax.dot_general(
        onehot, gain_table, (((0,), (0,)), ((), ())),
        preferred_element_type=F32, precision=HIGHEST,
    )
    row = row_ref[...].astype(F32)
    rows2[c] = jnp.broadcast_to(jnp.concatenate([row, row], axis=1), rows2.shape[1:])
    rows_copy = remote(rows2.at[c], rows2.at[c], rsend, rrecv, sibling)
    rows_copy.start()

    load.wait()
    turn = jnp.where(lax.broadcasted_iota(jnp.int32, (1, 1, q), 2) < R, F32(1.0), F32(-1.0))
    chunk = 16

    def weighted_copy(i):
        span = pl.ds(pl.multiple_of(i * chunk, chunk), chunk)
        return remote(both.at[span, :, c], both.at[span, :, c], wsend.at[i], wrecv.at[i], sibling)

    @pl.loop(0, m_all // chunk)
    def _(i):
        span = pl.ds(pl.multiple_of(i * chunk, chunk), chunk)
        wide = part[:, span, :].astype(F32) * gain[:, None, :]
        w = jnp.swapaxes(wide, 0, 1).astype(BF16)
        both[span, 0, c] = w
        both[span, 1, c] = (pltpu.roll(w.astype(F32), R, 2) * turn).astype(BF16)
        weighted_copy(i).start()

    cres[...] = jnp.zeros_like(cres)
    energy[...] = jnp.zeros_like(energy)
    below = lax.broadcasted_iota(jnp.int32, (window, G), 0) - lax.broadcasted_iota(jnp.int32, (window, G), 1)
    for p in range(dp // 2):
        pick = (below == -((p * n2 * G) // nall)).astype(F32)
        span = jnp.dot(pick, power, precision=HIGHEST, preferred_element_type=F32)
        table[p * window:(p + 1) * window, :] = span

    def products(block, cc):
        total = None
        for i in range(mb):
            m = (block * 2 + cc) * mb + i
            r = lax.rem(m, ROT)
            images = both[m].reshape(2 * n2, q)
            ref = held[block, cc, i]
            cres[r] += lax.dot_general(
                ref, images, (((1,), (1,)), ((), ())), preferred_element_type=F32
            )
            wide = ref.astype(F32)
            total = wide * wide if total is None else total + wide * wide
        energy[...] += total

    def z_copy(d, s, e):
        piece = held.at[chip(z - sign_of(s) * d, x), jnp.bitwise_xor(c, e)]
        return remote(piece, piece, az_s.at[slot(d, s, e)], az_r.at[slot(d + 1, s, e)],
                      at(z + sign_of(s), x, c))

    def z_wait(d, s, e):
        piece = held.at[chip(z - sign_of(s) * d, x), jnp.bitwise_xor(c, e)]
        return remote(piece, piece, az_s.at[slot(d, s, e)], az_r.at[slot(d, s, e)], sibling)

    def x_copy(d, s, e):
        piece = held.at[chip(z - sign_of(s) * d, x), jnp.bitwise_xor(c, e)]
        return remote(piece, piece, ax_s.at[slot(d, s, e)], ax_r.at[slot(d, s, e)], at(z, y, c))

    def x_wait(d, s, e):
        piece = held.at[chip(z - sign_of(s) * d, y), jnp.bitwise_xor(c, e)]
        return remote(piece, piece, ax_s.at[slot(d, s, e)], ax_r.at[slot(d, s, e)], sibling)

    def e_piece(s):
        return held.at[chip(s * end, y), o]

    def e_copy(s):
        piece = e_piece(s)
        return remote(piece, piece, ae_s.at[s], ae_r.at[s], at(z + sign_of(s), x, c))

    def by_x(zo, e):
        return jnp.logical_not(jnp.logical_and(e == 1, is_end(zo)))

    def z_held(d, s):
        return jnp.logical_and(d < zn, inside(z - sign_of(s) * d))

    def x_held(d, s, e):
        far = jnp.logical_and(inside(z - sign_of(s) * d), by_x(z - sign_of(s) * d, e))
        if isinstance(d, int):
            return far
        return jnp.logical_or(jnp.logical_and(d > 0, far), jnp.logical_and(d == 0, s == 0))

    def z_forward(d, s, e):
        @pl.when(z_held(d, s))
        def _():
            z_wait(d, s, e).wait_recv()

            if not fixed(d, end):
                @pl.when(inside(z + sign_of(s)))
                def _():
                    z_copy(d, s, e).start()

            if not (fixed(d, end) and e == 1):
                @pl.when(by_x(z - sign_of(s) * d, e))
                def _():
                    x_copy(d, s, e).start()

    def x_take(d, s, e):
        x_wait(d - 1, s, e).wait_recv()
        for t in range(2):
            if e == 1 and (not isinstance(d, int) or d == 1):
                @pl.when(z == t * end if isinstance(d, int) else jnp.logical_and(d == 1, z == t * end))
                def _():
                    e_copy(t).start()

        products(chip(z - sign_of(s) * (d - 1), y), jnp.bitwise_xor(c, e))

    def e_take(d, s):
        gone = z if s == 0 else end - z

        @pl.when(jnp.logical_and(gone == d - 1, gone > 0))
        def _():
            e_copy(s).wait_recv()

            if not fixed(d, zn):
                @pl.when(gone < end)
                def _():
                    e_copy(s).start()

            products(chip(s * end, y), o)

    def opening():
        @pl.loop(0, m_all // chunk)
        def _(i):
            weighted_copy(i).wait_recv()

        own_half.wait_recv()

        @pl.loop(0, 2)
        def _(cc):
            products(here, cc)

    mine.wait()

    def gather_step(d):
        for e in range(2):
            if not fixed(d, zn):
                for s in range(2):
                    z_forward(d, s, e)

            if e == 0:
                if isinstance(d, int):
                    if d == 1:
                        opening()
                else:
                    pl.when(d == 1)(opening)

            if not fixed(d, zn):
                for s in range(2):
                    @pl.when(z_held(d, s))
                    def _():
                        products(chip(z - sign_of(s) * d, x), jnp.bitwise_xor(c, e))

            if e == 0 and not fixed(d, 1):
                for s in range(2):
                    e_take(d, s)

            if fixed(d, 1):
                x_take(d, 0, e)
            elif not (fixed(d, zn) and e == 1):
                for s in range(2):
                    @pl.when(x_held(d - 1, s, e))
                    def _():
                        x_take(d, s, e)

    def x_arrive(e):
        x_wait(0, 0, e).wait_recv()
        if e == 1:
            for t in range(2):
                @pl.when(z == t * end)
                def _():
                    e_copy(t).start()

    def z_products(d, e):
        for s in range(2):
            @pl.when(z_held(d, s))
            def _():
                products(chip(z - sign_of(s) * d, x), jnp.bitwise_xor(c, e))

    def e_taken(s, d):
        gone = z if s == 0 else end - z
        return jnp.logical_and(gone == d - 1, gone > 0)

    def gather_fixed(d):
        if d < zn:
            for s in range(2):
                z_forward(d, s, 0)
        if d == 1:
            x_arrive(1)
            opening()
        else:
            for s in range(2):
                @pl.when(e_taken(s, d))
                def _():
                    e_copy(s).wait_recv()
                    if d < zn:
                        e_copy(s).start()
        if d < zn:
            z_products(d, 0)
        if d > 1:
            for s in range(2):
                @pl.when(e_taken(s, d))
                def _():
                    products(chip(s * end, y), o)
        if d < zn:
            for s in range(2):
                z_forward(d, s, 1)
        if d == 1:
            x_arrive(0)
        for e in range(2):
            if e == 1 and d < zn:
                z_products(d, 1)
            if d == 1:
                products(chip(z, y), jnp.bitwise_xor(c, 1 - e))
            elif not (d == zn and e == 1):
                for s in range(2):
                    @pl.when(x_held(d - 1, s, e))
                    def _():
                        x_take(d, s, e)

    if zn <= 8:
        for d in range(1, zn + 1):
            gather_fixed(d)
    else:
        each(1, zn + 1, gather_step)

    rows_copy.wait_recv()
    group = jnp.concatenate([rows2[0, 0:1, :n], rows2[1, 0:1, :n]], axis=1)
    hot_g = (group == lax.broadcasted_iota(jnp.int32, (G, n2), 0).astype(F32)).astype(F32)
    quad = lax.dot_general(
        energy[...], power, (((1,), (1,)), ((), ())), preferred_element_type=F32, precision=HIGHEST,
    )
    norm = jnp.dot(quad, hot_g, precision=HIGHEST, preferred_element_type=F32)
    diag = lax.broadcasted_iota(jnp.int32, (kh, k), 0) + c * kh == lax.broadcasted_iota(jnp.int32, (kh, k), 1)
    prior = jnp.sum(jnp.where(diag, jnp.broadcast_to(prior_ref[...], (kh, k)), 0.0), axis=1, keepdims=True)
    psum[...] = jnp.log(prior) - 0.5 * norm

    rows = 8

    def score_rows(i, top):
        span = pl.ds(pl.multiple_of(i * rows, rows), rows)
        re, im = pl.ds(0, n2), pl.ds(n2, n2)
        corr = turns(lambda r: cres[r, span, re], lambda r: cres[r, span, im])
        best = None
        for j in range(ROT):
            sbuf[j, span, :] = corr[j]
            best = corr[j] if best is None else jnp.maximum(best, corr[j])
        return jnp.maximum(top, best + psum[span, :])

    top = lax.fori_loop(0, kh // rows, score_rows, jnp.full((rows, n2), -jnp.inf, F32))
    top = jnp.max(top, axis=0, keepdims=True)

    def exp_rows(i, total):
        span = pl.ds(pl.multiple_of(i * rows, rows), rows)
        part_sum = None
        shift = psum[span, :] - top
        for j in range(ROT):
            value = jnp.exp(sbuf[j, span, :] + shift)
            sbuf[j, span, :] = value
            part_sum = value if part_sum is None else part_sum + value
        psum[span, :] = part_sum
        return total + part_sum

    total = lax.fori_loop(0, kh // rows, exp_rows, jnp.zeros((rows, n2), F32))
    total = jnp.sum(total, axis=0, keepdims=True)
    which = lax.broadcasted_iota(jnp.int32, stat.shape, 0)
    stat[...] = jnp.where(which == 0, top, total)
    stat_copy = remote(stat, stat_got, ssend, srecv, sibling)
    stat_copy.start()

    @pl.loop(0, kh // rows)
    def _(i):
        span = pl.ds(pl.multiple_of(i * rows, rows), rows)
        real, imag = harmonics(lambda j: sbuf[j, span, :])
        for r in range(NC):
            sbuf[r, span, :] = real[r]
        for r in range(1, HALF):
            sbuf[HALF + r, span, :] = imag[r]

    stat_copy.wait_recv()
    other_top, other_total = stat_got[0:1, :], stat_got[1:2, :]
    most = jnp.maximum(top, other_top)
    shrink = jnp.exp(top - most)
    whole = total * shrink + other_total * jnp.exp(other_top - most)
    evidence = most + jnp.log(whole)
    ev_ref[...] = jnp.where(c == 0, evidence[:, :n], evidence[:, n:])
    scale = shrink / whole

    tile = 16

    @pl.loop(0, kh // tile)
    def _(i):
        span = pl.ds(pl.multiple_of(i * tile, tile), tile)
        for r in range(NC):
            re = (sbuf[r, span, :] * scale).astype(BF16)
            pp[r, span, 0:n2] = re
            if r in (0, HALF):
                pp[r, span, n2:] = jnp.zeros_like(re)
            else:
                im = (sbuf[HALF + r, span, :] * scale).astype(BF16)
                pp[r, span, n2:] = -im
                pp[ROT - r, span, 0:n2] = re
                pp[ROT - r, span, n2:] = im

    def numer(block, cc, i):
        m = (block * 2 + cc) * mb + i
        r = lax.rem(m, ROT)
        return jnp.dot(pp[r], both[m].reshape(2 * n2, q), preferred_element_type=F32)

    def e_sum(s):
        return remote(esend.at[s], erecv.at[s], re_s.at[s], re_r.at[s], at(z + sign_of(s), x, c))

    def x_sum(d, s, e):
        return remote(xsend.at[slot(d, s, e)], xrecv.at[slot(d, s, e)],
                      rx_s.at[slot(d, s, e)], rx_r.at[slot(d, s, e)], at(z, y, c))

    def x_last(e):
        return remote(xlast.at[e], finx.at[c], rx_s.at[slot(0, 0, e)], fx_r.at[c],
                      at(z, y, jnp.bitwise_xor(c, e)))

    def x_goes(d, s, e):
        zo = z + sign_of(s) * d
        return jnp.logical_and(inside(zo), by_x(zo, e))

    def x_step(t):
        d = end - t
        for e in (1, 0):
            for s in range(2):
                if fixed(d, end) and e == 1:
                    continue

                @pl.when(x_goes(d, s, e))
                def _():
                    for i in range(mb):
                        xsend[slot(d, s, e), i] = numer(
                            chip(z + sign_of(s) * d, y), jnp.bitwise_xor(c, e), i
                        ).astype(BF16)
                    x_sum(d, s, e).start()

    x_step(0)
    for s in range(2):
        @pl.when(z == s * end)
        def _():
            for i in range(mb):
                esend[s, i] = numer(chip(end - s * end, y), o, i).astype(BF16)
            e_sum(s).start()

    each(1, zn - 1, x_step)

    def send_last(e, extra):
        for i in range(mb):
            value = numer(chip(z, y), jnp.bitwise_xor(c, e), i)
            if extra is not None:
                value = value + erecv[extra, i].astype(F32)
            xlast[e, i] = value.astype(BF16)
        x_last(e).start()

    @pl.loop(0, 2)
    def _(e):
        @pl.when(by_x(z, e))
        def _():
            send_last(e, None)

    def z_sum(d, s, e):
        return remote(zsend.at[slot(d, s, e)], zrecv.at[slot(d - 1, s, e)],
                      rz_s.at[slot(d, s, e)], rz_r.at[slot(d - 1, s, e)], at(z + sign_of(s), x, c))

    def z_got(d, s, e):
        return remote(zsend.at[slot(d, s, e)], zrecv.at[slot(d, s, e)],
                      rz_s.at[slot(d, s, e)], rz_r.at[slot(d, s, e)], sibling)

    def z_last(s, e):
        return remote(zsend.at[slot(1, s, e)], finz.at[s, c], rz_s.at[slot(1, s, e)], fz_r.at[s, c],
                      at(z + sign_of(s), x, jnp.bitwise_xor(c, e)))

    near = (2 * z < zn).astype(jnp.int32)

    def e_pass(d):
        for s in range(2):
            left = (end - z) if s == 0 else z

            @pl.when(jnp.logical_and(left == d - 1, jnp.logical_and(left > 0, left < end)))
            def _():
                e_sum(s).wait_recv()
                for i in range(mb):
                    esend[s, i] = (numer(chip(end - s * end, y), o, i) + erecv[s, i].astype(F32)).astype(BF16)
                e_sum(s).start()

    def e_cross():
        for s in range(2):
            @pl.when(z == (1 - s) * end)
            def _():
                e_sum(s).wait_recv()
                send_last(1, s)

    def z_step(t, between=None):
        d = end - t

        def part(j):
            e = 1 - j // 2
            s = jnp.bitwise_xor(j % 2, near)
            zo = z + sign_of(s) * d

            @pl.when(inside(zo))
            def _():
                here_slot = slot(d, s, e)
                crossed = by_x(zo, e)
                line = inside(z - sign_of(s))
                for i in range(mb):
                    acc[c, i] = numer(chip(zo, x), jnp.bitwise_xor(c, e), i)

                @pl.when(crossed)
                def _():
                    x_sum(d, s, e).wait_recv()
                    for i in range(mb):
                        acc[c, i] += xrecv[here_slot, i].astype(F32)

                @pl.when(line)
                def _():
                    z_got(d, s, e).wait_recv()
                    for i in range(mb):
                        zsend[here_slot, i] = (acc[c, i] + zrecv[here_slot, i].astype(F32)).astype(BF16)

                @pl.when(jnp.logical_not(line))
                def _():
                    for i in range(mb):
                        zsend[here_slot, i] = acc[c, i].astype(BF16)

                if isinstance(d, int):
                    (z_sum(d, s, e) if d > 1 else z_last(s, e)).start()
                else:
                    @pl.when(d > 1)
                    def _():
                        z_sum(d, s, e).start()

                    @pl.when(d == 1)
                    def _():
                        z_last(s, e).start()

        for j in range(2):
            part(j)
        if between is not None:
            between()
        if isinstance(d, int):
            if d == 1:
                e_cross()
            else:
                e_pass(d)
        else:
            pl.when(d == 1)(e_cross)
            e_pass(d)
        for j in range(2, 4):
            part(j)

    chips = dp // 2

    def mass_copy(g):
        return remote(mass, mslots.at[here], msend.at[g], mrecv.at[g], lax.rem(here + g, chips) * 2 + c)

    def mass_wait(g):
        return remote(mass, mslots.at[lax.rem(here + chips - g, chips)], msend.at[g], mrecv.at[g], sibling)

    halves_copy = remote(halves.at[c], halves.at[c], msend.at[0], mrecv.at[0], sibling)
    sib_copy = remote(sib, acc.at[c], bsend, brecv, sibling)

    def side_work():
        start = (here * n2 * G) // nall
        hot = (
            group == (lax.broadcasted_iota(jnp.int32, (window, n2), 0) + start).astype(F32)
        ).astype(F32)
        part_mass = lax.dot_general(
            hot, psum[...] * scale, (((1,), (1,)), ((), ())), preferred_element_type=F32, precision=HIGHEST,
        )
        nothing = jnp.zeros_like(part_mass)
        halves[c] = jnp.where(
            c == 0, jnp.concatenate([part_mass, nothing], axis=1), jnp.concatenate([nothing, part_mass], axis=1)
        )
        halves_copy.start()
        for i in range(mb):
            sib[i] = numer(here, o, i)
        sib_copy.start()
        halves_copy.wait_recv()
        both_mass = halves[0] + halves[1]
        mass[...] = both_mass
        mslots[here] = both_mass

        @pl.loop(1, dp // 2)
        def _(g):
            mass_copy(g).start()

    z_step(0, side_work)
    each(1, zn - 1, z_step)

    for i in range(mb):
        acc[c, i] = numer(here, c, i)

    for e in range(2):
        for s in range(2):
            @pl.when(inside(z + sign_of(s)))
            def _():
                first_z(s, e).wait_send()
        first_x(e).wait_send()
    own_half.wait_send()
    rows_copy.wait_send()
    stat_copy.wait_send()
    sib_copy.wait_send()

    @pl.loop(0, m_all // chunk)
    def _(i):
        weighted_copy(i).wait_send()

    @pl.loop(1, zn)
    def _(d):
        @pl.loop(0, 4)
        def _(j):
            e, s = j // 2, j % 2
            zo = z - sign_of(s) * d

            @pl.when(z_held(d, s))
            def _():
                @pl.when(inside(z + sign_of(s)))
                def _():
                    z_copy(d, s, e).wait_send()

                @pl.when(by_x(zo, e))
                def _():
                    x_copy(d, s, e).wait_send()

            @pl.when(x_goes(d, s, e))
            def _():
                x_sum(d, s, e).wait_send()

    for s in range(2):
        @pl.when(inside(z + sign_of(s)))
        def _():
            e_copy(s).wait_send()
            e_sum(s).wait_send()

    halves_copy.wait_send()

    @pl.loop(1, dp // 2)
    def _(g):
        mass_copy(g).wait_send()

    @pl.loop(1, dp // 2)
    def _(g):
        mass_wait(g).wait_recv()

    denom = 1.0 + lax.dot_general(
        mslots[...].reshape(dp // 2 * window, k), table[...], (((0,), (0,)), ((), ())),
        preferred_element_type=F32, precision=HIGHEST,
    )
    inv[...] = (1.0 / denom).reshape(inv.shape)
    sib_copy.wait_recv()

    def got_x(h):
        remote(xlast.at[0], finx.at[h], rx_s.at[slot(0, 0, 0)], fx_r.at[h], sibling).wait_recv()

    def got_z(s, h):
        remote(xlast.at[0], finz.at[s, h], rx_s.at[slot(0, 0, 0)], fz_r.at[s, h], sibling).wait_recv()

    for h in range(2):
        got_z(near, h)
        for i in range(mb):
            acc[h, i] += finz[near, h, i].astype(F32)
    for h in range(2):
        got_x(h)

    @pl.when(is_end(z))
    def _():
        for h in range(2):
            for i in range(mb):
                out_ref[i, h] = (acc[h, i] + finx[h, i].astype(F32)) * inv[h]

    @pl.when(jnp.logical_not(is_end(z)))
    def _():
        for h in range(2):
            got_z(1 - near, h)
            for i in range(mb):
                total = acc[h, i] + finx[h, i].astype(F32)
                out_ref[i, h] = (total + finz[1 - near, h, i].astype(F32)) * inv[h]

    def sums_sent(d):
        for s in range(2):
            @pl.when(inside(z + sign_of(s) * d))
            def _():
                for e in range(2):
                    z_got(d, s, e).wait_send()

    each(1, zn, sums_sent)

    for e in range(2):
        x_last(e).wait_send()


def finish_kernel(total_ref, ev_ref, out_ref, evidence_ref, sem):
    copy = pltpu.make_async_copy(total_ref, out_ref, sem)
    copy.start()
    evidence_ref[...] = ev_ref[...]
    copy.wait()


def shards(dp, particles, refs, ctf_group, defocus, class_prior, cycle_weight):
    n, m_all, q = particles.shape
    mb, k, _ = refs.shape
    zn = dp // 4
    nall = n * dp
    kh = k // 2
    n2 = 2 * n
    window = -(-((n2 * G) // nall + 3) // 8) * 8
    slots = 4 * zn
    weighted_chunks = m_all // 16

    vmem = pl.BlockSpec(memory_space=pltpu.VMEM)
    hbm = pl.BlockSpec(memory_space=pl.ANY)
    sem = pltpu.SemaphoreType.DMA
    total, ev = pl.pallas_call(
        functools.partial(step_kernel, zn, dp, window),
        out_shape=(
            jax.ShapeDtypeStruct((mb, 2, kh, q), F32),
            jax.ShapeDtypeStruct((1, n), F32),
        ),
        in_specs=[pl.BlockSpec(memory_space=pltpu.MemorySpace.HBM)] * 6,
        out_specs=(vmem, vmem),
        scratch_shapes=[
            pltpu.VMEM((2, kh, q), F32),
            pltpu.VMEM((1, n), jnp.int32), pltpu.VMEM((1, G), F32),
            pltpu.VMEM((1, R), F32), pltpu.VMEM((1, k), F32), sem((4,)),
            pltpu.VMEM((n, m_all, q), BF16),
            pltpu.VMEM((m_all, 2, 2, n, q), BF16),
            pltpu.VMEM((dp // 2, 2, mb, kh, q), BF16),
            pltpu.VMEM((ROT, kh, 2 * n2), F32),
            pltpu.VMEM((kh, q), F32),
            pltpu.VMEM((ROT, kh, n2), F32),
            pltpu.VMEM((kh, n2), F32),
            pltpu.VMEM((ROT, kh, 2 * n2), BF16),
            pltpu.VMEM((2, 8, n2), F32),
            pltpu.VMEM((dp // 2 * window, q), F32),
            pltpu.VMEM((8, n2), F32),
            pltpu.VMEM((8, n2), F32),
            pltpu.VMEM((2, window, k), F32),
            pltpu.VMEM((window, k), F32),
            pltpu.VMEM((dp // 2, window, k), F32),
            pltpu.VMEM((slots, mb, kh, q), BF16),
            pltpu.VMEM((slots, mb, kh, q), BF16),
            pltpu.VMEM((slots, mb, kh, q), BF16),
            pltpu.VMEM((slots, mb, kh, q), BF16),
            pltpu.VMEM((2, mb, kh, q), BF16),
            pltpu.VMEM((2, mb, kh, q), BF16),
            pltpu.VMEM((2, mb, kh, q), BF16),
            pltpu.VMEM((mb, kh, q), F32),
            pltpu.VMEM((2, mb, kh, q), F32),
            pltpu.VMEM((2, mb, kh, q), BF16),
            pltpu.VMEM((2, 2, mb, kh, q), BF16),
            sem, sem, sem, sem, sem((weighted_chunks,)), sem((weighted_chunks,)), sem, sem,
            sem((slots,)), sem((slots,)), sem((slots,)), sem((slots + 4,)), sem((2,)), sem((2,)),
            sem, sem, sem((dp // 2,)), sem((dp // 2,)),
            sem((slots,)), sem((slots,)), sem((slots,)), sem((slots,)), sem((2,)), sem((2,)),
            sem((2,)), sem((2, 2)), sem, sem,
        ],
        compiler_params=pltpu.CompilerParams(
            collective_id=0, has_side_effects=True, vmem_limit_bytes=40 << 20
        ),
        name="step",
    )(*(
        pltpu.with_memory_space_constraint(a, pltpu.MemorySpace.HBM) for a in (
            refs.reshape(mb, 2, kh, q), particles, ctf_group[None, :], defocus[None, :],
            cycle_weight[None, :], class_prior[None, :],
        )
    ))

    new_refs, evidence = pl.pallas_call(
        finish_kernel,
        out_shape=(
            jax.ShapeDtypeStruct((mb, 2, kh, q), F32),
            jax.ShapeDtypeStruct((1, n), F32),
        ),
        in_specs=[vmem] * 2,
        out_specs=(hbm, vmem),
        scratch_shapes=[sem],
        compiler_params=pltpu.CompilerParams(vmem_limit_bytes=8 << 20),
        name="finish",
    )(total, ev)
    return (new_refs.reshape(mb, k, q), evidence[0])


def solution(mesh):
    in_specs = (
        P(("groups", "dp"), None, None),
        P("dp", "groups", None),
        P(("groups", "dp")),
        P("groups"),
        P("groups"),
        P(),
    )
    out_specs = (P("dp", "groups", None), P(("groups", "dp")))
    return jax.shard_map(
        functools.partial(shards, mesh.shape["dp"]),
        mesh=mesh, in_specs=in_specs, out_specs=out_specs, check_vma=False,
    )
```

```python
import functools
import math

import jax
import jax.numpy as jnp
from jax import lax
from jax.experimental import pallas as pl
from jax.experimental.pallas import tpu as pltpu
from jax.sharding import PartitionSpec as P

R = 64
ROT = 36
HALF = ROT // 2
NC = HALF + 1
G = 32
MESH = pl.DeviceIdType.MESH
HIGHEST = lax.Precision.HIGHEST
F32 = jnp.float32
BF16 = jnp.bfloat16


def dev(index):
    return {"dp": index}


def cosine9(x, a):
    c1, c2, c4 = (jnp.float32(math.cos(2.0 * math.pi * p / 9)) for p in (1, 2, 4))
    a1, a2, a3, a4 = a
    both = a1 + a2 + a4
    near = x + a3
    base = x - a3 * jnp.float32(0.5)
    d1, d2 = a1 - a4, a2 - a4
    y1 = c1 * d1 + c2 * d2
    y2 = c2 * d1 + c4 * d2
    return [near + both, base + y1, base + y2, near - both * jnp.float32(0.5), base - (y1 + y2)]


def sine9(b):
    s1, s4 = (jnp.float32(math.sin(2.0 * math.pi * p / 9)) for p in (1, 4))
    half = jnp.float32(math.sqrt(3.0) / 2.0)
    b1, b2, b3, b4 = b
    e1, e2 = b1 + b2, b2 + b4
    e3 = b1 - b4
    t = half * b3
    z1 = s1 * e1 + s4 * e2
    z2 = s1 * e3 + s4 * e1
    return [z1 + t, z2 - t, half * (b1 - b2 + b4), (z2 - z1) + t]


def turns(real, imag):
    a = {r: real(r) + real(ROT - r) for r in range(1, ROT) if r % 9 in (1, 2, 3, 4)}
    b = {r: imag(r) - imag(ROT - r) for r in a}
    a9, b9 = real(9) + real(27), imag(9) - imag(27)
    first, last = real(0), real(18)
    up, down = first + last, first - last
    flat = [up + a9, down - b9, up - a9, down + b9]
    cos_in, sin_in = [[], [], [], []], [[], [], [], []]
    for p in range(1, 5):
        r = [(9 * i + 28 * p) % ROT for i in range(4)]
        re, im = [a[v] for v in r], [b[v] for v in r]
        re02, re13, im02, im13 = re[0] + re[2], re[1] + re[3], im[0] + im[2], im[1] + im[3]
        dr02, dr13, di02, di13 = re[0] - re[2], re[1] - re[3], im[0] - im[2], im[1] - im[3]
        for t, v in enumerate((re02 + re13, dr02 - di13, re02 - re13, dr02 + di13)):
            cos_in[t].append(v)
        for t, v in enumerate((im02 + im13, di02 + dr13, im02 - im13, di02 - dr13)):
            sin_in[t].append(v)
    out = {}
    for t in range(4):
        cosine, sine = cosine9(flat[t], cos_in[t]), sine9(sin_in[t])
        out[(9 * t) % ROT] = cosine[0]
        for g in range(1, 5):
            out[(9 * t + 4 * g) % ROT] = cosine[g] - sine[g - 1]
            out[(9 * t + 4 * (9 - g)) % ROT] = cosine[g] + sine[g - 1]
    return out


def harmonics(value):
    real, imag = [], []
    for t in range(4):
        v = [value((9 * t + 4 * g) % ROT) for g in range(9)]
        real.append(cosine9(v[0], [v[g] + v[9 - g] for g in range(1, 5)]))
        imag.append(sine9([v[g] - v[9 - g] for g in range(1, 5)]))
    re, im = {}, {}

    def put(r, x, y):
        if r <= HALF:
            re[r] = x
            if y is not None:
                im[r] = y
        else:
            re[ROT - r] = x
            if y is not None:
                im[ROT - r] = -y

    x = [real[t][0] for t in range(4)]
    put(0, (x[0] + x[2]) + (x[1] + x[3]), None)
    put(18, (x[0] + x[2]) - (x[1] + x[3]), None)
    put(9, x[0] - x[2], x[1] - x[3])
    for p in range(1, 5):
        x = [real[t][p] for t in range(4)]
        y = [imag[t][p - 1] for t in range(4)]
        sx, tx, sy, ty = x[0] + x[2], x[1] + x[3], y[0] + y[2], y[1] + y[3]
        dx, ex, dy, ey = x[0] - x[2], x[1] - x[3], y[0] - y[2], y[1] - y[3]
        put((28 * p) % ROT, sx + tx, sy + ty)
        put((9 + 28 * p) % ROT, dx - ey, dy + ex)
        put((18 + 28 * p) % ROT, sx - tx, sy - ty)
        put((27 + 28 * p) % ROT, dx + ey, dy - ex)
    return re, im


def step_kernel(zn, dp, window, *refs):
    (refs_ref, part_ref, row_hbm, focus_hbm, cw_hbm, prior_hbm,
     out_ref, ev_ref,
     inv, row_ref, focus_ref, cw_ref, prior_ref, small, part, both, held, cres, energy, sbuf, psum, pp, rows2, table,
     stat, stat_got, halves, mass, mslots,
     xsend, xrecv, zsend, zrecv, xlast, esend, erecv, sib, acc, finx, finz,
     psem, keep, ksend, krecv, wsend, wrecv, rsend, rrecv,
     ax_s, ax_r, az_s, az_r, ae_s, ae_r, ssend, srecv, msend, mrecv,
     rx_s, rx_r, rz_s, rz_r, re_s, re_r, fx_r, fz_r, bsend, brecv) = refs
    me = lax.axis_index("dp")
    z, x, c = me // 4, (me // 2) % 2, me % 2
    o = 1 - c
    y = 1 - x
    n = part.shape[0]
    m_all, q = both.shape[0], both.shape[-1]
    mb, kh = held.shape[2], held.shape[3]
    k = 2 * kh
    n2 = 2 * n
    nall = n * dp
    end = zn - 1

    def at(zz, xx, cc):
        return zz * 4 + xx * 2 + cc

    def chip(zz, xx):
        return zz * 2 + xx

    def remote(src, dst, ss, rs, target):
        return pltpu.make_async_remote_copy(
            src_ref=src, dst_ref=dst, send_sem=ss, recv_sem=rs,
            device_id=dev(target), device_id_type=MESH,
        )

    def is_end(zz):
        return jnp.logical_or(zz == 0, zz == end)

    def inside(zz):
        return jnp.logical_and(zz >= 0, zz < zn)

    def sign_of(s):
        return 1 - 2 * s

    def slot(d, s, e):
        return (d * 2 + s) * 2 + e

    sibling = at(z, x, o)

    def each(low, high, body):
        if high - low <= 8:
            for value in range(low, high):
                body(value)
        else:
            pl.loop(low, high)(body)

    def fixed(d, value):
        return isinstance(d, int) and d == value

    barrier = pltpu.get_barrier_semaphore()

    def greet(target):
        pl.semaphore_signal(barrier, inc=1, device_id=dev(target), device_id_type=MESH)

    greet(sibling)
    greet(at(z, y, 0))
    greet(at(z, y, 1))
    for zz in (z - 1, z + 1):
        @pl.when(inside(zz))
        def _():
            greet(at(zz, x, 0))
            greet(at(zz, x, 1))

    smalls = [
        pltpu.make_async_copy(a, b, small.at[i])
        for i, (a, b) in enumerate((
            (row_hbm, row_ref), (focus_hbm, focus_ref), (cw_hbm, cw_ref), (prior_hbm, prior_ref)
        ))
    ]
    for copy in smalls:
        copy.start()
    load = pltpu.make_async_copy(part_ref, part, psem)
    load.start()
    mine = pltpu.make_async_copy(refs_ref.at[:, c], held.at[chip(z, x), c], keep)
    mine.start()

    pl.semaphore_wait(
        barrier, 3 + 2 * (z > 0).astype(jnp.int32) + 2 * (z < end).astype(jnp.int32)
    )

    here = chip(z, x)

    def first_z(s, e):
        cc = jnp.bitwise_xor(c, e)
        return remote(refs_ref.at[:, cc], held.at[here, c], az_s.at[slot(0, s, e)],
                      az_r.at[slot(1, s, e)], at(z + sign_of(s), x, cc))

    def first_x(e):
        cc = jnp.bitwise_xor(c, e)
        return remote(refs_ref.at[:, cc], held.at[here, c], ax_s.at[slot(0, 0, e)],
                      ax_r.at[slot(0, 0, e)], at(z, y, cc))

    for e in range(2):
        for s in range(2):
            @pl.when(inside(z + sign_of(s)))
            def _():
                first_z(s, e).start()
        first_x(1 - e).start()
    own_half = remote(refs_ref.at[:, o], held.at[here, c], ksend, krecv, sibling)
    own_half.start()

    for copy in smalls:
        copy.wait()
    lane = lax.broadcasted_iota(jnp.int32, (G, q), 1)
    radius = (jnp.where(lane < R, lane, lane - R).astype(F32) + 1.0) / R
    eye = lax.broadcasted_iota(jnp.int32, (G, G), 0) == lax.broadcasted_iota(jnp.int32, (G, G), 1)
    focus = jnp.sum(jnp.where(eye, jnp.broadcast_to(focus_ref[...], (G, G)), 0.0), axis=1, keepdims=True)
    phase = 20.0 * focus * (radius * radius)
    ctf = -(0.995 * jnp.sin(phase) + 0.1 * jnp.cos(phase))
    cw = jnp.concatenate([cw_ref[...], cw_ref[...]], axis=1)
    gain_table = cw * ctf
    power = gain_table * ctf

    onehot = (row_ref[...] == lax.broadcasted_iota(jnp.int32, (G, n), 0)).astype(F32)
    gain = lax.dot_general(
        onehot, gain_table, (((0,), (0,)), ((), ())),
        preferred_element_type=F32, precision=HIGHEST,
    )
    row = row_ref[...].astype(F32)
    rows2[c] = jnp.broadcast_to(jnp.concatenate([row, row], axis=1), rows2.shape[1:])
    rows_copy = remote(rows2.at[c], rows2.at[c], rsend, rrecv, sibling)
    rows_copy.start()

    load.wait()
    turn = jnp.where(lax.broadcasted_iota(jnp.int32, (1, 1, q), 2) < R, F32(1.0), F32(-1.0))
    chunk = 16

    def weighted_copy(i):
        span = pl.ds(pl.multiple_of(i * chunk, chunk), chunk)
        return remote(both.at[span, :, c], both.at[span, :, c], wsend.at[i], wrecv.at[i], sibling)

    @pl.loop(0, m_all // chunk)
    def _(i):
        span = pl.ds(pl.multiple_of(i * chunk, chunk), chunk)
        wide = part[:, span, :].astype(F32) * gain[:, None, :]
        w = jnp.swapaxes(wide, 0, 1).astype(BF16)
        both[span, 0, c] = w
        both[span, 1, c] = (pltpu.roll(w.astype(F32), R, 2) * turn).astype(BF16)
        weighted_copy(i).start()

    cres[...] = jnp.zeros_like(cres)
    energy[...] = jnp.zeros_like(energy)
    below = lax.broadcasted_iota(jnp.int32, (window, G), 0) - lax.broadcasted_iota(jnp.int32, (window, G), 1)
    for p in range(dp // 2):
        pick = (below == -((p * n2 * G) // nall)).astype(F32)
        span = jnp.dot(pick, power, precision=HIGHEST, preferred_element_type=F32)
        table[p * window:(p + 1) * window, :] = span

    def products(block, cc):
        total = None
        for i in range(mb):
            m = (block * 2 + cc) * mb + i
            r = lax.rem(m, ROT)
            images = both[m].reshape(2 * n2, q)
            ref = held[block, cc, i]
            cres[r] += lax.dot_general(
                ref, images, (((1,), (1,)), ((), ())), preferred_element_type=F32
            )
            wide = ref.astype(F32)
            total = wide * wide if total is None else total + wide * wide
        energy[...] += total

    def z_copy(d, s, e):
        piece = held.at[chip(z - sign_of(s) * d, x), jnp.bitwise_xor(c, e)]
        return remote(piece, piece, az_s.at[slot(d, s, e)], az_r.at[slot(d + 1, s, e)],
                      at(z + sign_of(s), x, c))

    def z_wait(d, s, e):
        piece = held.at[chip(z - sign_of(s) * d, x), jnp.bitwise_xor(c, e)]
        return remote(piece, piece, az_s.at[slot(d, s, e)], az_r.at[slot(d, s, e)], sibling)

    def x_copy(d, s, e):
        piece = held.at[chip(z - sign_of(s) * d, x), jnp.bitwise_xor(c, e)]
        return remote(piece, piece, ax_s.at[slot(d, s, e)], ax_r.at[slot(d, s, e)], at(z, y, c))

    def x_wait(d, s, e):
        piece = held.at[chip(z - sign_of(s) * d, y), jnp.bitwise_xor(c, e)]
        return remote(piece, piece, ax_s.at[slot(d, s, e)], ax_r.at[slot(d, s, e)], sibling)

    def e_piece(s):
        return held.at[chip(s * end, y), o]

    def e_copy(s):
        piece = e_piece(s)
        return remote(piece, piece, ae_s.at[s], ae_r.at[s], at(z + sign_of(s), x, c))

    def by_x(zo, e):
        return jnp.logical_not(jnp.logical_and(e == 1, is_end(zo)))

    def z_held(d, s):
        return jnp.logical_and(d < zn, inside(z - sign_of(s) * d))

    def x_held(d, s, e):
        far = jnp.logical_and(inside(z - sign_of(s) * d), by_x(z - sign_of(s) * d, e))
        if isinstance(d, int):
            return far
        return jnp.logical_or(jnp.logical_and(d > 0, far), jnp.logical_and(d == 0, s == 0))

    def z_forward(d, s, e):
        @pl.when(z_held(d, s))
        def _():
            z_wait(d, s, e).wait_recv()

            if not fixed(d, end):
                @pl.when(inside(z + sign_of(s)))
                def _():
                    z_copy(d, s, e).start()

            if not (fixed(d, end) and e == 1):
                @pl.when(by_x(z - sign_of(s) * d, e))
                def _():
                    x_copy(d, s, e).start()

    def x_take(d, s, e):
        x_wait(d - 1, s, e).wait_recv()
        for t in range(2):
            if e == 1 and (not isinstance(d, int) or d == 1):
                @pl.when(z == t * end if isinstance(d, int) else jnp.logical_and(d == 1, z == t * end))
                def _():
                    e_copy(t).start()

        products(chip(z - sign_of(s) * (d - 1), y), jnp.bitwise_xor(c, e))

    def e_take(d, s):
        gone = z if s == 0 else end - z

        @pl.when(jnp.logical_and(gone == d - 1, gone > 0))
        def _():
            e_copy(s).wait_recv()

            if not fixed(d, zn):
                @pl.when(gone < end)
                def _():
                    e_copy(s).start()

            products(chip(s * end, y), o)

    def opening():
        @pl.loop(0, m_all // chunk)
        def _(i):
            weighted_copy(i).wait_recv()

        own_half.wait_recv()

        @pl.loop(0, 2)
        def _(cc):
            products(here, cc)

    mine.wait()

    def gather_step(d):
        for e in range(2):
            if not fixed(d, zn):
                for s in range(2):
                    z_forward(d, s, e)

            if e == 0:
                if isinstance(d, int):
                    if d == 1:
                        opening()
                else:
                    pl.when(d == 1)(opening)

            if not fixed(d, zn):
                for s in range(2):
                    @pl.when(z_held(d, s))
                    def _():
                        products(chip(z - sign_of(s) * d, x), jnp.bitwise_xor(c, e))

            if e == 0 and not fixed(d, 1):
                for s in range(2):
                    e_take(d, s)

            if fixed(d, 1):
                x_take(d, 0, e)
            elif not (fixed(d, zn) and e == 1):
                for s in range(2):
                    @pl.when(x_held(d - 1, s, e))
                    def _():
                        x_take(d, s, e)

    def x_arrive(e):
        x_wait(0, 0, e).wait_recv()
        if e == 1:
            for t in range(2):
                @pl.when(z == t * end)
                def _():
                    e_copy(t).start()

    def z_products(d, e):
        for s in range(2):
            @pl.when(z_held(d, s))
            def _():
                products(chip(z - sign_of(s) * d, x), jnp.bitwise_xor(c, e))

    def e_taken(s, d):
        gone = z if s == 0 else end - z
        return jnp.logical_and(gone == d - 1, gone > 0)

    def gather_fixed(d):
        if d < zn:
            for s in range(2):
                z_forward(d, s, 0)
        if d == 1:
            x_arrive(1)
            opening()
        else:
            for s in range(2):
                @pl.when(e_taken(s, d))
                def _():
                    e_copy(s).wait_recv()
                    if d < zn:
                        e_copy(s).start()
        if d < zn:
            z_products(d, 0)
        if d > 1:
            for s in range(2):
                @pl.when(e_taken(s, d))
                def _():
                    products(chip(s * end, y), o)
        if d < zn:
            for s in range(2):
                z_forward(d, s, 1)
        if d == 1:
            x_arrive(0)
        for e in range(2):
            if e == 1 and d < zn:
                z_products(d, 1)
            if d == 1:
                products(chip(z, y), jnp.bitwise_xor(c, 1 - e))
            elif not (d == zn and e == 1):
                for s in range(2):
                    @pl.when(x_held(d - 1, s, e))
                    def _():
                        x_take(d, s, e)

    if zn <= 8:
        for d in range(1, zn + 1):
            gather_fixed(d)
    else:
        each(1, zn + 1, gather_step)

    rows_copy.wait_recv()
    group = jnp.concatenate([rows2[0, 0:1, :n], rows2[1, 0:1, :n]], axis=1)
    hot_g = (group == lax.broadcasted_iota(jnp.int32, (G, n2), 0).astype(F32)).astype(F32)
    quad = lax.dot_general(
        energy[...], power, (((1,), (1,)), ((), ())), preferred_element_type=F32, precision=HIGHEST,
    )
    norm = jnp.dot(quad, hot_g, precision=HIGHEST, preferred_element_type=F32)
    diag = lax.broadcasted_iota(jnp.int32, (kh, k), 0) + c * kh == lax.broadcasted_iota(jnp.int32, (kh, k), 1)
    prior = jnp.sum(jnp.where(diag, jnp.broadcast_to(prior_ref[...], (kh, k)), 0.0), axis=1, keepdims=True)
    psum[...] = jnp.log(prior) - 0.5 * norm

    rows = 16

    def score_rows(i, top):
        span = pl.ds(pl.multiple_of(i * rows, rows), rows)
        re, im = pl.ds(0, n2), pl.ds(n2, n2)
        corr = turns(lambda r: cres[r, span, re], lambda r: cres[r, span, im])
        best = None
        for j in range(ROT):
            sbuf[j, span, :] = corr[j]
            best = corr[j] if best is None else jnp.maximum(best, corr[j])
        return jnp.maximum(top, best + psum[span, :])

    top = lax.fori_loop(0, kh // rows, score_rows, jnp.full((rows, n2), -jnp.inf, F32))
    top = jnp.max(top, axis=0, keepdims=True)

    def exp_rows(i, total):
        span = pl.ds(pl.multiple_of(i * rows, rows), rows)
        part_sum = None
        shift = psum[span, :] - top
        for j in range(ROT):
            value = jnp.exp(sbuf[j, span, :] + shift)
            sbuf[j, span, :] = value
            part_sum = value if part_sum is None else part_sum + value
        psum[span, :] = part_sum
        return total + part_sum

    total = lax.fori_loop(0, kh // rows, exp_rows, jnp.zeros((rows, n2), F32))
    total = jnp.sum(total, axis=0, keepdims=True)
    which = lax.broadcasted_iota(jnp.int32, stat.shape, 0)
    stat[...] = jnp.where(which == 0, top, total)
    stat_copy = remote(stat, stat_got, ssend, srecv, sibling)
    stat_copy.start()

    @pl.loop(0, kh // rows)
    def _(i):
        span = pl.ds(pl.multiple_of(i * rows, rows), rows)
        real, imag = harmonics(lambda j: sbuf[j, span, :])
        for r in range(NC):
            sbuf[r, span, :] = real[r]
        for r in range(1, HALF):
            sbuf[HALF + r, span, :] = imag[r]

    stat_copy.wait_recv()
    other_top, other_total = stat_got[0:1, :], stat_got[1:2, :]
    most = jnp.maximum(top, other_top)
    shrink = jnp.exp(top - most)
    whole = total * shrink + other_total * jnp.exp(other_top - most)
    evidence = most + jnp.log(whole)
    ev_ref[...] = jnp.where(c == 0, evidence[:, :n], evidence[:, n:])
    scale = shrink / whole

    tile = 16

    @pl.loop(0, kh // tile)
    def _(i):
        span = pl.ds(pl.multiple_of(i * tile, tile), tile)
        for r in range(NC):
            re = (sbuf[r, span, :] * scale).astype(BF16)
            pp[r, span, 0:n2] = re
            if r in (0, HALF):
                pp[r, span, n2:] = jnp.zeros_like(re)
            else:
                im = (sbuf[HALF + r, span, :] * scale).astype(BF16)
                pp[r, span, n2:] = -im
                pp[ROT - r, span, 0:n2] = re
                pp[ROT - r, span, n2:] = im

    def numer(block, cc, i):
        m = (block * 2 + cc) * mb + i
        r = lax.rem(m, ROT)
        return jnp.dot(pp[r], both[m].reshape(2 * n2, q), preferred_element_type=F32)

    def e_sum(s):
        return remote(esend.at[s], erecv.at[s], re_s.at[s], re_r.at[s], at(z + sign_of(s), x, c))

    def x_sum(d, s, e):
        return remote(xsend.at[slot(d, s, e)], xrecv.at[slot(d, s, e)],
                      rx_s.at[slot(d, s, e)], rx_r.at[slot(d, s, e)], at(z, y, c))

    def x_last(e):
        return remote(xlast.at[e], finx.at[c], rx_s.at[slot(0, 0, e)], fx_r.at[c],
                      at(z, y, jnp.bitwise_xor(c, e)))

    def x_goes(d, s, e):
        zo = z + sign_of(s) * d
        return jnp.logical_and(inside(zo), by_x(zo, e))

    def x_step(t):
        d = end - t
        for e in (1, 0):
            for s in range(2):
                if fixed(d, end) and e == 1:
                    continue

                @pl.when(x_goes(d, s, e))
                def _():
                    for i in range(mb):
                        xsend[slot(d, s, e), i] = numer(
                            chip(z + sign_of(s) * d, y), jnp.bitwise_xor(c, e), i
                        ).astype(BF16)
                    x_sum(d, s, e).start()

    x_step(0)
    for s in range(2):
        @pl.when(z == s * end)
        def _():
            for i in range(mb):
                esend[s, i] = numer(chip(end - s * end, y), o, i).astype(BF16)
            e_sum(s).start()

    each(1, zn - 1, x_step)

    def send_last(e, extra):
        for i in range(mb):
            value = numer(chip(z, y), jnp.bitwise_xor(c, e), i)
            if extra is not None:
                value = value + erecv[extra, i].astype(F32)
            xlast[e, i] = value.astype(BF16)
        x_last(e).start()

    @pl.loop(0, 2)
    def _(e):
        @pl.when(by_x(z, e))
        def _():
            send_last(e, None)

    def z_sum(d, s, e):
        return remote(zsend.at[slot(d, s, e)], zrecv.at[slot(d - 1, s, e)],
                      rz_s.at[slot(d, s, e)], rz_r.at[slot(d - 1, s, e)], at(z + sign_of(s), x, c))

    def z_got(d, s, e):
        return remote(zsend.at[slot(d, s, e)], zrecv.at[slot(d, s, e)],
                      rz_s.at[slot(d, s, e)], rz_r.at[slot(d, s, e)], sibling)

    def z_last(s, e):
        return remote(zsend.at[slot(1, s, e)], finz.at[s, c], rz_s.at[slot(1, s, e)], fz_r.at[s, c],
                      at(z + sign_of(s), x, jnp.bitwise_xor(c, e)))

    near = (2 * z < zn).astype(jnp.int32)

    def e_pass(d):
        for s in range(2):
            left = (end - z) if s == 0 else z

            @pl.when(jnp.logical_and(left == d - 1, jnp.logical_and(left > 0, left < end)))
            def _():
                e_sum(s).wait_recv()
                for i in range(mb):
                    esend[s, i] = (numer(chip(end - s * end, y), o, i) + erecv[s, i].astype(F32)).astype(BF16)
                e_sum(s).start()

    def e_cross():
        for s in range(2):
            @pl.when(z == (1 - s) * end)
            def _():
                e_sum(s).wait_recv()
                send_last(1, s)

    def z_step(t, between=None):
        d = end - t

        def part(j):
            e = 1 - j // 2
            s = jnp.bitwise_xor(j % 2, near)
            zo = z + sign_of(s) * d

            @pl.when(inside(zo))
            def _():
                here_slot = slot(d, s, e)
                crossed = by_x(zo, e)
                line = inside(z - sign_of(s))
                for i in range(mb):
                    acc[c, i] = numer(chip(zo, x), jnp.bitwise_xor(c, e), i)

                @pl.when(crossed)
                def _():
                    x_sum(d, s, e).wait_recv()
                    for i in range(mb):
                        acc[c, i] += xrecv[here_slot, i].astype(F32)

                @pl.when(line)
                def _():
                    z_got(d, s, e).wait_recv()
                    for i in range(mb):
                        zsend[here_slot, i] = (acc[c, i] + zrecv[here_slot, i].astype(F32)).astype(BF16)

                @pl.when(jnp.logical_not(line))
                def _():
                    for i in range(mb):
                        zsend[here_slot, i] = acc[c, i].astype(BF16)

                if isinstance(d, int):
                    (z_sum(d, s, e) if d > 1 else z_last(s, e)).start()
                else:
                    @pl.when(d > 1)
                    def _():
                        z_sum(d, s, e).start()

                    @pl.when(d == 1)
                    def _():
                        z_last(s, e).start()

        for j in range(2):
            part(j)
        if between is not None:
            between()
        if isinstance(d, int):
            if d == 1:
                e_cross()
            else:
                e_pass(d)
        else:
            pl.when(d == 1)(e_cross)
            e_pass(d)
        for j in range(2, 4):
            part(j)

    chips = dp // 2

    def mass_copy(g):
        return remote(mass, mslots.at[here], msend.at[g], mrecv.at[g], lax.rem(here + g, chips) * 2 + c)

    def mass_wait(g):
        return remote(mass, mslots.at[lax.rem(here + chips - g, chips)], msend.at[g], mrecv.at[g], sibling)

    halves_copy = remote(halves.at[c], halves.at[c], msend.at[0], mrecv.at[0], sibling)
    sib_copy = remote(sib, acc.at[c], bsend, brecv, sibling)

    def side_work():
        start = (here * n2 * G) // nall
        hot = (
            group == (lax.broadcasted_iota(jnp.int32, (window, n2), 0) + start).astype(F32)
        ).astype(F32)
        part_mass = lax.dot_general(
            hot, psum[...] * scale, (((1,), (1,)), ((), ())), preferred_element_type=F32, precision=HIGHEST,
        )
        nothing = jnp.zeros_like(part_mass)
        halves[c] = jnp.where(
            c == 0, jnp.concatenate([part_mass, nothing], axis=1), jnp.concatenate([nothing, part_mass], axis=1)
        )
        halves_copy.start()
        for i in range(mb):
            sib[i] = numer(here, o, i)
        sib_copy.start()
        halves_copy.wait_recv()
        both_mass = halves[0] + halves[1]
        mass[...] = both_mass
        mslots[here] = both_mass

        @pl.loop(1, dp // 2)
        def _(g):
            mass_copy(g).start()

    z_step(0, side_work)
    each(1, zn - 1, z_step)

    for i in range(mb):
        acc[c, i] = numer(here, c, i)

    for e in range(2):
        for s in range(2):
            @pl.when(inside(z + sign_of(s)))
            def _():
                first_z(s, e).wait_send()
        first_x(e).wait_send()
    own_half.wait_send()
    rows_copy.wait_send()
    stat_copy.wait_send()
    sib_copy.wait_send()

    @pl.loop(0, m_all // chunk)
    def _(i):
        weighted_copy(i).wait_send()

    @pl.loop(1, zn)
    def _(d):
        @pl.loop(0, 4)
        def _(j):
            e, s = j // 2, j % 2
            zo = z - sign_of(s) * d

            @pl.when(z_held(d, s))
            def _():
                @pl.when(inside(z + sign_of(s)))
                def _():
                    z_copy(d, s, e).wait_send()

                @pl.when(by_x(zo, e))
                def _():
                    x_copy(d, s, e).wait_send()

            @pl.when(x_goes(d, s, e))
            def _():
                x_sum(d, s, e).wait_send()

    for s in range(2):
        @pl.when(inside(z + sign_of(s)))
        def _():
            e_copy(s).wait_send()
            e_sum(s).wait_send()

    halves_copy.wait_send()

    @pl.loop(1, dp // 2)
    def _(g):
        mass_copy(g).wait_send()

    @pl.loop(1, dp // 2)
    def _(g):
        mass_wait(g).wait_recv()

    denom = 1.0 + lax.dot_general(
        mslots[...].reshape(dp // 2 * window, k), table[...], (((0,), (0,)), ((), ())),
        preferred_element_type=F32, precision=HIGHEST,
    )
    inv[...] = (1.0 / denom).reshape(inv.shape)
    sib_copy.wait_recv()

    def got_x(h):
        remote(xlast.at[0], finx.at[h], rx_s.at[slot(0, 0, 0)], fx_r.at[h], sibling).wait_recv()

    def got_z(s, h):
        remote(xlast.at[0], finz.at[s, h], rx_s.at[slot(0, 0, 0)], fz_r.at[s, h], sibling).wait_recv()

    for h in range(2):
        got_z(near, h)
        for i in range(mb):
            acc[h, i] += finz[near, h, i].astype(F32)
    for h in range(2):
        got_x(h)

    @pl.when(is_end(z))
    def _():
        for h in range(2):
            for i in range(mb):
                out_ref[i, h] = (acc[h, i] + finx[h, i].astype(F32)) * inv[h]

    @pl.when(jnp.logical_not(is_end(z)))
    def _():
        for h in range(2):
            got_z(1 - near, h)
            for i in range(mb):
                total = acc[h, i] + finx[h, i].astype(F32)
                out_ref[i, h] = (total + finz[1 - near, h, i].astype(F32)) * inv[h]

    def sums_sent(d):
        for s in range(2):
            @pl.when(inside(z + sign_of(s) * d))
            def _():
                for e in range(2):
                    z_got(d, s, e).wait_send()

    each(1, zn, sums_sent)

    for e in range(2):
        x_last(e).wait_send()


def finish_kernel(total_ref, ev_ref, out_ref, evidence_ref, sem):
    copy = pltpu.make_async_copy(total_ref, out_ref, sem)
    copy.start()
    evidence_ref[...] = ev_ref[...]
    copy.wait()


def shards(dp, particles, refs, ctf_group, defocus, class_prior, cycle_weight):
    n, m_all, q = particles.shape
    mb, k, _ = refs.shape
    zn = dp // 4
    nall = n * dp
    kh = k // 2
    n2 = 2 * n
    window = -(-((n2 * G) // nall + 3) // 8) * 8
    slots = 4 * zn
    weighted_chunks = m_all // 16

    vmem = pl.BlockSpec(memory_space=pltpu.VMEM)
    hbm = pl.BlockSpec(memory_space=pl.ANY)
    sem = pltpu.SemaphoreType.DMA
    total, ev = pl.pallas_call(
        functools.partial(step_kernel, zn, dp, window),
        out_shape=(
            jax.ShapeDtypeStruct((mb, 2, kh, q), F32),
            jax.ShapeDtypeStruct((1, n), F32),
        ),
        in_specs=[pl.BlockSpec(memory_space=pltpu.MemorySpace.HBM)] * 6,
        out_specs=(vmem, vmem),
        scratch_shapes=[
            pltpu.VMEM((2, kh, q), F32),
            pltpu.VMEM((1, n), jnp.int32), pltpu.VMEM((1, G), F32),
            pltpu.VMEM((1, R), F32), pltpu.VMEM((1, k), F32), sem((4,)),
            pltpu.VMEM((n, m_all, q), BF16),
            pltpu.VMEM((m_all, 2, 2, n, q), BF16),
            pltpu.VMEM((dp // 2, 2, mb, kh, q), BF16),
            pltpu.VMEM((ROT, kh, 2 * n2), F32),
            pltpu.VMEM((kh, q), F32),
            pltpu.VMEM((ROT, kh, n2), F32),
            pltpu.VMEM((kh, n2), F32),
            pltpu.VMEM((ROT, kh, 2 * n2), BF16),
            pltpu.VMEM((2, 8, n2), F32),
            pltpu.VMEM((dp // 2 * window, q), F32),
            pltpu.VMEM((8, n2), F32),
            pltpu.VMEM((8, n2), F32),
            pltpu.VMEM((2, window, k), F32),
            pltpu.VMEM((window, k), F32),
            pltpu.VMEM((dp // 2, window, k), F32),
            pltpu.VMEM((slots, mb, kh, q), BF16),
            pltpu.VMEM((slots, mb, kh, q), BF16),
            pltpu.VMEM((slots, mb, kh, q), BF16),
            pltpu.VMEM((slots, mb, kh, q), BF16),
            pltpu.VMEM((2, mb, kh, q), BF16),
            pltpu.VMEM((2, mb, kh, q), BF16),
            pltpu.VMEM((2, mb, kh, q), BF16),
            pltpu.VMEM((mb, kh, q), F32),
            pltpu.VMEM((2, mb, kh, q), F32),
            pltpu.VMEM((2, mb, kh, q), BF16),
            pltpu.VMEM((2, 2, mb, kh, q), BF16),
            sem, sem, sem, sem, sem((weighted_chunks,)), sem((weighted_chunks,)), sem, sem,
            sem((slots,)), sem((slots,)), sem((slots,)), sem((slots + 4,)), sem((2,)), sem((2,)),
            sem, sem, sem((dp // 2,)), sem((dp // 2,)),
            sem((slots,)), sem((slots,)), sem((slots,)), sem((slots,)), sem((2,)), sem((2,)),
            sem((2,)), sem((2, 2)), sem, sem,
        ],
        compiler_params=pltpu.CompilerParams(
            collective_id=0, has_side_effects=True, vmem_limit_bytes=40 << 20
        ),
        name="step",
    )(*(
        pltpu.with_memory_space_constraint(a, pltpu.MemorySpace.HBM) for a in (
            refs.reshape(mb, 2, kh, q), particles, ctf_group[None, :], defocus[None, :],
            cycle_weight[None, :], class_prior[None, :],
        )
    ))

    new_refs, evidence = pl.pallas_call(
        finish_kernel,
        out_shape=(
            jax.ShapeDtypeStruct((mb, 2, kh, q), F32),
            jax.ShapeDtypeStruct((1, n), F32),
        ),
        in_specs=[vmem] * 2,
        out_specs=(hbm, vmem),
        scratch_shapes=[sem],
        compiler_params=pltpu.CompilerParams(vmem_limit_bytes=8 << 20),
        name="finish",
    )(total, ev)
    return (new_refs.reshape(mb, k, q), evidence[0])


def solution(mesh):
    in_specs = (
        P(("groups", "dp"), None, None),
        P("dp", "groups", None),
        P(("groups", "dp")),
        P("groups"),
        P("groups"),
        P(),
    )
    out_specs = (P("dp", "groups", None), P(("groups", "dp")))
    return jax.shard_map(
        functools.partial(shards, mesh.shape["dp"]),
        mesh=mesh, in_specs=in_specs, out_specs=out_specs, check_vma=False,
    )
```
